128 devices in a mesh: band: 4 (over y), expert: 32 (over z, x, core).
Axes of the slice: x: 4, y: 4, z: 4, core: 2. Of those that a mesh axis runs over, the one named last changes fastest.
Arguments:
- features: bfloat16 [32, 32, 64, 512], P('expert', None, 'band'), may hold values from -18 to 18
- routes: int32 [32, 4, 32, 16, 1], P('expert', 'band'), may hold values from 0 to 31; in each aligned block of 512 rows (0 to 511, 512 to 1023, ..., all dimensions but the last counted through in order) at most 32 rows name the same one
- qkv_regular: bfloat16 [512, 1536], replicated, may hold values from -0.25 to 0.25
- proj_regular: bfloat16 [512, 512], replicated, may hold values from -0.25 to 0.25
- table_regular: float32 [225, 16], replicated, may hold values from -4 to 4
- gain_regular: float32 [512], replicated, may hold values from 0.5 to 1.5
- mlp_up: bfloat16 [512, 2048], replicated, may hold values from -0.25 to 0.25
- mlp_down: bfloat16 [2048, 512], replicated, may hold values from -0.125 to 0.125
- gain_mlp: float32 [512], replicated, may hold values from 0.5 to 1.5
- qkv_shifted: bfloat16 [512, 1536], replicated, may hold values from -0.25 to 0.25
- proj_shifted: bfloat16 [512, 512], replicated, may hold values from -0.25 to 0.25
- table_shifted: float32 [225, 16], replicated, may hold values from -4 to 4
- gain_shifted: float32 [512], replicated, may hold values from 0.5 to 1.5
- expert_in: bfloat16 [32, 512, 2048], P('expert', None, 'band'), may hold values from -0.25 to 0.25
- expert_out: bfloat16 [32, 2048, 512], P('expert', 'band'), may hold values from -0.125 to 0.125
- gain_expert: float32 [512], replicated, may hold values from 0.5 to 1.5
Outputs:
- encoded: bfloat16 [32, 32, 64, 512], P('expert', None, 'band')
The draws below stay inside these ranges and needn't reach their ends.
Inputs may be any that keep to these rules, and one draw needn't show every extreme that they name: `routes`: within one crop and one band (an aligned block of 512 tokens) no expert is named by more than 32 tokens, a bound that some block reaches.
All inputs are finite; a program needn't handle non-finite values.
Results may differ from the reference program's by a relative error of at most 0.015.
Values may be sent and summed in bfloat16 or wider, within the bound.
A program may use at most 128 MiB of HBM per device.

```python
import math
import jax
import jax.numpy as jnp
import numpy as np
from jax import lax

D = 512
HEADS = 16
FF = 2048
WIN = 8
GRID_H = 32
BAND_W = 16
BANDS = 4
GRID_W = 64
CROPS = 32
EXPERTS = 32
SEC = 512
CAP = 32
TABLE = 225


def draw_features(key, part):
    key_base = jax.random.fold_in(key, 11)
    key_noise, key_rows, key_cols = jax.random.split(key_base, 3)
    full_shape = (CROPS, GRID_H, GRID_W, D)
    noise = jnp.clip(jax.random.normal(key_noise, full_shape, jnp.float32), -3.0, 3.0)
    row_scale = jnp.exp(jax.random.uniform(key_rows, (CROPS, GRID_H, GRID_W, 1), jnp.float32, math.log(0.3), math.log(3.0)))
    col_scale = jnp.exp(jax.random.uniform(key_cols, (D,), jnp.float32, math.log(0.5), math.log(2.0)))
    return (noise * row_scale * col_scale).astype(jnp.bfloat16)


def shard_levels(key, shape, pieces, least, top_value):
    loudness, own = 1.0, jax.random.fold_in(key, 6)
    for dim, parts in pieces:
        steps = jnp.exp(jax.random.uniform(jax.random.fold_in(own, dim), (parts,), jnp.float32, least / len(pieces), top_value / len(pieces)))
        loudness = loudness * jnp.repeat(steps, shape[dim] // parts).reshape([-1 if axis == dim else 1 for axis in range(len(shape))])
    return loudness


def routed_block(own_key, own, number, rows, amount, top, most, lean):
    order = jax.random.permutation(own_key, amount)
    crowded, usual = load_shares(amount, rows * top, most, lean, True), load_shares(amount, rows * top, most, lean, False)
    places = jnp.arange(amount)

    def named(sizes, rotation):
        used = int((sizes > 0).sum())
        fixed = max(1, used // 4)
        shifted = fixed + (places - fixed + rotation * (used - fixed)) % max(1, amount - fixed)
        return jnp.zeros((amount,), jnp.int32).at[order[jnp.where(places < fixed, places, shifted)]].set(jnp.asarray(sizes, jnp.int32))

    sizes = jnp.where(number % 4 == 0, named(crowded, number // 4), named(usual, number - number // 4 - 1))
    mixed = jax.random.permutation(jax.random.fold_in(own, 3), amount)
    giver, receiver = mixed[0:amount // 2 * 2:2], mixed[1:amount // 2 * 2:2]
    slack = jnp.minimum(sizes[giver] - 1, most - sizes[receiver]) // 2
    slack = jnp.where((giver == order[0]) | (receiver == order[0]) | (sizes[receiver] == 0), 0, jnp.maximum(slack, 0))
    shifted = jax.random.randint(jax.random.fold_in(own, 4), (amount // 2,), 0, 1 << 20) % (slack + 1)
    sizes = sizes.at[giver].add(-shifted).at[receiver].add(shifted)
    items = jnp.searchsorted(jnp.cumsum(sizes), jnp.arange(rows * top), side="right").astype(jnp.int32)
    listing = items.reshape(top, rows).T
    listing = listing[jax.random.permutation(jax.random.fold_in(own, 1), rows)]
    rotation = jax.random.randint(jax.random.fold_in(own, 2), (rows, 1), 0, top)
    return jnp.take_along_axis(listing, (jnp.arange(top)[None, :] + rotation) % top, axis=1)


def load_shares(number_of, total, reach, slope, full):
    portions = [(1 << 20) // math.isqrt(standing ** slope) + 1 for standing in range(1, number_of + 1)]
    largest = reach if full else min(reach, max(-(-total // number_of), total * portions[0] // sum(portions)))
    least = 1 if total - largest >= number_of - 1 else 0
    counts, rest = [largest] + [least] * (number_of - 1), total - largest - least * (number_of - 1)
    while rest > 0:
        candidates = [i for i in range(1, number_of) if counts[i] < largest] or [i for i in range(1, number_of) if counts[i] < reach]
        whole, remaining = sum([portions[i] for i in candidates]), rest
        for i in candidates:
            more = min(reach - counts[i], max(1, remaining * portions[i] // whole), rest)
            counts[i] = counts[i] + more
            rest = rest - more
    return np.array(counts)


def gaussian(own_key, shape, width, reach, shards=(), kind=jnp.bfloat16):
    result = width * jax.random.normal(own_key, shape, jnp.float32)
    if shards:
        result = result * shard_levels(own_key, shape, shards, -0.22, 0.18)
    return jnp.clip(result, -reach, reach).astype(kind)


def setup_inputs(seed: int = 0) -> dict:
    seeds = jax.random.split(jax.random.key(seed), 17)
    features = draw_features(jax.random.fold_in(seeds[16], 71), 0)
    routes_keys = jax.random.split(jax.random.fold_in(seeds[1], 1), CROPS * BANDS * GRID_H * BAND_W // SEC)
    routes_turns = jax.random.permutation(jax.random.fold_in(seeds[1], 3), CROPS * BANDS * GRID_H * BAND_W // SEC)
    routes = jax.vmap(lambda own, number: routed_block(jax.random.fold_in(seeds[1], 2), own, number, SEC, EXPERTS, 1, CAP, 2))(routes_keys, routes_turns).reshape((CROPS, BANDS, GRID_H, BAND_W, 1))
    qkv_regular = gaussian(seeds[2], (D, 3 * D), D ** -0.5, 0.25)
    proj_regular = gaussian(seeds[3], (D, D), D ** -0.5, 0.25)
    table_regular = gaussian(seeds[4], (TABLE, HEADS), 1.0, 4.0, (), jnp.float32)
    gain_regular = jnp.clip(1.0 + 0.1 * jax.random.normal(seeds[5], (D,), jnp.float32), 0.5, 1.5)
    mlp_up = gaussian(seeds[6], (D, FF), D ** -0.5, 0.25)
    mlp_down = gaussian(seeds[7], (FF, D), FF ** -0.5, 0.125)
    gain_mlp = jnp.clip(1.0 + 0.1 * jax.random.normal(seeds[8], (D,), jnp.float32), 0.5, 1.5)
    qkv_shifted = gaussian(seeds[9], (D, 3 * D), D ** -0.5, 0.25)
    proj_shifted = gaussian(seeds[10], (D, D), D ** -0.5, 0.25)
    table_shifted = gaussian(seeds[11], (TABLE, HEADS), 1.0, 4.0, (), jnp.float32)
    gain_shifted = jnp.clip(1.0 + 0.1 * jax.random.normal(seeds[12], (D,), jnp.float32), 0.5, 1.5)
    expert_in = gaussian(seeds[13], (EXPERTS, D, FF), D ** -0.5, 0.25, ((0, 32), (2, 4)))
    expert_out = gaussian(seeds[14], (EXPERTS, FF, D), FF ** -0.5, 0.125, ((0, 32), (1, 4)))
    gain_expert = jnp.clip(1.0 + 0.1 * jax.random.normal(seeds[15], (D,), jnp.float32), 0.5, 1.5)
    return dict(features=features, routes=routes, qkv_regular=qkv_regular, proj_regular=proj_regular, table_regular=table_regular, gain_regular=gain_regular, mlp_up=mlp_up, mlp_down=mlp_down, gain_mlp=gain_mlp, qkv_shifted=qkv_shifted, proj_shifted=proj_shifted, table_shifted=table_shifted, gain_shifted=gain_shifted, expert_in=expert_in, expert_out=expert_out, gain_expert=gain_expert)


def layer_norm(values, gain_vec):
    centre = lax.optimization_barrier(jnp.mean(values, axis=-1, keepdims=True))
    offsets = values - centre
    spread = lax.optimization_barrier(jnp.mean(offsets * offsets, axis=-1, keepdims=True))
    return offsets * lax.rsqrt(spread + 1e-05) * gain_vec

def band_labels(places, length_cells, window):
    half_win = window // 2
    return jnp.where(places < length_cells - window, 0, jnp.where(places < length_cells - half_win, 1, 2)).astype(jnp.int32)

def partition(grid_vals, window):
    height, width_cells = grid_vals.shape[:2]
    trailing = grid_vals.shape[2:]
    split_up = grid_vals.reshape((height // window, window, width_cells // window, window) + trailing)
    order = (0, 2, 1, 3) + tuple(range(4, 4 + len(trailing)))
    return split_up.transpose(order).reshape((-1, window * window) + trailing)

def merge_windows(window_vals, height, width_cells, window):
    model_width = window_vals.shape[-1]
    split_up = window_vals.reshape(height // window, width_cells // window, window, window, model_width)
    return split_up.transpose(0, 2, 1, 3, 4).reshape(height, width_cells, model_width)

def attend(grid_in, qkv_weight, table, label_grid):
    height, width_cells, model_width = grid_in.shape
    window = WIN
    head_count = HEADS
    head_dim = model_width // head_count
    cell_count = window * window
    span_cells = 2 * window - 1
    cell_ids = jnp.arange(cell_count, dtype=jnp.int32)
    cell_row = cell_ids // window
    cell_col = cell_ids % window
    index_grid = (cell_row[:, None] - cell_row[None, :] + window - 1) * span_cells + (cell_col[:, None] - cell_col[None, :] + window - 1)
    bias_heads = jnp.take(table, index_grid.reshape(-1), axis=0).reshape(cell_count, cell_count, head_count).transpose(2, 0, 1)
    qkv_all = jnp.dot(grid_in.reshape(-1, model_width), qkv_weight, preferred_element_type=jnp.float32).astype(jnp.bfloat16)
    parted = partition(qkv_all.reshape(height, width_cells, 3 * model_width), window)
    queries = parted[:, :, :model_width].reshape(-1, cell_count, head_count, head_dim).astype(jnp.float32)
    key_rows = parted[:, :, model_width:2 * model_width].reshape(-1, cell_count, head_count, head_dim).astype(jnp.float32)
    value_rows = parted[:, :, 2 * model_width:].reshape(-1, cell_count, head_count, head_dim).astype(jnp.float32)
    label_cells = partition(label_grid, window)
    mask_add = jnp.where(label_cells[:, :, None] == label_cells[:, None, :], 0.0, -100.0).astype(jnp.float32)
    scores = jnp.einsum('wqhd,wkhd->whqk', queries, key_rows) * head_dim ** (-0.5) + bias_heads[None] + mask_add[:, None]
    weights = jnp.exp(scores - lax.optimization_barrier(jnp.max(scores, axis=-1, keepdims=True)))
    weights = (weights / lax.optimization_barrier(jnp.sum(weights, axis=-1, keepdims=True))).astype(jnp.bfloat16)
    mixed_heads = jnp.einsum('whqk,wkhd->wqhd', weights.astype(jnp.float32), value_rows).astype(jnp.bfloat16)
    return merge_windows(mixed_heads.reshape(-1, cell_count, model_width), height, width_cells, window)

def crop_blocks(grid_in, qkv_regular, proj_regular, table_regular, gain_regular, mlp_up, mlp_down, gain_mlp, qkv_shifted, proj_shifted, table_shifted, gain_shifted):
    height, width_cells, model_width = grid_in.shape
    half_win = WIN // 2
    zero_labels = jnp.zeros((height, width_cells), jnp.int32)
    heads_regular = attend(grid_in, qkv_regular, table_regular, zero_labels)
    flat_in = grid_in.reshape(-1, model_width).astype(jnp.float32)
    projected = jnp.dot(heads_regular.reshape(-1, model_width), proj_regular, preferred_element_type=jnp.float32)
    first_out = (flat_in + layer_norm(projected, gain_regular)).astype(jnp.bfloat16)
    hidden_mlp = jax.nn.gelu(jnp.dot(first_out, mlp_up, preferred_element_type=jnp.float32), approximate=False).astype(jnp.bfloat16)
    dense_out = jnp.dot(hidden_mlp, mlp_down, preferred_element_type=jnp.float32)
    second_out = (first_out.astype(jnp.float32) + layer_norm(dense_out, gain_mlp)).astype(jnp.bfloat16)
    rolled = jnp.roll(second_out.reshape(height, width_cells, model_width), (-half_win, -half_win), axis=(0, 1))
    row_places = jnp.arange(height, dtype=jnp.int32)
    col_places = jnp.arange(width_cells, dtype=jnp.int32)
    label_grid = band_labels(row_places, height, WIN)[:, None] * 3 + band_labels(col_places, width_cells, WIN)[None, :]
    heads_shifted = jnp.roll(attend(rolled, qkv_shifted, table_shifted, label_grid), (half_win, half_win), axis=(0, 1))
    projected_two = jnp.dot(heads_shifted.reshape(-1, model_width), proj_shifted, preferred_element_type=jnp.float32)
    third_out = (second_out.astype(jnp.float32) + layer_norm(projected_two, gain_shifted)).astype(jnp.bfloat16)
    return third_out.reshape(height, width_cells, model_width)

def reference(features, routes, qkv_regular, proj_regular, table_regular, gain_regular, mlp_up, mlp_down, gain_mlp, qkv_shifted, proj_shifted, table_shifted, gain_shifted, expert_in, expert_out, gain_expert):

    def crop_step(grid_in):
        return crop_blocks(grid_in, qkv_regular, proj_regular, table_regular, gain_regular, mlp_up, mlp_down, gain_mlp, qkv_shifted, proj_shifted, table_shifted, gain_shifted)
    streams = lax.map(crop_step, features)
    section_count = CROPS * BANDS
    sections = streams.reshape(CROPS, GRID_H, BANDS, BAND_W, D).transpose(0, 2, 1, 3, 4).reshape(section_count, SEC, D)
    route_rows = routes.reshape(section_count, SEC).astype(jnp.int32)
    onehot = (route_rows[:, :, None] == jnp.arange(EXPERTS, dtype=jnp.int32)[None, None, :]).astype(jnp.int32)
    positions = lax.optimization_barrier(jnp.sum(jnp.cumsum(onehot, axis=1) * onehot, axis=2)) - 1
    section_ids = jnp.arange(section_count, dtype=jnp.int32)[:, None]
    target = ((route_rows * section_count + section_ids) * CAP + positions).reshape(-1).astype(jnp.int32)
    buffer_rows = jnp.zeros((EXPERTS * section_count * CAP, D), jnp.bfloat16).at[target].set(sections.reshape(-1, D))

    def one_expert(packed):
        rows_in, weight_in, weight_out = packed
        hidden = jax.nn.gelu(jnp.dot(rows_in, weight_in, preferred_element_type=jnp.float32), approximate=False).astype(jnp.bfloat16)
        return jnp.dot(hidden, weight_out, preferred_element_type=jnp.float32).astype(jnp.bfloat16)
    mapped = lax.map(one_expert, (buffer_rows.reshape(EXPERTS, section_count * CAP, D), expert_in, expert_out))
    expert_rows = mapped.reshape(-1, D)[target]
    encoded = (sections.reshape(-1, D).astype(jnp.float32) + layer_norm(expert_rows.astype(jnp.float32), gain_expert)).astype(jnp.bfloat16)
    return encoded.reshape(CROPS, BANDS, GRID_H, BAND_W, D).transpose(0, 2, 1, 3, 4).reshape(CROPS, GRID_H, GRID_W, D)
```

```python
import jax
import jax.numpy as jnp
from jax import lax
from jax.sharding import PartitionSpec as P

HEADS = 16
WIN = 8


def from_behind(block, axis, distance):
    devices = range(lax.axis_size(axis))
    route = [((i - distance) % len(devices), i) for i in devices]
    return lax.ppermute(block, axis, route)


def layer_norm(values, gain_vec):
    centre = jnp.mean(values, axis=-1, keepdims=True)
    offsets = values - centre
    spread = jnp.mean(offsets * offsets, axis=-1, keepdims=True)
    return offsets * lax.rsqrt(spread + 1e-05) * gain_vec


def band_labels(places, length_cells, window):
    half_win = window // 2
    return jnp.where(
        places < length_cells - window, 0, jnp.where(places < length_cells - half_win, 1, 2)
    ).astype(jnp.int32)


def column_labels(anchor, length_cells, grid_width, window):
    half_win = window // 2
    places = jnp.mod(anchor + jnp.arange(length_cells, dtype=jnp.int32), grid_width)
    return jnp.where(places >= grid_width - half_win, 1, jnp.where(places < half_win, 2, 0)).astype(
        jnp.int32
    )


def window_bias(table, window):
    span_cells = 2 * window - 1
    cell_ids = jnp.arange(window * window, dtype=jnp.int32)
    cell_row = cell_ids // window
    cell_col = cell_ids % window
    index_grid = (cell_row[:, None] - cell_row[None, :] + window - 1) * span_cells + (
        cell_col[:, None] - cell_col[None, :] + window - 1
    )
    onehot = (
        index_grid.reshape(-1)[:, None]
        == jnp.arange(span_cells * span_cells, dtype=jnp.int32)[None, :]
    ).astype(jnp.float32)
    picked = jnp.dot(onehot, table, precision=lax.Precision.HIGHEST)
    return picked.reshape(window * window, window * window, -1).transpose(2, 0, 1)


def partition(grid_vals, window):
    crop_count, height, width_cells = grid_vals.shape[:3]
    trailing = grid_vals.shape[3:]
    split_up = grid_vals.reshape(
        (crop_count, height // window, window, width_cells // window, window) + trailing
    )
    order = (0, 1, 3, 2, 4) + tuple(range(5, 5 + len(trailing)))
    return split_up.transpose(order).reshape((-1, window * window) + trailing)


def merge_windows(window_vals, crop_count, height, width_cells, window):
    model_width = window_vals.shape[-1]
    split_up = window_vals.reshape(
        crop_count, height // window, width_cells // window, window, window, model_width
    )
    return split_up.transpose(0, 1, 3, 2, 4, 5).reshape(
        crop_count, height, width_cells, model_width
    )


def window_attention(grid_in, qkv_weight, bias_heads, label_grid, window, head_count):
    crop_count, height, width_cells, model_width = grid_in.shape
    head_dim = model_width // head_count
    cell_count = window * window
    qkv_all = jnp.dot(
        grid_in.reshape(-1, model_width), qkv_weight, preferred_element_type=jnp.float32
    ).astype(jnp.bfloat16)
    parted = partition(qkv_all.reshape(crop_count, height, width_cells, 3 * model_width), window)
    queries = parted[:, :, :model_width].reshape(-1, cell_count, head_count, head_dim)
    key_rows = parted[:, :, model_width : 2 * model_width].reshape(
        -1, cell_count, head_count, head_dim
    )
    value_rows = parted[:, :, 2 * model_width :].reshape(-1, cell_count, head_count, head_dim)
    label_cells = partition(jnp.broadcast_to(label_grid, (crop_count, height, width_cells)), window)
    mask_add = jnp.where(label_cells[:, :, None] == label_cells[:, None, :], 0.0, -100.0).astype(
        jnp.float32
    )
    scores = (
        jnp.einsum("wqhd,wkhd->whqk", queries, key_rows, preferred_element_type=jnp.float32)
        * head_dim ** (-0.5)
        + bias_heads[None]
        + mask_add[:, None]
    )
    weights = jnp.exp(scores - jnp.max(scores, axis=-1, keepdims=True))
    weights = (weights / jnp.sum(weights, axis=-1, keepdims=True)).astype(jnp.bfloat16)
    mixed_heads = jnp.einsum(
        "whqk,wkhd->wqhd", weights, value_rows, preferred_element_type=jnp.float32
    ).astype(jnp.bfloat16)
    return merge_windows(
        mixed_heads.reshape(-1, cell_count, model_width), crop_count, height, width_cells, window
    )


def slot_ids(route_row, experts, capacity):
    count = route_row.shape[0]
    onehot = (route_row[:, None] == jnp.arange(experts, dtype=jnp.int32)[None, :]).astype(
        jnp.bfloat16
    )
    order = jnp.arange(count, dtype=jnp.int32)
    earlier = (order[None, :] < order[:, None]).astype(jnp.bfloat16)
    ahead = jnp.dot(earlier, onehot, preferred_element_type=jnp.float32)
    position = jnp.sum(ahead * onehot, axis=-1).astype(jnp.int32)
    return route_row * capacity + position


def local(
    features,
    routes,
    qkv_regular,
    proj_regular,
    table_regular,
    gain_regular,
    mlp_up,
    mlp_down,
    gain_mlp,
    qkv_shifted,
    proj_shifted,
    table_shifted,
    gain_shifted,
    expert_in,
    expert_out,
    gain_expert,
):
    crop_count, height, band_width, model_width = features.shape
    window = WIN
    half_win = window // 2
    head_count = HEADS
    section = height * band_width
    band_count = lax.axis_size("band")
    band_index = lax.axis_index("band")
    grid_width = band_width * band_count
    local_experts = expert_in.shape[0]
    experts = local_experts * lax.axis_size("expert")
    weight_in = lax.all_gather(expert_in[0], "band", axis=1, tiled=True)
    weight_out = lax.all_gather(expert_out[0], "band", axis=0, tiled=True)
    flat_in = features.reshape(-1, model_width)
    zero_labels = jnp.zeros((height, band_width), jnp.int32)
    heads_regular = window_attention(
        features, qkv_regular, window_bias(table_regular, window), zero_labels, window, head_count
    )
    projected = jnp.dot(
        heads_regular.reshape(-1, model_width), proj_regular, preferred_element_type=jnp.float32
    )
    first_out = (flat_in.astype(jnp.float32) + layer_norm(projected, gain_regular)).astype(
        jnp.bfloat16
    )
    hidden_mlp = jax.nn.gelu(
        jnp.dot(first_out, mlp_up, preferred_element_type=jnp.float32), approximate=False
    ).astype(jnp.bfloat16)
    dense_out = jnp.dot(hidden_mlp, mlp_down, preferred_element_type=jnp.float32)
    second_out = (first_out.astype(jnp.float32) + layer_norm(dense_out, gain_mlp)).astype(
        jnp.bfloat16
    )
    rolled = jnp.roll(
        second_out.reshape(crop_count, height, band_width, model_width), -half_win, axis=1
    )
    row_labels = band_labels(jnp.arange(height, dtype=jnp.int32), height, window)
    bias_shift = window_bias(table_shifted, window)
    arriving = from_behind(rolled[:, :, :half_win, :], "band", -1)
    window_in = jnp.concatenate([rolled[:, :, half_win:, :], arriving], axis=2)
    anchor = band_index * band_width + half_win
    col_labels = column_labels(anchor, band_width, grid_width, window)
    mixed_rows = window_attention(
        window_in,
        qkv_shifted,
        bias_shift,
        row_labels[:, None] * 3 + col_labels[None, :],
        window,
        head_count,
    )
    returning = from_behind(mixed_rows[:, :, band_width - half_win :, :], "band", 1)
    mixed_rows = jnp.concatenate([returning, mixed_rows[:, :, : band_width - half_win, :]], axis=2)
    heads_shifted = jnp.roll(mixed_rows, half_win, axis=1)
    projected_two = jnp.dot(
        heads_shifted.reshape(-1, model_width), proj_shifted, preferred_element_type=jnp.float32
    )
    third_out = (second_out.astype(jnp.float32) + layer_norm(projected_two, gain_shifted)).astype(
        jnp.bfloat16
    )
    capacity = 2 * section // experts
    route_rows = routes.reshape(section)
    slots = slot_ids(route_rows, experts, capacity)
    place = (slots[None, :] == jnp.arange(experts * capacity, dtype=jnp.int32)[:, None]).astype(
        jnp.bfloat16
    )
    outgoing = jnp.dot(place, third_out, preferred_element_type=jnp.float32).astype(jnp.bfloat16)
    arrived = lax.all_to_all(
        outgoing.reshape(experts, capacity, model_width),
        "expert",
        split_axis=0,
        concat_axis=0,
        tiled=True,
    ).reshape(experts * capacity, model_width)
    hidden = jax.nn.gelu(
        jnp.dot(arrived, weight_in, preferred_element_type=jnp.float32), approximate=False
    ).astype(jnp.bfloat16)
    rows_out = jnp.dot(hidden, weight_out, preferred_element_type=jnp.float32).astype(jnp.bfloat16)
    returned = lax.all_to_all(
        rows_out.reshape(experts, capacity, model_width),
        "expert",
        split_axis=0,
        concat_axis=0,
        tiled=True,
    ).reshape(experts * capacity, model_width)
    take = (slots[:, None] == jnp.arange(experts * capacity, dtype=jnp.int32)[None, :]).astype(
        jnp.bfloat16
    )
    expert_rows = jnp.dot(take, returned, preferred_element_type=jnp.float32)
    encoded = (
        third_out.astype(jnp.float32) + layer_norm(expert_rows.astype(jnp.float32), gain_expert)
    ).astype(jnp.bfloat16)
    return encoded.reshape(crop_count, height, band_width, model_width)


def solution(mesh):
    return jax.shard_map(
        local,
        mesh=mesh,
        in_specs=(
            P("expert", None, "band", None),
            P("expert", "band", None, None, None),
            P(),
            P(),
            P(),
            P(),
            P(),
            P(),
            P(),
            P(),
            P(),
            P(),
            P(),
            P("expert", None, "band"),
            P("expert", "band", None),
            P(),
        ),
        out_specs=P("expert", None, "band", None),
        check_vma=False,
    )
```

```python
import functools
import jax
import jax.numpy as jnp
from jax import lax
from jax.experimental import pallas as pl
from jax.experimental.pallas import tpu as pltpu
from jax.sharding import PartitionSpec as P

MESH = pl.DeviceIdType.MESH
F32 = jnp.float32
BF16 = jnp.bfloat16
WIN = 8
HALF = WIN // 2
CELLS = WIN * WIN
LANES = 128
LOG2E = 1.4426950408889634
ROOT_HALF = 0.7071067811865476


def dot(a, b):
    return jnp.dot(a, b, preferred_element_type=F32)


def dot_over(a, b, dim_a, dim_b):
    return lax.dot_general(a, b, (((dim_a,), (dim_b,)), ((), ())), preferred_element_type=F32)


def gelu(v):
    return (0.5 * v) * (1.0 + lax.erf(v * ROOT_HALF))


def layer_norm(values, gain_vec):
    centre = jnp.mean(values, axis=-1, keepdims=True)
    offsets = values - centre
    spread = jnp.mean(offsets * offsets, axis=-1, keepdims=True)
    return offsets * lax.rsqrt(spread + 1e-05) * gain_vec


def turn(tiles):
    return pltpu.roll(tiles, HALF, axis=tiles.ndim - 2)


def cell_is_low(shape):
    return lax.broadcasted_iota(jnp.int32, shape, len(shape) - 2) < HALF


def window_bias(flat_ref, first_head, bias_ref):
    pitch = 2 * WIN
    width = pitch * pitch
    even = lax.broadcasted_iota(jnp.int32, (WIN, LANES), 1) % pitch < WIN
    for group in range(4):
        for pair in range(2):
            head = first_head + group * 4 + pair * 2
            row_even = jnp.broadcast_to(flat_ref[head : head + 1, :], (WIN, width))
            row_odd = jnp.broadcast_to(flat_ref[head + 1 : head + 2, :], (WIN, width))
            for key_row in range(WIN):
                back = (WIN - 1 - key_row) * pitch + WIN - 1
                a = pltpu.roll(row_even, (width - back) % width, axis=1, stride=1, stride_axis=0)
                b = pltpu.roll(
                    row_odd, (width - back + WIN) % width, axis=1, stride=1, stride_axis=0
                )
                bias_ref[
                    group,
                    key_row * WIN : (key_row + 1) * WIN,
                    pair * LANES : (pair + 1) * LANES,
                ] = jnp.where(even, a[:, :LANES], b[:, :LANES])


def spread_heads(q):
    head = lax.broadcasted_iota(jnp.int32, (1, 1, LANES), 2) // 32
    tiles = q.astype(F32).reshape(WIN, WIN, LANES)
    pieces = []
    for pair in range(2):
        both = [jnp.where(head == pair * 2 + k, tiles, 0.0)[:, None] for k in range(2)]
        pieces.append(jnp.concatenate(both, axis=1).reshape(2 * CELLS, LANES))
    return jnp.concatenate(pieces, axis=0).astype(BF16)


def gather_heads(o):
    head = lax.broadcasted_iota(jnp.int32, (1, 1, LANES), 2) // 32
    parts = o.reshape(2, WIN, 2, WIN, LANES)
    low = jnp.where(head == 0, parts[0, :, 0], parts[0, :, 1])
    high = jnp.where(head == 2, parts[1, :, 0], parts[1, :, 1])
    return jnp.where(head < 2, low, high).reshape(CELLS, LANES)


def soften(s):
    e = jnp.exp2(s - jnp.max(s, axis=0, keepdims=True))
    return (e * (1.0 / jnp.sum(e, axis=0, keepdims=True))).astype(BF16)


def front_kernel(
    x_ref,
    flat_ref,
    gains_ref,
    qkv_r_hbm,
    proj_r_hbm,
    up_hbm,
    down_hbm,
    qkv_s_hbm,
    proj_s_hbm,
    out_ref,
    qkv_r,
    proj_r,
    up,
    down,
    qkv_s,
    proj_s,
    load_sem,
    bias_r,
    bias_s,
    tiles,
    qkv_buf,
    edge_buf,
    heads,
    to_left,
    to_right,
    from_left,
    from_right,
    send_sem,
    recv_sem,
):
    band = lax.axis_index("band")
    bands = lax.axis_size("band")
    right = lax.rem(band + 1, bands)
    left = lax.rem(band + bands - 1, bands)
    loads = [
        pltpu.make_async_copy(src, dst, load_sem.at[n])
        for n, (src, dst) in enumerate(
            (
                (qkv_r_hbm, qkv_r),
                (proj_r_hbm, proj_r),
                (up_hbm, up),
                (down_hbm, down),
                (qkv_s_hbm, qkv_s),
                (proj_s_hbm, proj_s),
            )
        )
    ]
    for load in loads:
        load.start()
    barrier = pltpu.get_barrier_semaphore()
    for other in (left, right):
        pl.semaphore_signal(barrier, inc=1, device_id={"band": other}, device_id_type=MESH)
    pl.semaphore_wait(barrier, 2)

    scale = LOG2E * 32**-0.5
    window_bias(flat_ref, 0, bias_r)
    window_bias(flat_ref, 16, bias_s)
    for load in loads[:4]:
        load.wait()

    def sends(part):
        return [
            pltpu.make_async_remote_copy(
                src_ref=to_left.at[part],
                dst_ref=from_right.at[part],
                send_sem=send_sem.at[0, part],
                recv_sem=recv_sem.at[0, part],
                device_id={"band": left},
                device_id_type=MESH,
            ),
            pltpu.make_async_remote_copy(
                src_ref=to_right.at[part],
                dst_ref=from_left.at[part],
                send_sem=send_sem.at[1, part],
                recv_sem=recv_sem.at[1, part],
                device_id={"band": right},
                device_id_type=MESH,
            ),
        ]

    low_cell = cell_is_low((1, WIN, 512))

    def first_part(part, carry):
        x3 = x_ref[0, pl.ds(part * 16, 16)].astype(F32)
        xf = jnp.concatenate(
            [
                x3[r * 8 : r * 8 + 8, c * 8 : c * 8 + 8, :].reshape(CELLS, 512)
                for r in range(2)
                for c in range(2)
            ],
            axis=0,
        )
        qkv_buf[...] = dot(xf.astype(BF16), qkv_r[...]).astype(BF16)
        for w in range(4):
            rows = slice(w * CELLS, (w + 1) * CELLS)
            for g in range(4):
                q = qkv_buf[rows, g * 128 : g * 128 + 128]
                k = qkv_buf[rows, 512 + g * 128 : 640 + g * 128]
                v = qkv_buf[rows, 1024 + g * 128 : 1152 + g * 128]
                s = dot_over(k, spread_heads(q), 1, 1) * scale + bias_r[g]
                heads[rows, g * 128 : g * 128 + 128] = gather_heads(
                    dot_over(soften(s), v, 0, 0)
                ).astype(BF16)
        first = (xf + layer_norm(dot(heads[...], proj_r[...]), gains_ref[0:1, :])).astype(BF16)
        total = jnp.zeros((256, 512), F32)
        for f in range(4):
            hidden = gelu(dot(first, up[:, f * 512 : f * 512 + 512])).astype(BF16)
            total = total + dot(hidden, down[f * 512 : f * 512 + 512, :])
        second = (first.astype(F32) + layer_norm(total, gains_ref[1:2, :])).astype(BF16).astype(F32)
        for r in range(2):
            rows = pl.ds(part * 16 + r * 8, 8)
            w0 = second[r * 128 : r * 128 + 64].reshape(WIN, WIN, 512)
            w1 = second[r * 128 + 64 : r * 128 + 128].reshape(WIN, WIN, 512)
            tiles[rows, 1] = w0
            tiles[rows, 2] = w1
            to_left[part, r * 32 : r * 32 + 32] = (
                jnp.where(low_cell, w0[:HALF], turn(w0[HALF:])).reshape(32, 512).astype(BF16)
            )
            to_right[part, r * 32 : r * 32 + 32] = (
                jnp.where(low_cell, turn(w1[HALF:]), w1[:HALF]).reshape(32, 512).astype(BF16)
            )
        for send in sends(part):
            send.start()
        return carry

    lax.fori_loop(0, 2, first_part, 0)

    def shifted(column):
        pieces = []
        for w in range(4):
            for start in (w * 8 + 4, (w * 8 + 8) % 32):
                a = tiles[start : start + 4, column]
                b = tiles[start : start + 4, column + 1]
                pieces.append(turn(jnp.where(low_cell, b, a)))
        return jnp.concatenate(pieces, axis=0)

    def finish(x, first_row):
        third = x + layer_norm(dot(heads[...], proj_s[...]), gains_ref[2:3, :])
        out_ref[first_row : first_row + 256, :] = third.astype(BF16)

    key = lax.broadcasted_iota(jnp.int32, (CELLS, 256), 0)
    lane = lax.broadcasted_iota(jnp.int32, (CELLS, 256), 1)
    low_j = lane % 8 < HALF
    row_apart = (key // 8 < HALF) != ((lane // 16) % 8 < HALF)
    col_apart = ((key % 8 < HALF) != low_j) & (
        (low_j & (band == bands - 1)) | (jnp.logical_not(low_j) & (band == 0))
    )
    mask_row = jnp.where(row_apart, -100.0 * LOG2E, 0.0)
    mask_col = jnp.where(col_apart, -100.0 * LOG2E, 0.0)
    mask_both = jnp.where(row_apart | col_apart, -100.0 * LOG2E, 0.0)

    for load in loads[4:]:
        load.wait()
    mid = shifted(1).reshape(256, 512)
    qkv_buf[...] = dot(mid.astype(BF16), qkv_s[...]).astype(BF16)
    for w in range(4):
        rows = slice(w * CELLS, (w + 1) * CELLS)
        for g in range(4):
            q = qkv_buf[rows, g * 128 : g * 128 + 128]
            k = qkv_buf[rows, 512 + g * 128 : 640 + g * 128]
            v = qkv_buf[rows, 1024 + g * 128 : 1152 + g * 128]
            s = dot_over(k, spread_heads(q), 1, 1) * scale + bias_s[g]
            if w == 3:
                s = s + mask_row
            heads[rows, g * 128 : g * 128 + 128] = gather_heads(
                dot_over(soften(s), v, 0, 0)
            ).astype(BF16)
    finish(mid, 0)

    for part in range(2):
        for send in sends(part):
            send.wait()
        for r in range(2):
            top = part * 16 + r * 8
            h = from_left[part, r * 32 : r * 32 + 32].astype(F32).reshape(HALF, WIN, 512)
            tiles[top : top + 4, 0] = h
            tiles[top + 4 : top + 8, 0] = turn(h)
            h = from_right[part, r * 32 : r * 32 + 32].astype(F32).reshape(HALF, WIN, 512)
            tiles[top : top + 4, 3] = h
            tiles[top + 4 : top + 8, 3] = turn(h)
    edge0 = shifted(0)
    edge2 = shifted(2)
    edge = jnp.where(low_cell, edge2, edge0).reshape(256, 512)
    qkv_buf[:, :512] = dot(edge.astype(BF16), qkv_s[:, :512]).astype(BF16)
    qkv_buf[:, 512:] = dot(edge0.reshape(256, 512).astype(BF16), qkv_s[:, 512:]).astype(BF16)
    edge_buf[...] = dot(edge2.reshape(256, 512).astype(BF16), qkv_s[:, 512:]).astype(BF16)
    for w in range(4):
        rows = slice(w * CELLS, (w + 1) * CELLS)
        for g in range(4):
            q = spread_heads(qkv_buf[rows, g * 128 : g * 128 + 128])
            k0 = qkv_buf[rows, 512 + g * 128 : 640 + g * 128]
            v0 = qkv_buf[rows, 1024 + g * 128 : 1152 + g * 128]
            k2 = edge_buf[rows, g * 128 : g * 128 + 128]
            v2 = edge_buf[rows, 512 + g * 128 : 640 + g * 128]
            s = jnp.where(low_j, dot_over(k2, q, 1, 1), dot_over(k0, q, 1, 1))
            s = s * scale + bias_s[g] + (mask_both if w == 3 else mask_col)
            p = soften(s).astype(F32)
            p = jnp.concatenate([jnp.where(low_j, p, 0.0), jnp.where(low_j, 0.0, p)], axis=0)
            v = jnp.concatenate([v2, v0], axis=0)
            heads[rows, g * 128 : g * 128 + 128] = gather_heads(
                dot_over(p.astype(BF16), v, 0, 0)
            ).astype(BF16)
    finish(edge, 256)


def front(features, flat, gains, weights):
    vmem = pl.BlockSpec(memory_space=pltpu.VMEM)
    hbm = pl.BlockSpec(memory_space=pl.ANY)
    dma = pltpu.SemaphoreType.DMA
    return pl.pallas_call(
        front_kernel,
        out_shape=jax.ShapeDtypeStruct((512, 512), BF16),
        in_specs=[vmem] * 3 + [hbm] * 6,
        out_specs=vmem,
        scratch_shapes=[pltpu.VMEM(w.shape, BF16) for w in weights]
        + [
            dma((6,)),
            pltpu.VMEM((4, CELLS, 256), F32),
            pltpu.VMEM((4, CELLS, 256), F32),
            pltpu.VMEM((32, 4, WIN, 512), F32),
            pltpu.VMEM((256, 1536), BF16),
            pltpu.VMEM((256, 1024), BF16),
            pltpu.VMEM((256, 512), BF16),
        ]
        + [pltpu.VMEM((2, 64, 512), BF16)] * 4
        + [dma((2, 2)), dma((2, 2))],
        compiler_params=pltpu.CompilerParams(
            collective_id=0, has_side_effects=True, vmem_limit_bytes=60 * 1024 * 1024
        ),
        name="front",
    )(features, flat, gains, *weights)


def flat_tables(table):
    span = 2 * WIN - 1
    grid = table.reshape(span, span, -1) * LOG2E
    grid = jnp.pad(grid, ((0, 1), (0, 1), (0, 0)))
    return grid.reshape(256, -1).T


def slot_ids(route_row, experts, capacity):
    count = route_row.shape[0]
    onehot = (route_row[:, None] == jnp.arange(experts, dtype=jnp.int32)[None, :]).astype(
        jnp.bfloat16
    )
    order = jnp.arange(count, dtype=jnp.int32)
    earlier = (order[None, :] < order[:, None]).astype(jnp.bfloat16)
    ahead = jnp.dot(earlier, onehot, preferred_element_type=jnp.float32)
    position = jnp.sum(ahead * onehot, axis=-1).astype(jnp.int32)
    return route_row * capacity + position


def regroup(grid):
    rolled = jnp.roll(grid, (-HALF, -HALF), (0, 1))
    parts = rolled.reshape((4, WIN, 2, WIN) + grid.shape[2:])
    return jnp.moveaxis(parts, 2, 0).reshape((-1,) + grid.shape[2:])


def ungroup(tokens):
    parts = tokens.reshape((2, 4, WIN, WIN) + tokens.shape[1:])
    grid = jnp.moveaxis(parts, 0, 2).reshape((32, 16) + tokens.shape[1:])
    return jnp.roll(grid, (HALF, HALF), (0, 1))


def local(
    features,
    routes,
    qkv_regular,
    proj_regular,
    table_regular,
    gain_regular,
    mlp_up,
    mlp_down,
    gain_mlp,
    qkv_shifted,
    proj_shifted,
    table_shifted,
    gain_shifted,
    expert_in,
    expert_out,
    gain_expert,
):
    weight_in = lax.all_gather(expert_in[0], "band", axis=1, tiled=True)
    weight_out = lax.all_gather(expert_out[0], "band", axis=0, tiled=True)
    flat = jnp.concatenate([flat_tables(table_regular), flat_tables(table_shifted)], axis=0)
    gains = jnp.stack([gain_regular, gain_mlp, gain_shifted, gain_expert])
    third_out = front(
        features,
        flat,
        gains,
        (qkv_regular, proj_regular, mlp_up, mlp_down, qkv_shifted, proj_shifted),
    )
    model_width = 512
    experts = lax.axis_size("expert")
    capacity = 32
    route_rows = regroup(routes.reshape(32, 16))
    slots = slot_ids(route_rows, experts, capacity)
    place = (slots[None, :] == jnp.arange(experts * capacity, dtype=jnp.int32)[:, None]).astype(
        jnp.bfloat16
    )
    outgoing = jnp.dot(place, third_out, preferred_element_type=jnp.float32).astype(jnp.bfloat16)
    arrived = lax.all_to_all(
        outgoing.reshape(experts, capacity, model_width),
        "expert",
        split_axis=0,
        concat_axis=0,
        tiled=True,
    ).reshape(experts * capacity, model_width)
    hidden = jax.nn.gelu(
        jnp.dot(arrived, weight_in, preferred_element_type=jnp.float32), approximate=False
    ).astype(jnp.bfloat16)
    rows_out = jnp.dot(hidden, weight_out, preferred_element_type=jnp.float32).astype(jnp.bfloat16)
    returned = lax.all_to_all(
        rows_out.reshape(experts, capacity, model_width),
        "expert",
        split_axis=0,
        concat_axis=0,
        tiled=True,
    ).reshape(experts * capacity, model_width)
    take = (slots[:, None] == jnp.arange(experts * capacity, dtype=jnp.int32)[None, :]).astype(
        jnp.bfloat16
    )
    expert_rows = jnp.dot(take, returned, preferred_element_type=jnp.float32)
    encoded = (
        third_out.astype(jnp.float32) + layer_norm(expert_rows.astype(jnp.float32), gain_expert)
    ).astype(jnp.bfloat16)
    return ungroup(encoded)[None]


def solution(mesh):
    return jax.shard_map(
        local,
        mesh=mesh,
        in_specs=(
            P("expert", None, "band", None),
            P("expert", "band", None, None, None),
        )
        + (P(),) * 11
        + (P("expert", None, "band"), P("expert", "band", None), P()),
        out_specs=P("expert", None, "band", None),
        check_vma=False,
    )
```

```python
import functools
import jax
import jax.numpy as jnp
from jax import lax
from jax.experimental import pallas as pl
from jax.experimental.pallas import tpu as pltpu
from jax.sharding import PartitionSpec as P

MESH = pl.DeviceIdType.MESH
F32 = jnp.float32
BF16 = jnp.bfloat16
WIN = 8
HALF = WIN // 2
CELLS = WIN * WIN
LANES = 128
LOG2E = 1.4426950408889634
ROOT_HALF = 0.7071067811865476


def dot(a, b):
    return jnp.dot(a, b, preferred_element_type=F32)


def dot_over(a, b, dim_a, dim_b):
    return lax.dot_general(a, b, (((dim_a,), (dim_b,)), ((), ())), preferred_element_type=F32)


def gelu(v):
    return (0.5 * v) * (1.0 + lax.erf(v * ROOT_HALF))


def layer_norm(values, gain_vec):
    centre = jnp.mean(values, axis=-1, keepdims=True)
    offsets = values - centre
    spread = jnp.mean(offsets * offsets, axis=-1, keepdims=True)
    return offsets * lax.rsqrt(spread + 1e-05) * gain_vec


def turn(tiles):
    return pltpu.roll(tiles, HALF, axis=tiles.ndim - 2)


def cell_is_low(shape):
    return lax.broadcasted_iota(jnp.int32, shape, len(shape) - 2) < HALF


def window_bias(table_ref, pad_ref, bias_ref):
    span = 2 * WIN - 1
    pad_ref[...] = jnp.zeros(pad_ref.shape, F32)
    for a in range(span):
        pad_ref[a * 16 : a * 16 + span, 0:16] = table_ref[a * span : a * span + span, :] * LOG2E
    flat = jnp.transpose(pad_ref[...])
    pitch = 2 * WIN
    width = pitch * pitch
    even = lax.broadcasted_iota(jnp.int32, (WIN, LANES), 1) % pitch < WIN
    for group in range(4):
        for pair in range(2):
            head = group * 4 + pair * 2
            row_even = jnp.broadcast_to(flat[head : head + 1, :], (WIN, width))
            row_odd = jnp.broadcast_to(flat[head + 1 : head + 2, :], (WIN, width))
            for key_row in range(WIN):
                back = (WIN - 1 - key_row) * pitch + WIN - 1
                a = pltpu.roll(row_even, (width - back) % width, axis=1, stride=1, stride_axis=0)
                b = pltpu.roll(
                    row_odd, (width - back + WIN) % width, axis=1, stride=1, stride_axis=0
                )
                bias_ref[
                    group,
                    key_row * WIN : (key_row + 1) * WIN,
                    pair * LANES : (pair + 1) * LANES,
                ] = jnp.where(even, a[:, :LANES], b[:, :LANES])


def spread_heads(q):
    head = lax.broadcasted_iota(jnp.int32, (1, 1, LANES), 2) // 32
    tiles = q.astype(F32).reshape(WIN, WIN, LANES)
    pieces = []
    for pair in range(2):
        both = [jnp.where(head == pair * 2 + k, tiles, 0.0)[:, None] for k in range(2)]
        pieces.append(jnp.concatenate(both, axis=1).reshape(2 * CELLS, LANES))
    return jnp.concatenate(pieces, axis=0).astype(BF16)


def gather_heads(o):
    head = lax.broadcasted_iota(jnp.int32, (1, 1, LANES), 2) // 32
    parts = o.reshape(2, WIN, 2, WIN, LANES)
    low = jnp.where(head == 0, parts[0, :, 0], parts[0, :, 1])
    high = jnp.where(head == 2, parts[1, :, 0], parts[1, :, 1])
    return jnp.where(head < 2, low, high).reshape(CELLS, LANES)


def soften(s):
    e = jnp.exp2(s - jnp.max(s, axis=0, keepdims=True))
    return (e * (1.0 / jnp.sum(e, axis=0, keepdims=True))).astype(BF16)


def front_kernel(
    x_ref,
    table_r_ref,
    table_s_ref,
    gain_r_ref,
    gain_m_ref,
    gain_s_ref,
    qkv_r_hbm,
    proj_r_hbm,
    up_hbm,
    down_hbm,
    qkv_s_hbm,
    proj_s_hbm,
    own_in,
    own_out,
    out_ref,
    got_in,
    got_out,
    qkv_r,
    proj_r,
    up,
    down,
    qkv_s,
    proj_s,
    load_sem,
    pad,
    bias_r,
    bias_s,
    tiles,
    qkv_buf,
    edge_buf,
    heads,
    to_left,
    to_right,
    from_left,
    from_right,
    send_sem,
    recv_sem,
    shard_send,
    shard_recv,
):
    band = lax.axis_index("band")
    bands = lax.axis_size("band")
    right = lax.rem(band + 1, bands)
    left = lax.rem(band + bands - 1, bands)
    loads = [
        pltpu.make_async_copy(src, dst, load_sem.at[n])
        for n, (src, dst) in enumerate(
            (
                (qkv_r_hbm, qkv_r),
                (proj_r_hbm, proj_r),
                (up_hbm, up),
                (down_hbm, down),
                (qkv_s_hbm, qkv_s),
                (proj_s_hbm, proj_s),
            )
        )
    ]
    for load in loads:
        load.start()
    barrier = pltpu.get_barrier_semaphore()
    for other in (left, right):
        pl.semaphore_signal(barrier, inc=1, device_id={"band": other}, device_id_type=MESH)
    pl.semaphore_wait(barrier, 2)

    def shard_sends(own, got, first):
        return [
            pltpu.make_async_remote_copy(
                src_ref=own.at[0],
                dst_ref=got.at[n],
                send_sem=shard_send.at[first + n],
                recv_sem=shard_recv.at[first + n],
                device_id={"band": other},
                device_id_type=MESH,
            )
            for n, other in enumerate((right, left))
        ]

    for send in shard_sends(own_in, got_in, 0):
        send.start()

    scale = LOG2E * 32**-0.5
    window_bias(table_r_ref, pad, bias_r)
    window_bias(table_s_ref, pad, bias_s)
    for load in loads[:4]:
        load.wait()

    def sends(part):
        return [
            pltpu.make_async_remote_copy(
                src_ref=to_left.at[part],
                dst_ref=from_right.at[part],
                send_sem=send_sem.at[0, part],
                recv_sem=recv_sem.at[0, part],
                device_id={"band": left},
                device_id_type=MESH,
            ),
            pltpu.make_async_remote_copy(
                src_ref=to_right.at[part],
                dst_ref=from_left.at[part],
                send_sem=send_sem.at[1, part],
                recv_sem=recv_sem.at[1, part],
                device_id={"band": right},
                device_id_type=MESH,
            ),
        ]

    low_cell = cell_is_low((1, WIN, 512))

    def first_part(part, carry):
        x3 = x_ref[0, pl.ds(part * 16, 16)].astype(F32)
        xf = jnp.concatenate(
            [
                x3[r * 8 : r * 8 + 8, c * 8 : c * 8 + 8, :].reshape(CELLS, 512)
                for r in range(2)
                for c in range(2)
            ],
            axis=0,
        )
        qkv_buf[...] = dot(xf.astype(BF16), qkv_r[...]).astype(BF16)
        for w in range(4):
            rows = slice(w * CELLS, (w + 1) * CELLS)
            for g in range(4):
                q = qkv_buf[rows, g * 128 : g * 128 + 128]
                k = qkv_buf[rows, 512 + g * 128 : 640 + g * 128]
                v = qkv_buf[rows, 1024 + g * 128 : 1152 + g * 128]
                s = dot_over(k, spread_heads(q), 1, 1) * scale + bias_r[g]
                heads[rows, g * 128 : g * 128 + 128] = gather_heads(
                    dot_over(soften(s), v, 0, 0)
                ).astype(BF16)
        first = (xf + layer_norm(dot(heads[...], proj_r[...]), gain_r_ref[...])).astype(BF16)
        total = jnp.zeros((256, 512), F32)
        for f in range(4):
            hidden = gelu(dot(first, up[:, f * 512 : f * 512 + 512])).astype(BF16)
            total = total + dot(hidden, down[f * 512 : f * 512 + 512, :])
        second = (first.astype(F32) + layer_norm(total, gain_m_ref[...])).astype(BF16).astype(F32)
        for r in range(2):
            rows = pl.ds(part * 16 + r * 8, 8)
            w0 = second[r * 128 : r * 128 + 64].reshape(WIN, WIN, 512)
            w1 = second[r * 128 + 64 : r * 128 + 128].reshape(WIN, WIN, 512)
            tiles[rows, 1] = w0
            tiles[rows, 2] = w1
            to_left[part, r * 32 : r * 32 + 32] = (
                jnp.where(low_cell, w0[:HALF], turn(w0[HALF:])).reshape(32, 512).astype(BF16)
            )
            to_right[part, r * 32 : r * 32 + 32] = (
                jnp.where(low_cell, turn(w1[HALF:]), w1[:HALF]).reshape(32, 512).astype(BF16)
            )
        for send in sends(part):
            send.start()
        return carry

    lax.fori_loop(0, 2, first_part, 0)
    for send in shard_sends(own_out, got_out, 2):
        send.start()

    def shifted(column):
        pieces = []
        for w in range(4):
            for start in (w * 8 + 4, (w * 8 + 8) % 32):
                a = tiles[start : start + 4, column]
                b = tiles[start : start + 4, column + 1]
                pieces.append(turn(jnp.where(low_cell, b, a)))
        return jnp.concatenate(pieces, axis=0)

    def finish(x, first_row):
        third = x + layer_norm(dot(heads[...], proj_s[...]), gain_s_ref[...])
        out_ref[first_row : first_row + 256, :] = third.astype(BF16)

    key = lax.broadcasted_iota(jnp.int32, (CELLS, 256), 0)
    lane = lax.broadcasted_iota(jnp.int32, (CELLS, 256), 1)
    low_j = lane % 8 < HALF
    row_apart = (key // 8 < HALF) != ((lane // 16) % 8 < HALF)
    col_apart = ((key % 8 < HALF) != low_j) & (
        (low_j & (band == bands - 1)) | (jnp.logical_not(low_j) & (band == 0))
    )
    mask_row = jnp.where(row_apart, -100.0 * LOG2E, 0.0)
    mask_col = jnp.where(col_apart, -100.0 * LOG2E, 0.0)
    mask_both = jnp.where(row_apart | col_apart, -100.0 * LOG2E, 0.0)

    for load in loads[4:]:
        load.wait()
    mid = shifted(1).reshape(256, 512)
    qkv_buf[...] = dot(mid.astype(BF16), qkv_s[...]).astype(BF16)
    for w in range(4):
        rows = slice(w * CELLS, (w + 1) * CELLS)
        for g in range(4):
            q = qkv_buf[rows, g * 128 : g * 128 + 128]
            k = qkv_buf[rows, 512 + g * 128 : 640 + g * 128]
            v = qkv_buf[rows, 1024 + g * 128 : 1152 + g * 128]
            s = dot_over(k, spread_heads(q), 1, 1) * scale + bias_s[g]
            if w == 3:
                s = s + mask_row
            heads[rows, g * 128 : g * 128 + 128] = gather_heads(
                dot_over(soften(s), v, 0, 0)
            ).astype(BF16)
    finish(mid, 0)

    for part in range(2):
        for send in sends(part):
            send.wait()
        for r in range(2):
            top = part * 16 + r * 8
            h = from_left[part, r * 32 : r * 32 + 32].astype(F32).reshape(HALF, WIN, 512)
            tiles[top : top + 4, 0] = h
            tiles[top + 4 : top + 8, 0] = turn(h)
            h = from_right[part, r * 32 : r * 32 + 32].astype(F32).reshape(HALF, WIN, 512)
            tiles[top : top + 4, 3] = h
            tiles[top + 4 : top + 8, 3] = turn(h)
    edge0 = shifted(0)
    edge2 = shifted(2)
    edge = jnp.where(low_cell, edge2, edge0).reshape(256, 512)
    qkv_buf[:, :512] = dot(edge.astype(BF16), qkv_s[:, :512]).astype(BF16)
    qkv_buf[:, 512:] = dot(edge0.reshape(256, 512).astype(BF16), qkv_s[:, 512:]).astype(BF16)
    edge_buf[...] = dot(edge2.reshape(256, 512).astype(BF16), qkv_s[:, 512:]).astype(BF16)
    for w in range(4):
        rows = slice(w * CELLS, (w + 1) * CELLS)
        for g in range(4):
            q = spread_heads(qkv_buf[rows, g * 128 : g * 128 + 128])
            k0 = qkv_buf[rows, 512 + g * 128 : 640 + g * 128]
            v0 = qkv_buf[rows, 1024 + g * 128 : 1152 + g * 128]
            k2 = edge_buf[rows, g * 128 : g * 128 + 128]
            v2 = edge_buf[rows, 512 + g * 128 : 640 + g * 128]
            s = jnp.where(low_j, dot_over(k2, q, 1, 1), dot_over(k0, q, 1, 1))
            s = s * scale + bias_s[g] + (mask_both if w == 3 else mask_col)
            p = soften(s).astype(F32)
            p = jnp.concatenate([jnp.where(low_j, p, 0.0), jnp.where(low_j, 0.0, p)], axis=0)
            v = jnp.concatenate([v2, v0], axis=0)
            heads[rows, g * 128 : g * 128 + 128] = gather_heads(
                dot_over(p.astype(BF16), v, 0, 0)
            ).astype(BF16)
    finish(edge, 256)
    for send in shard_sends(own_in, got_in, 0) + shard_sends(own_out, got_out, 2):
        send.wait()


def front(features, tables, gains, weights, shards):
    vmem = pl.BlockSpec(memory_space=pltpu.VMEM)
    hbm = pl.BlockSpec(memory_space=pl.ANY)
    dma = pltpu.SemaphoreType.DMA
    pair = jax.ShapeDtypeStruct((2, 512, 512), BF16)
    return pl.pallas_call(
        front_kernel,
        out_shape=(jax.ShapeDtypeStruct((512, 512), BF16), pair, pair),
        in_specs=[vmem] * 6 + [hbm] * 8,
        out_specs=(vmem, hbm, hbm),
        scratch_shapes=[pltpu.VMEM(w.shape, BF16) for w in weights]
        + [
            dma((6,)),
            pltpu.VMEM((256, 128), F32),
            pltpu.VMEM((4, CELLS, 256), F32),
            pltpu.VMEM((4, CELLS, 256), F32),
            pltpu.VMEM((32, 4, WIN, 512), F32),
            pltpu.VMEM((256, 1536), BF16),
            pltpu.VMEM((256, 1024), BF16),
            pltpu.VMEM((256, 512), BF16),
        ]
        + [pltpu.VMEM((2, 64, 512), BF16)] * 4
        + [dma((2, 2)), dma((2, 2)), dma((4,)), dma((4,))],
        compiler_params=pltpu.CompilerParams(
            collective_id=0, has_side_effects=True, vmem_limit_bytes=60 * 1024 * 1024
        ),
        name="front",
    )(features, *tables, *gains, *weights, *shards)


AWAY = sorted(
    ((z, x) for z in range(4) for x in range(4)),
    key=lambda d: (min(d[0], 4 - d[0]) + min(d[1], 4 - d[1]), d),
)
PEERS = 32
CAP = 32
GROUPS = 4
PER_GROUP = PEERS // GROUPS
ROWS = PER_GROUP * CAP


def moe_kernel(
    third_ref,
    routes_ref,
    gain_ref,
    own_in,
    own_out,
    got_in,
    got_out,
    enc_ref,
    w_in,
    w_out,
    load_sem,
    outgoing,
    arrived,
    total,
    result,
    returned,
    take,
    go_send,
    go_recv,
    back_send,
    back_recv,
    far_send,
    far_recv,
):
    band = lax.axis_index("band")
    bands = lax.axis_size("band")
    right = lax.rem(band + 1, bands)
    left = lax.rem(band + bands - 1, bands)
    me = lax.axis_index("expert")
    my_z, my_x, my_core = me // 8, (me // 2) % 4, me % 2

    def peer(place, sign):
        z, x = AWAY[place // 2]
        return (
            (my_z + 4 + sign * z) % 4 * 4 + (my_x + 4 + sign * x) % 4
        ) * 2 + (my_core + place % 2) % 2

    barrier = pltpu.get_barrier_semaphore()
    for place in range(1, PEERS):
        pl.semaphore_signal(
            barrier, inc=1, device_id={"expert": peer(place, 1)}, device_id_type=MESH
        )
    for other in (left, right):
        pl.semaphore_signal(barrier, inc=1, device_id={"band": other}, device_id_type=MESH)

    loads = [
        pltpu.make_async_copy(src, dst, load_sem.at[n])
        for n, (src, dst) in enumerate(
            (
                (own_in.at[0], w_in.at[0]),
                (own_out.at[0], w_out.at[0]),
                (got_in.at[0], w_in.at[1]),
                (got_out.at[0], w_out.at[1]),
                (got_in.at[1], w_in.at[2]),
                (got_out.at[1], w_out.at[2]),
            )
        )
    ]
    for load in loads:
        load.start()
    fars = [
        pltpu.make_async_remote_copy(
            src_ref=src,
            dst_ref=dst.at[3],
            send_sem=far_send.at[n],
            recv_sem=far_recv.at[n],
            device_id={"band": other},
            device_id_type=MESH,
        )
        for n, (src, dst, other) in enumerate(
            ((got_in.at[0], w_in, right), (got_out.at[1], w_out, left))
        )
    ]
    goes = [
        pltpu.make_async_remote_copy(
            src_ref=outgoing.at[place],
            dst_ref=arrived.at[place],
            send_sem=go_send.at[place],
            recv_sem=go_recv.at[place],
            device_id={"expert": peer(place, 1)},
            device_id_type=MESH,
        )
        for place in range(1, PEERS)
    ]
    backs = [
        pltpu.make_async_remote_copy(
            src_ref=result.at[place],
            dst_ref=returned.at[place],
            send_sem=back_send.at[place],
            recv_sem=back_recv.at[place],
            device_id={"expert": peer(place, -1)},
            device_id_type=MESH,
        )
        for place in range(1, PEERS)
    ]

    routes = routes_ref[...]
    code = (((routes >> 3) - my_z) & 3) * 4 + (((routes >> 1) - my_x) & 3)
    spot = jnp.zeros_like(routes)
    for n, (z, x) in enumerate(AWAY):
        spot = jnp.where(code == z * 4 + x, n, spot)
    spot = spot * 2 + ((routes - my_core) & 1)
    chosen = lax.broadcasted_iota(jnp.int32, (PEERS, 512), 0) == spot
    onehot = jnp.where(chosen, 1.0, 0.0)
    before = lax.broadcasted_iota(jnp.int32, (512, 512), 0) < lax.broadcasted_iota(
        jnp.int32, (512, 512), 1
    )
    ahead = dot(onehot.astype(BF16), jnp.where(before, 1.0, 0.0).astype(BF16))
    slot = spot.astype(F32) * CAP + jnp.sum(onehot * ahead, axis=0, keepdims=True)

    third = third_ref[...]
    for g in range(GROUPS):
        rows = (lax.broadcasted_iota(jnp.int32, (ROWS, 512), 0) + g * ROWS).astype(F32)
        place = jnp.where(rows == slot, 1.0, 0.0).astype(BF16)
        block = dot(place, third).astype(BF16).reshape(PER_GROUP, CAP, 512)
        if g == 0:
            arrived[0] = block[0]
            outgoing[1:PER_GROUP] = block[1:]
        else:
            outgoing[g * PER_GROUP : (g + 1) * PER_GROUP] = block
        if g == 0:
            pl.semaphore_wait(barrier, PEERS - 1 + 2)
            for far in fars:
                far.start()
        for go in goes[max(g * PER_GROUP - 1, 0) : (g + 1) * PER_GROUP - 1]:
            go.start()

    slot_column = jnp.transpose(jnp.broadcast_to(slot, (LANES, 512)))
    lane = lax.broadcasted_iota(jnp.int32, (512, LANES), 1).astype(F32)
    for n in range(PEERS * CAP // LANES):
        take[:, n * LANES : (n + 1) * LANES] = jnp.where(
            slot_column == lane + n * LANES, 1.0, 0.0
        ).astype(BF16)

    def layer(rows, n):
        hidden = gelu(dot(rows, w_in[n])).astype(BF16)
        return dot(hidden, w_out[n])

    for load in loads:
        load.wait()
    for g in range(GROUPS):
        for go in goes[max(g * PER_GROUP - 1, 0) : (g + 1) * PER_GROUP - 1]:
            go.wait_recv()
        rows = arrived[g * PER_GROUP : (g + 1) * PER_GROUP].reshape(ROWS, 512)
        total[g * ROWS : (g + 1) * ROWS] = layer(rows, 0) + layer(rows, 1) + layer(rows, 2)
    for far in fars:
        far.wait()
    for g in range(GROUPS):
        rows = arrived[g * PER_GROUP : (g + 1) * PER_GROUP].reshape(ROWS, 512)
        block = (total[g * ROWS : (g + 1) * ROWS] + layer(rows, 3)).astype(BF16)
        block = block.reshape(PER_GROUP, CAP, 512)
        if g == 0:
            returned[0] = block[0]
            result[1:PER_GROUP] = block[1:]
        else:
            result[g * PER_GROUP : (g + 1) * PER_GROUP] = block
        for back in backs[max(g * PER_GROUP - 1, 0) : (g + 1) * PER_GROUP - 1]:
            back.start()
    for go in goes:
        go.wait_send()
    for back in backs:
        back.wait()
    rows = dot(take[...], returned[...].reshape(PEERS * CAP, 512))
    encoded = third.astype(F32) + layer_norm(rows, gain_ref[...])
    low_cell = cell_is_low((1, WIN, 512))
    for w in range(4):
        mid = encoded[w * CELLS : (w + 1) * CELLS].reshape(WIN, WIN, 512)
        edge = encoded[256 + w * CELLS : 256 + (w + 1) * CELLS].reshape(WIN, WIN, 512)
        w0 = turn(jnp.where(low_cell, mid, edge))
        w1 = turn(jnp.where(low_cell, edge, mid))
        block = jnp.concatenate([w0, w1], axis=1).astype(BF16)
        for half in range(2):
            top = (w * 8 + 4 + half * 4) % 32
            enc_ref[0, top : top + 4] = block[half * 4 : half * 4 + 4]


def moe(third, routes, gain, shards, got):
    vmem = pl.BlockSpec(memory_space=pltpu.VMEM)
    hbm = pl.BlockSpec(memory_space=pl.ANY)
    dma = pltpu.SemaphoreType.DMA
    return pl.pallas_call(
        moe_kernel,
        out_shape=jax.ShapeDtypeStruct((1, 32, 16, 512), BF16),
        in_specs=[vmem] * 3 + [hbm] * 4,
        out_specs=vmem,
        scratch_shapes=[
            pltpu.VMEM((4, 512, 512), BF16),
            pltpu.VMEM((4, 512, 512), BF16),
            dma((6,)),
            pltpu.VMEM((PEERS, CAP, 512), BF16),
            pltpu.VMEM((PEERS, CAP, 512), BF16),
            pltpu.VMEM((PEERS * CAP, 512), F32),
            pltpu.VMEM((PEERS, CAP, 512), BF16),
            pltpu.VMEM((PEERS, CAP, 512), BF16),
            pltpu.VMEM((512, PEERS * CAP), BF16),
        ]
        + [dma((PEERS,))] * 4
        + [dma((2,))] * 2,
        compiler_params=pltpu.CompilerParams(
            collective_id=1, has_side_effects=True, vmem_limit_bytes=60 * 1024 * 1024
        ),
        name="moe",
    )(third, routes, gain, *shards, *got)


def regroup(grid):
    rolled = jnp.roll(grid, (-HALF, -HALF), (0, 1))
    return rolled.reshape(4, WIN, 2, WIN).transpose(2, 0, 1, 3)


def local(
    features,
    routes,
    qkv_regular,
    proj_regular,
    table_regular,
    gain_regular,
    mlp_up,
    mlp_down,
    gain_mlp,
    qkv_shifted,
    proj_shifted,
    table_shifted,
    gain_shifted,
    expert_in,
    expert_out,
    gain_expert,
):
    shards = (expert_in, expert_out)
    third, *got = front(
        features,
        (table_regular, table_shifted),
        [g.reshape(1, 512) for g in (gain_regular, gain_mlp, gain_shifted)],
        (qkv_regular, proj_regular, mlp_up, mlp_down, qkv_shifted, proj_shifted),
        shards,
    )
    order = regroup(routes.reshape(32, 16)).reshape(1, 512)
    return moe(third, order, gain_expert.reshape(1, 512), shards, got)


def solution(mesh):
    return jax.shard_map(
        local,
        mesh=mesh,
        in_specs=(
            P("expert", None, "band", None),
            P("expert", "band", None, None, None),
        )
        + (P(),) * 11
        + (P("expert", None, "band"), P("expert", "band", None), P()),
        out_specs=P("expert", None, "band", None),
        check_vma=False,
    )
```

```python
import functools
import jax
import jax.numpy as jnp
from jax import lax
from jax.experimental import pallas as pl
from jax.experimental.pallas import tpu as pltpu
from jax.sharding import PartitionSpec as P

MESH = pl.DeviceIdType.MESH
F32 = jnp.float32
BF16 = jnp.bfloat16
WIN = 8
HALF = WIN // 2
CELLS = WIN * WIN
LANES = 128
LOG2E = 1.4426950408889634
ROOT_HALF = 0.7071067811865476


def dot(a, b):
    return jnp.dot(a, b, preferred_element_type=F32)


def dot_over(a, b, dim_a, dim_b):
    return lax.dot_general(a, b, (((dim_a,), (dim_b,)), ((), ())), preferred_element_type=F32)


def gelu(v):
    return (0.5 * v) * (1.0 + lax.erf(v * ROOT_HALF))


def layer_norm(values, gain_vec):
    centre = jnp.mean(values, axis=-1, keepdims=True)
    offsets = values - centre
    spread = jnp.mean(offsets * offsets, axis=-1, keepdims=True)
    return offsets * lax.rsqrt(spread + 1e-05) * gain_vec


def turn(tiles):
    return pltpu.roll(tiles, HALF, axis=tiles.ndim - 2)


def cell_is_low(shape):
    return lax.broadcasted_iota(jnp.int32, shape, len(shape) - 2) < HALF


def window_bias(table_ref, pad_ref, bias_ref):
    span = 2 * WIN - 1
    pitch = 2 * WIN
    width = pitch * pitch
    pad_ref[...] = jnp.zeros(pad_ref.shape, F32)
    pad_ref[:, : span * span] = table_ref[...] * LOG2E
    packed = pad_ref[...]
    line = lax.broadcasted_iota(jnp.int32, packed.shape, 1) // pitch
    flat = packed
    for a in range(1, span):
        flat = jnp.where(line == a, pltpu.roll(packed, a, axis=1), flat)
    even = lax.broadcasted_iota(jnp.int32, (WIN, LANES), 1) % pitch < WIN
    for group in range(4):
        for pair in range(2):
            head = group * 4 + pair * 2
            row_even = jnp.broadcast_to(flat[head : head + 1, :], (WIN, width))
            row_odd = jnp.broadcast_to(flat[head + 1 : head + 2, :], (WIN, width))
            for key_row in range(WIN):
                back = (WIN - 1 - key_row) * pitch + WIN - 1
                a = pltpu.roll(row_even, (width - back) % width, axis=1, stride=1, stride_axis=0)
                b = pltpu.roll(
                    row_odd, (width - back + WIN) % width, axis=1, stride=1, stride_axis=0
                )
                bias_ref[
                    group,
                    key_row * WIN : (key_row + 1) * WIN,
                    pair * LANES : (pair + 1) * LANES,
                ] = jnp.where(even, a[:, :LANES], b[:, :LANES])


def spread_heads(q):
    head = lax.broadcasted_iota(jnp.int32, (1, 1, LANES), 2) // 32
    tiles = q.astype(F32).reshape(WIN, WIN, LANES)
    pieces = []
    for pair in range(2):
        both = [jnp.where(head == pair * 2 + k, tiles, 0.0)[:, None] for k in range(2)]
        pieces.append(jnp.concatenate(both, axis=1).reshape(2 * CELLS, LANES))
    return jnp.concatenate(pieces, axis=0).astype(BF16)


def gather_heads(o):
    head = lax.broadcasted_iota(jnp.int32, (1, 1, LANES), 2) // 32
    parts = o.reshape(2, WIN, 2, WIN, LANES)
    low = jnp.where(head == 0, parts[0, :, 0], parts[0, :, 1])
    high = jnp.where(head == 2, parts[1, :, 0], parts[1, :, 1])
    return jnp.where(head < 2, low, high).reshape(CELLS, LANES)


def soften(s):
    e = jnp.exp2(s - jnp.max(s, axis=0, keepdims=True))
    return (e * (1.0 / jnp.sum(e, axis=0, keepdims=True))).astype(BF16)


AWAY = sorted(
    ((z, x) for z in range(4) for x in range(4)),
    key=lambda d: (min(d[0], 4 - d[0]) + min(d[1], 4 - d[1]), d),
)
PEERS = 32
CAP = 32
GROUPS = 4
PER_GROUP = PEERS // GROUPS
ROWS = PER_GROUP * CAP


def token_routes(routes_ref):
    grid = routes_ref[...].reshape(16, 32).astype(F32).astype(BF16)
    token = lax.broadcasted_iota(jnp.int32, (32, 512), 1)
    row = ((token // 64) % 4 * 8 + 4 + (token // 8) % 8) % 32
    at_row = jnp.where(lax.broadcasted_iota(jnp.int32, (32, 512), 0) == row, 1.0, 0.0)
    token = lax.broadcasted_iota(jnp.int32, (16, 512), 1)
    cell = token % 8
    column = jnp.where(token < 256, HALF + cell, (cell + 12) % 16)
    at_column = lax.broadcasted_iota(jnp.int32, (16, 512), 0) == column
    picked = jnp.where(at_column, dot(grid, at_row.astype(BF16)), 0.0)
    return jnp.sum(picked, axis=0, keepdims=True).astype(jnp.int32)


def kernel(
    x_ref,
    routes_ref,
    table_r_ref,
    table_s_ref,
    gain_r_ref,
    gain_m_ref,
    gain_s_ref,
    gain_e_ref,
    qkv_r_hbm,
    proj_r_hbm,
    up_hbm,
    down_hbm,
    qkv_s_hbm,
    proj_s_hbm,
    own_in,
    own_out,
    enc_ref,
    qkv_r,
    proj_r,
    up,
    down,
    qkv_s,
    proj_s,
    load_sem,
    pad,
    bias_r,
    bias_s,
    tiles,
    qkv_buf,
    edge_buf,
    heads,
    third_buf,
    to_left,
    to_right,
    from_left,
    from_right,
    send_sem,
    recv_sem,
    shard_send,
    shard_recv,
    w_in,
    w_out,
    place,
    take,
    outgoing,
    arrived,
    result,
    returned,
    go_send,
    go_recv,
    back_send,
    back_recv,
):
    band = lax.axis_index("band")
    bands = lax.axis_size("band")
    right = lax.rem(band + 1, bands)
    left = lax.rem(band + bands - 1, bands)
    me = lax.axis_index("expert")
    my_z, my_x, my_core = me // 8, (me // 2) % 4, me % 2

    def peer(n, sign):
        z, x = AWAY[n // 2]
        return (
            (my_z + 4 + sign * z) % 4 * 4 + (my_x + 4 + sign * x) % 4
        ) * 2 + (my_core + n % 2) % 2

    barrier = pltpu.get_barrier_semaphore()
    for n in range(1, PEERS):
        pl.semaphore_signal(barrier, inc=1, device_id={"expert": peer(n, 1)}, device_id_type=MESH)
    for other in (left, right):
        pl.semaphore_signal(barrier, inc=1, device_id={"band": other}, device_id_type=MESH)

    loads = [
        pltpu.make_async_copy(src, dst, load_sem.at[n])
        for n, (src, dst) in enumerate(
            (
                (qkv_r_hbm, qkv_r),
                (proj_r_hbm, proj_r),
                (up_hbm, up),
                (down_hbm, down),
                (qkv_s_hbm, qkv_s),
                (proj_s_hbm, proj_s),
                (own_in.at[0], w_in.at[0]),
                (own_out.at[0], w_out.at[0]),
            )
        )
    ]
    for load in loads:
        load.start()

    def remote(src, dst, send_sem, recv_sem, to):
        return pltpu.make_async_remote_copy(
            src_ref=src,
            dst_ref=dst,
            send_sem=send_sem,
            recv_sem=recv_sem,
            device_id=to,
            device_id_type=MESH,
        )

    def shard(n):
        to = {"band": left if n % 2 else right}
        if n < 2:
            src, dst = own_in.at[0], w_in.at[1 + n]
        elif n < 6:
            rows = pl.ds((n // 2 - 1) * 256, 256)
            src, dst = own_out.at[0, rows], w_out.at[1 + n % 2, rows]
        elif n == 6:
            src, dst = w_in.at[1], w_in.at[3]
        else:
            src, dst = w_out.at[2], w_out.at[3]
        return remote(src, dst, shard_send.at[n], shard_recv.at[n], to)

    def go(n):
        to = {"expert": peer(n, 1)}
        return remote(outgoing.at[n], arrived.at[n], go_send.at[n], go_recv.at[n], to)

    def back(n):
        to = {"expert": peer(n, -1)}
        return remote(result.at[n], returned.at[n], back_send.at[n], back_recv.at[n], to)

    routes = token_routes(routes_ref)
    code = (((routes >> 3) - my_z) & 3) * 4 + (((routes >> 1) - my_x) & 3)
    spot = jnp.zeros_like(routes)
    for n, (z, x) in enumerate(AWAY):
        spot = jnp.where(code == z * 4 + x, n, spot)
    spot = spot * 2 + ((routes - my_core) & 1)
    chosen = lax.broadcasted_iota(jnp.int32, (PEERS, 512), 0) == spot
    onehot = jnp.where(chosen, 1.0, 0.0)
    before = lax.broadcasted_iota(jnp.int32, (512, 512), 0) < lax.broadcasted_iota(
        jnp.int32, (512, 512), 1
    )
    ahead = dot(onehot.astype(BF16), jnp.where(before, 1.0, 0.0).astype(BF16))
    slot = spot.astype(F32) * CAP + jnp.sum(onehot * ahead, axis=0, keepdims=True)
    for g in range(GROUPS):
        rows = (lax.broadcasted_iota(jnp.int32, (ROWS, 512), 0) + g * ROWS).astype(F32)
        place[g * ROWS : (g + 1) * ROWS] = jnp.where(rows == slot, 1.0, 0.0).astype(BF16)
    slot_column = jnp.transpose(jnp.broadcast_to(slot, (LANES, 512)))
    lane = lax.broadcasted_iota(jnp.int32, (512, LANES), 1).astype(F32)
    for n in range(PEERS * CAP // LANES):
        take[:, n * LANES : (n + 1) * LANES] = jnp.where(
            slot_column == lane + n * LANES, 1.0, 0.0
        ).astype(BF16)
    scale = LOG2E * 32**-0.5
    window_bias(table_r_ref, pad, bias_r)
    window_bias(table_s_ref, pad, bias_s)

    pl.semaphore_wait(barrier, PEERS - 1 + 2)
    for n in range(2):
        shard(n).start()
    for load in loads[:4]:
        load.wait()

    def sends(part):
        return [
            remote(
                to_left.at[part],
                from_right.at[part],
                send_sem.at[0, part],
                recv_sem.at[0, part],
                {"band": left},
            ),
            remote(
                to_right.at[part],
                from_left.at[part],
                send_sem.at[1, part],
                recv_sem.at[1, part],
                {"band": right},
            ),
        ]

    low_cell = cell_is_low((1, WIN, 512))

    def first_part(part, carry):
        x3 = x_ref[0, pl.ds(part * 16, 16)].astype(F32)
        xf = jnp.concatenate(
            [
                x3[r * 8 : r * 8 + 8, c * 8 : c * 8 + 8, :].reshape(CELLS, 512)
                for r in range(2)
                for c in range(2)
            ],
            axis=0,
        )
        qkv_buf[...] = dot(xf.astype(BF16), qkv_r[...]).astype(BF16)
        for w in range(4):
            rows = slice(w * CELLS, (w + 1) * CELLS)
            for g in range(4):
                q = qkv_buf[rows, g * 128 : g * 128 + 128]
                k = qkv_buf[rows, 512 + g * 128 : 640 + g * 128]
                v = qkv_buf[rows, 1024 + g * 128 : 1152 + g * 128]
                s = dot_over(k, spread_heads(q), 1, 1) * scale + bias_r[g]
                heads[rows, g * 128 : g * 128 + 128] = gather_heads(
                    dot_over(soften(s), v, 0, 0)
                ).astype(BF16)
        first = (xf + layer_norm(dot(heads[...], proj_r[...]), gain_r_ref[...])).astype(BF16)
        total = jnp.zeros((256, 512), F32)
        for f in range(4):
            hidden = gelu(dot(first, up[:, f * 512 : f * 512 + 512])).astype(BF16)
            total = total + dot(hidden, down[f * 512 : f * 512 + 512, :])
        second = (first.astype(F32) + layer_norm(total, gain_m_ref[...])).astype(BF16).astype(F32)
        for r in range(2):
            rows = pl.ds(part * 16 + r * 8, 8)
            w0 = second[r * 128 : r * 128 + 64].reshape(WIN, WIN, 512)
            w1 = second[r * 128 + 64 : r * 128 + 128].reshape(WIN, WIN, 512)
            tiles[rows, 1] = w0
            tiles[rows, 2] = w1
            to_left[part, r * 32 : r * 32 + 32] = (
                jnp.where(low_cell, w0[:HALF], turn(w0[HALF:])).reshape(32, 512).astype(BF16)
            )
            to_right[part, r * 32 : r * 32 + 32] = (
                jnp.where(low_cell, turn(w1[HALF:]), w1[:HALF]).reshape(32, 512).astype(BF16)
            )
        for send in sends(part):
            send.start()

        @pl.when(part == 0)
        def _():
            for n in (2, 3):
                shard(n).start()

        return carry

    lax.fori_loop(0, 2, first_part, 0)
    for n in (4, 5):
        shard(n).start()
    shard(0).wait_recv()
    shard(6).start()

    def shifted(column):
        pieces = []
        for w in range(4):
            for start in (w * 8 + 4, (w * 8 + 8) % 32):
                a = tiles[start : start + 4, column]
                b = tiles[start : start + 4, column + 1]
                pieces.append(turn(jnp.where(low_cell, b, a)))
        return jnp.concatenate(pieces, axis=0)

    def finish(x, first_row):
        third = x + layer_norm(dot(heads[...], proj_s[...]), gain_s_ref[...])
        third_buf[first_row : first_row + 256, :] = third.astype(BF16)

    key = lax.broadcasted_iota(jnp.int32, (CELLS, 256), 0)
    lane = lax.broadcasted_iota(jnp.int32, (CELLS, 256), 1)
    low_j = lane % 8 < HALF
    row_apart = (key // 8 < HALF) != ((lane // 16) % 8 < HALF)
    col_apart = ((key % 8 < HALF) != low_j) & (
        (low_j & (band == bands - 1)) | (jnp.logical_not(low_j) & (band == 0))
    )
    mask_row = jnp.where(row_apart, -100.0 * LOG2E, 0.0)
    mask_col = jnp.where(col_apart, -100.0 * LOG2E, 0.0)
    mask_both = jnp.where(row_apart | col_apart, -100.0 * LOG2E, 0.0)

    for load in loads[4:6]:
        load.wait()
    mid = shifted(1).reshape(256, 512)
    qkv_buf[...] = dot(mid.astype(BF16), qkv_s[...]).astype(BF16)
    for w in range(4):
        rows = slice(w * CELLS, (w + 1) * CELLS)
        for g in range(4):
            q = qkv_buf[rows, g * 128 : g * 128 + 128]
            k = qkv_buf[rows, 512 + g * 128 : 640 + g * 128]
            v = qkv_buf[rows, 1024 + g * 128 : 1152 + g * 128]
            s = dot_over(k, spread_heads(q), 1, 1) * scale + bias_s[g]
            if w == 3:
                s = s + mask_row
            heads[rows, g * 128 : g * 128 + 128] = gather_heads(
                dot_over(soften(s), v, 0, 0)
            ).astype(BF16)
    finish(mid, 0)

    for part in range(2):
        for send in sends(part):
            send.wait()
        for r in range(2):
            top = part * 16 + r * 8
            h = from_left[part, r * 32 : r * 32 + 32].astype(F32).reshape(HALF, WIN, 512)
            tiles[top : top + 4, 0] = h
            tiles[top + 4 : top + 8, 0] = turn(h)
            h = from_right[part, r * 32 : r * 32 + 32].astype(F32).reshape(HALF, WIN, 512)
            tiles[top : top + 4, 3] = h
            tiles[top + 4 : top + 8, 3] = turn(h)
    edge0 = shifted(0)
    edge2 = shifted(2)
    edge = jnp.where(low_cell, edge2, edge0).reshape(256, 512)
    qkv_buf[:, :512] = dot(edge.astype(BF16), qkv_s[:, :512]).astype(BF16)
    qkv_buf[:, 512:] = dot(edge0.reshape(256, 512).astype(BF16), qkv_s[:, 512:]).astype(BF16)
    edge_buf[...] = dot(edge2.reshape(256, 512).astype(BF16), qkv_s[:, 512:]).astype(BF16)
    for w in range(4):
        rows = slice(w * CELLS, (w + 1) * CELLS)
        for g in range(4):
            q = spread_heads(qkv_buf[rows, g * 128 : g * 128 + 128])
            k0 = qkv_buf[rows, 512 + g * 128 : 640 + g * 128]
            v0 = qkv_buf[rows, 1024 + g * 128 : 1152 + g * 128]
            k2 = edge_buf[rows, g * 128 : g * 128 + 128]
            v2 = edge_buf[rows, 512 + g * 128 : 640 + g * 128]
            s = jnp.where(low_j, dot_over(k2, q, 1, 1), dot_over(k0, q, 1, 1))
            s = s * scale + bias_s[g] + (mask_both if w == 3 else mask_col)
            p = soften(s).astype(F32)
            p = jnp.concatenate([jnp.where(low_j, p, 0.0), jnp.where(low_j, 0.0, p)], axis=0)
            v = jnp.concatenate([v2, v0], axis=0)
            heads[rows, g * 128 : g * 128 + 128] = gather_heads(
                dot_over(p.astype(BF16), v, 0, 0)
            ).astype(BF16)
    finish(edge, 256)

    groups = range(GROUPS)[::-1]

    def places(g):
        return range(max(g * PER_GROUP, 1), (g + 1) * PER_GROUP)[::-1]

    third = third_buf[...]
    for g in groups:
        block = dot(place[g * ROWS : (g + 1) * ROWS], third).astype(BF16)
        block = block.reshape(PER_GROUP, CAP, 512)
        if g == 0:
            arrived[0] = block[0]
            outgoing[1:PER_GROUP] = block[1:]
        else:
            outgoing[g * PER_GROUP : (g + 1) * PER_GROUP] = block
        for n in places(g):
            go(n).start()

    for n in (3, 5):
        shard(n).wait_recv()
    shard(7).start()
    for n in (1, 2, 4):
        shard(n).wait_recv()
    for load in loads[6:]:
        load.wait()

    def layer(rows, n):
        hidden = gelu(dot(rows, w_in[n])).astype(BF16)
        return dot(hidden, w_out[n])

    for g in groups:
        for n in places(g):
            go(n).wait_recv()
        rows = arrived[g * PER_GROUP : (g + 1) * PER_GROUP].reshape(ROWS, 512)
        total = layer(rows, 0) + layer(rows, 1) + layer(rows, 2)
        if g == GROUPS - 1:
            for n in (6, 7):
                shard(n).wait_recv()
        block = (total + layer(rows, 3)).astype(BF16).reshape(PER_GROUP, CAP, 512)
        if g == 0:
            returned[0] = block[0]
            result[1:PER_GROUP] = block[1:]
        else:
            result[g * PER_GROUP : (g + 1) * PER_GROUP] = block
        for n in places(g):
            back(n).start()
    for n in range(8):
        shard(n).wait_send()
    rows = jnp.zeros((512, 512), F32)
    for g in groups:
        for n in places(g):
            back(n).wait_recv()
        block = returned[g * PER_GROUP : (g + 1) * PER_GROUP].reshape(ROWS, 512)
        rows = rows + dot(take[:, g * ROWS : (g + 1) * ROWS], block)
    encoded = third_buf[...].astype(F32) + layer_norm(rows, gain_e_ref[...])
    for w in range(4):
        mid = encoded[w * CELLS : (w + 1) * CELLS].reshape(WIN, WIN, 512)
        edge = encoded[256 + w * CELLS : 256 + (w + 1) * CELLS].reshape(WIN, WIN, 512)
        w0 = turn(jnp.where(low_cell, mid, edge))
        w1 = turn(jnp.where(low_cell, edge, mid))
        block = jnp.concatenate([w0, w1], axis=1).astype(BF16)
        for half in range(2):
            top = (w * 8 + 4 + half * 4) % 32
            enc_ref[0, top : top + 4] = block[half * 4 : half * 4 + 4]
    for g in groups:
        for n in places(g):
            go(n).wait_send()
            back(n).wait_send()


def block_pair(features, routes, tables, gains, weights, shards):
    vmem = pl.BlockSpec(memory_space=pltpu.VMEM)
    hbm = pl.BlockSpec(memory_space=pl.ANY)
    dma = pltpu.SemaphoreType.DMA
    return pl.pallas_call(
        kernel,
        out_shape=jax.ShapeDtypeStruct((1, 32, 16, 512), BF16),
        in_specs=[vmem] * 8 + [hbm] * 8,
        out_specs=vmem,
        scratch_shapes=[pltpu.VMEM(w.shape, BF16) for w in weights]
        + [
            dma((8,)),
            pltpu.VMEM((16, 256), F32),
            pltpu.VMEM((4, CELLS, 256), F32),
            pltpu.VMEM((4, CELLS, 256), F32),
            pltpu.VMEM((32, 4, WIN, 512), F32),
            pltpu.VMEM((256, 1536), BF16),
            pltpu.VMEM((256, 1024), BF16),
            pltpu.VMEM((256, 512), BF16),
            pltpu.VMEM((512, 512), BF16),
        ]
        + [pltpu.VMEM((2, 64, 512), BF16)] * 4
        + [dma((2, 2)), dma((2, 2)), dma((8,)), dma((8,))]
        + [
            pltpu.VMEM((4, 512, 512), BF16),
            pltpu.VMEM((4, 512, 512), BF16),
            pltpu.VMEM((PEERS * CAP, 512), BF16),
            pltpu.VMEM((512, PEERS * CAP), BF16),
        ]
        + [pltpu.VMEM((PEERS, CAP, 512), BF16)] * 4
        + [dma((PEERS,))] * 4,
        compiler_params=pltpu.CompilerParams(
            collective_id=0, has_side_effects=True, vmem_limit_bytes=62 * 1024 * 1024
        ),
        name="block_pair",
    )(features, routes, *tables, *gains, *weights, *shards)


def local(
    features,
    routes,
    qkv_regular,
    proj_regular,
    table_regular,
    gain_regular,
    mlp_up,
    mlp_down,
    gain_mlp,
    qkv_shifted,
    proj_shifted,
    table_shifted,
    gain_shifted,
    expert_in,
    expert_out,
    gain_expert,
):
    gains = (gain_regular, gain_mlp, gain_shifted, gain_expert)
    return block_pair(
        features,
        routes.reshape(32, 16).T.reshape(16, 1, 32),
        (table_regular.T, table_shifted.T),
        [g.reshape(1, 512) for g in gains],
        (qkv_regular, proj_regular, mlp_up, mlp_down, qkv_shifted, proj_shifted),
        (expert_in, expert_out),
    )


def solution(mesh):
    return jax.shard_map(
        local,
        mesh=mesh,
        in_specs=(
            P("expert", None, "band", None),
            P("expert", "band", None, None, None),
        )
        + (P(),) * 11
        + (P("expert", None, "band"), P("expert", "band", None), P()),
        out_specs=P("expert", None, "band", None),
        check_vma=False,
    )
```

```python
import functools
import jax
import jax.numpy as jnp
from jax import lax
from jax.experimental import pallas as pl
from jax.experimental.pallas import tpu as pltpu
from jax.sharding import PartitionSpec as P

MESH = pl.DeviceIdType.MESH
F32 = jnp.float32
BF16 = jnp.bfloat16
WIN = 8
HALF = WIN // 2
CELLS = WIN * WIN
LANES = 128
LOG2E = 1.4426950408889634
ROOT_HALF = 0.7071067811865476


def dot(a, b):
    return jnp.dot(a, b, preferred_element_type=F32)


def dot_over(a, b, dim_a, dim_b):
    return lax.dot_general(a, b, (((dim_a,), (dim_b,)), ((), ())), preferred_element_type=F32)


def gelu(v):
    return (0.5 * v) * (1.0 + lax.erf(v * ROOT_HALF))


def layer_norm(values, gain_vec):
    centre = jnp.mean(values, axis=-1, keepdims=True)
    offsets = values - centre
    spread = jnp.mean(offsets * offsets, axis=-1, keepdims=True)
    return offsets * lax.rsqrt(spread + 1e-05) * gain_vec


def turn(tiles):
    return pltpu.roll(tiles, HALF, axis=tiles.ndim - 2)


def cell_is_low(shape):
    return lax.broadcasted_iota(jnp.int32, shape, len(shape) - 2) < HALF


def window_bias(table_ref, pad_ref, bias_ref):
    span = 2 * WIN - 1
    pitch = 2 * WIN
    width = pitch * pitch
    pad_ref[...] = jnp.zeros(pad_ref.shape, F32)
    pad_ref[:, : span * span] = table_ref[...] * LOG2E
    packed = pad_ref[...]
    line = lax.broadcasted_iota(jnp.int32, packed.shape, 1) // pitch
    flat = packed
    for a in range(1, span):
        flat = jnp.where(line == a, pltpu.roll(packed, a, axis=1), flat)
    even = lax.broadcasted_iota(jnp.int32, (WIN, LANES), 1) % pitch < WIN
    for group in range(4):
        for pair in range(2):
            head = group * 4 + pair * 2
            row_even = jnp.broadcast_to(flat[head : head + 1, :], (WIN, width))
            row_odd = jnp.broadcast_to(flat[head + 1 : head + 2, :], (WIN, width))
            for key_row in range(WIN):
                back = (WIN - 1 - key_row) * pitch + WIN - 1
                a = pltpu.roll(row_even, (width - back) % width, axis=1, stride=1, stride_axis=0)
                b = pltpu.roll(
                    row_odd, (width - back + WIN) % width, axis=1, stride=1, stride_axis=0
                )
                bias_ref[
                    group,
                    key_row * WIN : (key_row + 1) * WIN,
                    pair * LANES : (pair + 1) * LANES,
                ] = jnp.where(even, a[:, :LANES], b[:, :LANES])


def spread_heads(q):
    head = lax.broadcasted_iota(jnp.int32, (1, 1, LANES), 2) // 32
    tiles = q.astype(F32).reshape(WIN, WIN, LANES)
    pieces = []
    for pair in range(2):
        both = [jnp.where(head == pair * 2 + k, tiles, 0.0)[:, None] for k in range(2)]
        pieces.append(jnp.concatenate(both, axis=1).reshape(2 * CELLS, LANES))
    return jnp.concatenate(pieces, axis=0).astype(BF16)


def gather_heads(o):
    head = lax.broadcasted_iota(jnp.int32, (1, 1, LANES), 2) // 32
    parts = o.reshape(2, WIN, 2, WIN, LANES)
    low = jnp.where(head == 0, parts[0, :, 0], parts[0, :, 1])
    high = jnp.where(head == 2, parts[1, :, 0], parts[1, :, 1])
    return jnp.where(head < 2, low, high).reshape(CELLS, LANES)


def soften(s):
    e = jnp.exp2(s - jnp.max(s, axis=0, keepdims=True))
    return (e * (1.0 / jnp.sum(e, axis=0, keepdims=True))).astype(BF16)


AWAY = sorted(
    ((z, x) for z in range(4) for x in range(4)),
    key=lambda d: (min(d[0], 4 - d[0]) + min(d[1], 4 - d[1]), d),
)
PEERS = 32
CAP = 32
GROUPS = 4
PER_GROUP = PEERS // GROUPS
ROWS = PER_GROUP * CAP


def token_routes(routes_ref):
    grid = routes_ref[...].reshape(16, 32).astype(F32).astype(BF16)
    token = lax.broadcasted_iota(jnp.int32, (32, 512), 1)
    row = ((token // 64) % 4 * 8 + 4 + (token // 8) % 8) % 32
    at_row = jnp.where(lax.broadcasted_iota(jnp.int32, (32, 512), 0) == row, 1.0, 0.0)
    token = lax.broadcasted_iota(jnp.int32, (16, 512), 1)
    cell = token % 8
    column = jnp.where(token < 256, HALF + cell, (cell + 12) % 16)
    at_column = lax.broadcasted_iota(jnp.int32, (16, 512), 0) == column
    picked = jnp.where(at_column, dot(grid, at_row.astype(BF16)), 0.0)
    return jnp.sum(picked, axis=0, keepdims=True).astype(jnp.int32)


def kernel(
    x_ref,
    routes_ref,
    table_r_ref,
    table_s_ref,
    gain_r_ref,
    gain_m_ref,
    gain_s_ref,
    gain_e_ref,
    qkv_r_hbm,
    proj_r_hbm,
    up_hbm,
    down_hbm,
    qkv_s_hbm,
    proj_s_hbm,
    own_in,
    own_out,
    enc_ref,
    qkv_r,
    proj_r,
    up,
    down,
    qkv_s,
    proj_s,
    load_sem,
    pad,
    bias_r,
    bias_s,
    tiles,
    qkv_buf,
    edge_buf,
    heads,
    third_buf,
    to_left,
    to_right,
    from_left,
    from_right,
    send_sem,
    recv_sem,
    shard_send,
    shard_recv,
    w_in,
    w_out,
    place,
    take,
    outgoing,
    arrived,
    result,
    returned,
    totals,
    go_send,
    go_recv,
    back_send,
    back_recv,
    heads_sem,
    ready_sem,
):
    band = lax.axis_index("band")
    bands = lax.axis_size("band")
    right = lax.rem(band + 1, bands)
    left = lax.rem(band + bands - 1, bands)
    me = lax.axis_index("expert")
    my_z, my_x, my_core = me // 8, (me // 2) % 4, me % 2

    def peer(n, sign):
        z, x = AWAY[n // 2]
        return (
            (my_z + 4 + sign * z) % 4 * 4 + (my_x + 4 + sign * x) % 4
        ) * 2 + (my_core + n % 2) % 2

    barrier = pltpu.get_barrier_semaphore()

    def tell(sem, to):
        pl.semaphore_signal(sem, inc=1, device_id={"expert": to}, device_id_type=MESH)

    head = my_z * 8
    is_head = me == head
    other_heads = [(head + 8 * n) % PEERS for n in (1, 2, 3)]
    for other in (left, right):
        pl.semaphore_signal(barrier, inc=1, device_id={"band": other}, device_id_type=MESH)

    @pl.when(is_head)
    def _():
        for other in other_heads:
            tell(barrier, other)

    @pl.when(jnp.logical_not(is_head))
    def _():
        tell(barrier, head)

    loads = [
        pltpu.make_async_copy(src, dst, load_sem.at[n])
        for n, (src, dst) in enumerate(
            (
                (qkv_r_hbm, qkv_r),
                (proj_r_hbm, proj_r),
                (up_hbm, up),
                (down_hbm, down),
                (qkv_s_hbm, qkv_s),
                (proj_s_hbm, proj_s),
                (own_in.at[0], w_in.at[0]),
                (own_out.at[0], w_out.at[0]),
            )
        )
    ]
    for load in loads:
        load.start()

    def remote(src, dst, send_sem, recv_sem, to):
        return pltpu.make_async_remote_copy(
            src_ref=src,
            dst_ref=dst,
            send_sem=send_sem,
            recv_sem=recv_sem,
            device_id=to,
            device_id_type=MESH,
        )

    def shard(n):
        side = n % 2
        to = {"band": left if side else right}
        array, first, count = (
            (0, 0, 512),
            (1, 0, 128),
            (1, 128, 384),
            (0, side * 256, 256),
            (1, side * 256, 256),
        )[n // 2]
        rows = pl.ds(first, count)
        kept = (w_in, w_out)[array]
        if n < 6:
            src, dst = (own_in, own_out)[array].at[0, rows], kept.at[1 + side, rows]
        else:
            src, dst = kept.at[1 + side, rows], kept.at[3, rows]
        return remote(src, dst, shard_send.at[n], shard_recv.at[n], to)

    def go(n):
        to = {"expert": peer(n, 1)}
        return remote(outgoing.at[n], arrived.at[n], go_send.at[n], go_recv.at[n], to)

    def back(n):
        to = {"expert": peer(n, -1)}
        return remote(result.at[n], returned.at[n], back_send.at[n], back_recv.at[n], to)


    @pl.when(is_head)
    def _():
        pl.semaphore_wait(barrier, 2 + 7 + 3)
        for other in other_heads:
            tell(heads_sem, other)

    @pl.when(jnp.logical_not(is_head))
    def _():
        pl.semaphore_wait(barrier, 2)

    for n in range(2):
        shard(n).start()

    routes = token_routes(routes_ref)
    code = (((routes >> 3) - my_z) & 3) * 4 + (((routes >> 1) - my_x) & 3)
    spot = jnp.zeros_like(routes)
    for n, (z, x) in enumerate(AWAY):
        spot = jnp.where(code == z * 4 + x, n, spot)
    spot = spot * 2 + ((routes - my_core) & 1)
    chosen = lax.broadcasted_iota(jnp.int32, (PEERS, 512), 0) == spot
    onehot = jnp.where(chosen, 1.0, 0.0)
    before = lax.broadcasted_iota(jnp.int32, (512, 512), 0) < lax.broadcasted_iota(
        jnp.int32, (512, 512), 1
    )
    ahead = dot(onehot.astype(BF16), jnp.where(before, 1.0, 0.0).astype(BF16))
    slot = spot.astype(F32) * CAP + jnp.sum(onehot * ahead, axis=0, keepdims=True)
    for g in range(GROUPS):
        rows = (lax.broadcasted_iota(jnp.int32, (ROWS, 512), 0) + g * ROWS).astype(F32)
        place[g * ROWS : (g + 1) * ROWS] = jnp.where(rows == slot, 1.0, 0.0).astype(BF16)
    slot_column = jnp.transpose(jnp.broadcast_to(slot, (LANES, 512)))
    lane = lax.broadcasted_iota(jnp.int32, (512, LANES), 1).astype(F32)
    for n in range(PEERS * CAP // LANES):
        take[:, n * LANES : (n + 1) * LANES] = jnp.where(
            slot_column == lane + n * LANES, 1.0, 0.0
        ).astype(BF16)
    scale = LOG2E * 32**-0.5
    window_bias(table_r_ref, pad, bias_r)
    window_bias(table_s_ref, pad, bias_s)


    @pl.when(is_head)
    def _():
        pl.semaphore_wait(heads_sem, 3)
        for n in range(1, 8):
            tell(ready_sem, head + n)

    for load in loads[:4]:
        load.wait()

    def sends(part):
        return [
            remote(
                to_left.at[part],
                from_right.at[part],
                send_sem.at[0, part],
                recv_sem.at[0, part],
                {"band": left},
            ),
            remote(
                to_right.at[part],
                from_left.at[part],
                send_sem.at[1, part],
                recv_sem.at[1, part],
                {"band": right},
            ),
        ]

    low_cell = cell_is_low((1, WIN, 512))

    def first_part(part, carry):
        x3 = x_ref[0, pl.ds(part * 16, 16)].astype(F32)
        xf = jnp.concatenate(
            [
                x3[r * 8 : r * 8 + 8, c * 8 : c * 8 + 8, :].reshape(CELLS, 512)
                for r in range(2)
                for c in range(2)
            ],
            axis=0,
        )
        qkv_buf[...] = dot(xf.astype(BF16), qkv_r[...]).astype(BF16)
        for w in range(4):
            rows = slice(w * CELLS, (w + 1) * CELLS)
            for g in range(4):
                q = qkv_buf[rows, g * 128 : g * 128 + 128]
                k = qkv_buf[rows, 512 + g * 128 : 640 + g * 128]
                v = qkv_buf[rows, 1024 + g * 128 : 1152 + g * 128]
                s = dot_over(k, spread_heads(q), 1, 1) * scale + bias_r[g]
                heads[rows, g * 128 : g * 128 + 128] = gather_heads(
                    dot_over(soften(s), v, 0, 0)
                ).astype(BF16)
        first = (xf + layer_norm(dot(heads[...], proj_r[...]), gain_r_ref[...])).astype(BF16)
        total = jnp.zeros((256, 512), F32)
        for f in range(4):
            hidden = gelu(dot(first, up[:, f * 512 : f * 512 + 512])).astype(BF16)
            total = total + dot(hidden, down[f * 512 : f * 512 + 512, :])
        second = (first.astype(F32) + layer_norm(total, gain_m_ref[...])).astype(BF16).astype(F32)
        for r in range(2):
            rows = pl.ds(part * 16 + r * 8, 8)
            w0 = second[r * 128 : r * 128 + 64].reshape(WIN, WIN, 512)
            w1 = second[r * 128 + 64 : r * 128 + 128].reshape(WIN, WIN, 512)
            tiles[rows, 1] = w0
            tiles[rows, 2] = w1
            to_left[part, r * 32 : r * 32 + 32] = (
                jnp.where(low_cell, w0[:HALF], turn(w0[HALF:])).reshape(32, 512).astype(BF16)
            )
            to_right[part, r * 32 : r * 32 + 32] = (
                jnp.where(low_cell, turn(w1[HALF:]), w1[:HALF]).reshape(32, 512).astype(BF16)
            )
        for send in sends(part):
            send.start()

        @pl.when(part == 0)
        def _():
            for n in (2, 3):
                shard(n).start()

        return carry

    lax.fori_loop(0, 2, first_part, 0)
    for n in (4, 5):
        shard(n).start()
    for n in (0, 1):
        shard(n).wait_recv()
    for n in (6, 7):
        shard(n).start()

    def shifted(column):
        pieces = []
        for w in range(4):
            for start in (w * 8 + 4, (w * 8 + 8) % 32):
                a = tiles[start : start + 4, column]
                b = tiles[start : start + 4, column + 1]
                pieces.append(turn(jnp.where(low_cell, b, a)))
        return jnp.concatenate(pieces, axis=0)

    def finish(x, first_row):
        third = x + layer_norm(dot(heads[...], proj_s[...]), gain_s_ref[...])
        third_buf[first_row : first_row + 256, :] = third.astype(BF16)

    key = lax.broadcasted_iota(jnp.int32, (CELLS, 256), 0)
    lane = lax.broadcasted_iota(jnp.int32, (CELLS, 256), 1)
    low_j = lane % 8 < HALF
    row_apart = (key // 8 < HALF) != ((lane // 16) % 8 < HALF)
    col_apart = ((key % 8 < HALF) != low_j) & (
        (low_j & (band == bands - 1)) | (jnp.logical_not(low_j) & (band == 0))
    )
    mask_row = jnp.where(row_apart, -100.0 * LOG2E, 0.0)
    mask_col = jnp.where(col_apart, -100.0 * LOG2E, 0.0)
    mask_both = jnp.where(row_apart | col_apart, -100.0 * LOG2E, 0.0)

    for load in loads[4:6]:
        load.wait()
    mid = shifted(1).reshape(256, 512)
    qkv_buf[...] = dot(mid.astype(BF16), qkv_s[...]).astype(BF16)
    for w in range(4):
        rows = slice(w * CELLS, (w + 1) * CELLS)
        for g in range(4):
            q = qkv_buf[rows, g * 128 : g * 128 + 128]
            k = qkv_buf[rows, 512 + g * 128 : 640 + g * 128]
            v = qkv_buf[rows, 1024 + g * 128 : 1152 + g * 128]
            s = dot_over(k, spread_heads(q), 1, 1) * scale + bias_s[g]
            if w == 3:
                s = s + mask_row
            heads[rows, g * 128 : g * 128 + 128] = gather_heads(
                dot_over(soften(s), v, 0, 0)
            ).astype(BF16)
    finish(mid, 0)

    for part in range(2):
        for send in sends(part):
            send.wait()
        for r in range(2):
            top = part * 16 + r * 8
            h = from_left[part, r * 32 : r * 32 + 32].astype(F32).reshape(HALF, WIN, 512)
            tiles[top : top + 4, 0] = h
            tiles[top + 4 : top + 8, 0] = turn(h)
            h = from_right[part, r * 32 : r * 32 + 32].astype(F32).reshape(HALF, WIN, 512)
            tiles[top : top + 4, 3] = h
            tiles[top + 4 : top + 8, 3] = turn(h)
    edge0 = shifted(0)
    edge2 = shifted(2)
    edge = jnp.where(low_cell, edge2, edge0).reshape(256, 512)
    qkv_buf[:, :512] = dot(edge.astype(BF16), qkv_s[:, :512]).astype(BF16)
    qkv_buf[:, 512:] = dot(edge0.reshape(256, 512).astype(BF16), qkv_s[:, 512:]).astype(BF16)
    edge_buf[...] = dot(edge2.reshape(256, 512).astype(BF16), qkv_s[:, 512:]).astype(BF16)
    for w in range(4):
        rows = slice(w * CELLS, (w + 1) * CELLS)
        for g in range(4):
            q = spread_heads(qkv_buf[rows, g * 128 : g * 128 + 128])
            k0 = qkv_buf[rows, 512 + g * 128 : 640 + g * 128]
            v0 = qkv_buf[rows, 1024 + g * 128 : 1152 + g * 128]
            k2 = edge_buf[rows, g * 128 : g * 128 + 128]
            v2 = edge_buf[rows, 512 + g * 128 : 640 + g * 128]
            s = jnp.where(low_j, dot_over(k2, q, 1, 1), dot_over(k0, q, 1, 1))
            s = s * scale + bias_s[g] + (mask_both if w == 3 else mask_col)
            p = soften(s).astype(F32)
            p = jnp.concatenate([jnp.where(low_j, p, 0.0), jnp.where(low_j, 0.0, p)], axis=0)
            v = jnp.concatenate([v2, v0], axis=0)
            heads[rows, g * 128 : g * 128 + 128] = gather_heads(
                dot_over(p.astype(BF16), v, 0, 0)
            ).astype(BF16)
    finish(edge, 256)

    @pl.when(jnp.logical_not(is_head))
    def _():
        pl.semaphore_wait(ready_sem, 1)

    groups = range(GROUPS)[::-1]

    def places(g):
        return range(max(g * PER_GROUP, 1), (g + 1) * PER_GROUP)[::-1]

    third = third_buf[...]
    for g in groups:
        block = dot(place[g * ROWS : (g + 1) * ROWS], third).astype(BF16)
        block = block.reshape(PER_GROUP, CAP, 512)
        if g == 0:
            arrived[0] = block[0]
            outgoing[1:PER_GROUP] = block[1:]
        else:
            outgoing[g * PER_GROUP : (g + 1) * PER_GROUP] = block
        for n in places(g):
            go(n).start()

    for n in (2, 3, 4, 5):
        shard(n).wait_recv()
    for n in (8, 9):
        shard(n).start()
    for load in loads[6:]:
        load.wait()

    def layer(rows, n):
        hidden = gelu(dot(rows, w_in[n])).astype(BF16)
        return dot(hidden, w_out[n])

    def near_shards(g):
        for n in places(g):
            go(n).wait_recv()
        rows = arrived[g * PER_GROUP : (g + 1) * PER_GROUP].reshape(ROWS, 512)
        return layer(rows, 0) + layer(rows, 1) + layer(rows, 2)

    def far_shard(g, total):
        rows = arrived[g * PER_GROUP : (g + 1) * PER_GROUP].reshape(ROWS, 512)
        block = (total + layer(rows, 3)).astype(BF16).reshape(PER_GROUP, CAP, 512)
        if g == 0:
            returned[0] = block[0]
            result[1:PER_GROUP] = block[1:]
        else:
            result[g * PER_GROUP : (g + 1) * PER_GROUP] = block
        for n in places(g):
            back(n).start()

    for g in groups[:-1]:
        totals[g * ROWS : (g + 1) * ROWS] = near_shards(g)
    for n in (6, 7, 8, 9):
        shard(n).wait_recv()
    for g in groups[:-1]:
        far_shard(g, totals[g * ROWS : (g + 1) * ROWS])
    far_shard(0, near_shards(0))
    for n in range(10):
        shard(n).wait_send()
    rows = jnp.zeros((512, 512), F32)
    for g in groups:
        for n in places(g):
            back(n).wait_recv()
        block = returned[g * PER_GROUP : (g + 1) * PER_GROUP].reshape(ROWS, 512)
        rows = rows + dot(take[:, g * ROWS : (g + 1) * ROWS], block)
    encoded = third_buf[...].astype(F32) + layer_norm(rows, gain_e_ref[...])
    for w in range(4):
        mid = encoded[w * CELLS : (w + 1) * CELLS].reshape(WIN, WIN, 512)
        edge = encoded[256 + w * CELLS : 256 + (w + 1) * CELLS].reshape(WIN, WIN, 512)
        w0 = turn(jnp.where(low_cell, mid, edge))
        w1 = turn(jnp.where(low_cell, edge, mid))
        block = jnp.concatenate([w0, w1], axis=1).astype(BF16)
        for half in range(2):
            top = (w * 8 + 4 + half * 4) % 32
            enc_ref[0, top : top + 4] = block[half * 4 : half * 4 + 4]
    for g in groups:
        for n in places(g):
            go(n).wait_send()
            back(n).wait_send()


def block_pair(features, routes, tables, gains, weights, shards):
    vmem = pl.BlockSpec(memory_space=pltpu.VMEM)
    hbm = pl.BlockSpec(memory_space=pl.ANY)
    dma = pltpu.SemaphoreType.DMA
    return pl.pallas_call(
        kernel,
        out_shape=jax.ShapeDtypeStruct((1, 32, 16, 512), BF16),
        in_specs=[vmem] * 8 + [hbm] * 8,
        out_specs=vmem,
        scratch_shapes=[pltpu.VMEM(w.shape, BF16) for w in weights]
        + [
            dma((8,)),
            pltpu.VMEM((16, 256), F32),
            pltpu.VMEM((4, CELLS, 256), F32),
            pltpu.VMEM((4, CELLS, 256), F32),
            pltpu.VMEM((32, 4, WIN, 512), F32),
            pltpu.VMEM((256, 1536), BF16),
            pltpu.VMEM((256, 1024), BF16),
            pltpu.VMEM((256, 512), BF16),
            pltpu.VMEM((512, 512), BF16),
        ]
        + [pltpu.VMEM((2, 64, 512), BF16)] * 4
        + [dma((2, 2)), dma((2, 2)), dma((10,)), dma((10,))]
        + [
            pltpu.VMEM((4, 512, 512), BF16),
            pltpu.VMEM((4, 512, 512), BF16),
            pltpu.VMEM((PEERS * CAP, 512), BF16),
            pltpu.VMEM((512, PEERS * CAP), BF16),
        ]
        + [pltpu.VMEM((PEERS, CAP, 512), BF16)] * 4
        + [pltpu.VMEM((PEERS * CAP, 512), F32)]
        + [dma((PEERS,))] * 4
        + [pltpu.SemaphoreType.REGULAR] * 2,
        compiler_params=pltpu.CompilerParams(
            collective_id=0, has_side_effects=True, vmem_limit_bytes=62 * 1024 * 1024
        ),
        name="block_pair",
    )(features, routes, *tables, *gains, *weights, *shards)


def local(
    features,
    routes,
    qkv_regular,
    proj_regular,
    table_regular,
    gain_regular,
    mlp_up,
    mlp_down,
    gain_mlp,
    qkv_shifted,
    proj_shifted,
    table_shifted,
    gain_shifted,
    expert_in,
    expert_out,
    gain_expert,
):
    gains = (gain_regular, gain_mlp, gain_shifted, gain_expert)
    return block_pair(
        features,
        routes.reshape(32, 16).T.reshape(16, 1, 32),
        (table_regular.T, table_shifted.T),
        [g.reshape(1, 512) for g in gains],
        (qkv_regular, proj_regular, mlp_up, mlp_down, qkv_shifted, proj_shifted),
        (expert_in, expert_out),
    )


def solution(mesh):
    return jax.shard_map(
        local,
        mesh=mesh,
        in_specs=(
            P("expert", None, "band", None),
            P("expert", "band", None, None, None),
        )
        + (P(),) * 11
        + (P("expert", None, "band"), P("expert", "band", None), P()),
        out_specs=P("expert", None, "band", None),
        check_vma=False,
    )
```

```python
import functools
import jax
import jax.numpy as jnp
from jax import lax
from jax.experimental import pallas as pl
from jax.experimental.pallas import tpu as pltpu
from jax.sharding import PartitionSpec as P

MESH = pl.DeviceIdType.MESH
F32 = jnp.float32
BF16 = jnp.bfloat16
WIN = 8
HALF = WIN // 2
CELLS = WIN * WIN
LANES = 128
LOG2E = 1.4426950408889634
ROOT_HALF = 0.7071067811865476


def dot(a, b):
    return jnp.dot(a, b, preferred_element_type=F32)


def dot_over(a, b, dim_a, dim_b):
    return lax.dot_general(a, b, (((dim_a,), (dim_b,)), ((), ())), preferred_element_type=F32)


def gelu(v):
    return (0.5 * v) * (1.0 + lax.erf(v * ROOT_HALF))


def layer_norm(values, gain_vec):
    centre = jnp.mean(values, axis=-1, keepdims=True)
    offsets = values - centre
    spread = jnp.mean(offsets * offsets, axis=-1, keepdims=True)
    return offsets * lax.rsqrt(spread + 1e-05) * gain_vec


def turn(tiles):
    return pltpu.roll(tiles, HALF, axis=tiles.ndim - 2)


def cell_is_low(shape):
    return lax.broadcasted_iota(jnp.int32, shape, len(shape) - 2) < HALF


def window_bias(table_ref, pad_ref, bias_ref):
    span = 2 * WIN - 1
    pitch = 2 * WIN
    width = pitch * pitch
    pad_ref[...] = jnp.zeros(pad_ref.shape, F32)
    pad_ref[:, : span * span] = table_ref[...] * LOG2E
    packed = pad_ref[...]
    line = lax.broadcasted_iota(jnp.int32, packed.shape, 1) // pitch
    flat = packed
    for a in range(1, span):
        flat = jnp.where(line == a, pltpu.roll(packed, a, axis=1), flat)
    even = lax.broadcasted_iota(jnp.int32, (WIN, LANES), 1) % pitch < WIN
    for group in range(4):
        for pair in range(2):
            head = group * 4 + pair * 2
            row_even = jnp.broadcast_to(flat[head : head + 1, :], (WIN, width))
            row_odd = jnp.broadcast_to(flat[head + 1 : head + 2, :], (WIN, width))
            for key_row in range(WIN):
                back = (WIN - 1 - key_row) * pitch + WIN - 1
                a = pltpu.roll(row_even, (width - back) % width, axis=1, stride=1, stride_axis=0)
                b = pltpu.roll(
                    row_odd, (width - back + WIN) % width, axis=1, stride=1, stride_axis=0
                )
                bias_ref[
                    group,
                    key_row * WIN : (key_row + 1) * WIN,
                    pair * LANES : (pair + 1) * LANES,
                ] = jnp.where(even, a[:, :LANES], b[:, :LANES])


def spread_heads(q):
    head = lax.broadcasted_iota(jnp.int32, (1, 1, LANES), 2) // 32
    tiles = q.astype(F32).reshape(WIN, WIN, LANES)
    pieces = []
    for pair in range(2):
        both = [jnp.where(head == pair * 2 + k, tiles, 0.0)[:, None] for k in range(2)]
        pieces.append(jnp.concatenate(both, axis=1).reshape(2 * CELLS, LANES))
    return jnp.concatenate(pieces, axis=0).astype(BF16)


def gather_heads(o):
    head = lax.broadcasted_iota(jnp.int32, (1, 1, LANES), 2) // 32
    parts = o.reshape(2, WIN, 2, WIN, LANES)
    low = jnp.where(head == 0, parts[0, :, 0], parts[0, :, 1])
    high = jnp.where(head == 2, parts[1, :, 0], parts[1, :, 1])
    return jnp.where(head < 2, low, high).reshape(CELLS, LANES)


def soften(s):
    e = jnp.exp2(s - jnp.max(s, axis=0, keepdims=True))
    return (e * (1.0 / jnp.sum(e, axis=0, keepdims=True))).astype(BF16)


AWAY = sorted(
    ((z, x) for z in range(4) for x in range(4)),
    key=lambda d: (min(d[0], 4 - d[0]) + min(d[1], 4 - d[1]), d),
)
PEERS = 32
CAP = 32
GROUPS = 4
PER_GROUP = PEERS // GROUPS
ROWS = PER_GROUP * CAP


def token_routes(routes_ref):
    grid = routes_ref[...].reshape(16, 32).astype(F32).astype(BF16)
    token = lax.broadcasted_iota(jnp.int32, (32, 512), 1)
    row = ((token // 64) % 4 * 8 + 4 + (token // 8) % 8) % 32
    at_row = jnp.where(lax.broadcasted_iota(jnp.int32, (32, 512), 0) == row, 1.0, 0.0)
    token = lax.broadcasted_iota(jnp.int32, (16, 512), 1)
    cell = token % 8
    column = jnp.where(token < 256, HALF + cell, (cell + 12) % 16)
    at_column = lax.broadcasted_iota(jnp.int32, (16, 512), 0) == column
    picked = jnp.where(at_column, dot(grid, at_row.astype(BF16)), 0.0)
    return jnp.sum(picked, axis=0, keepdims=True).astype(jnp.int32)


def kernel(
    x_ref,
    routes_ref,
    table_r_ref,
    table_s_ref,
    gain_r_ref,
    gain_m_ref,
    gain_s_ref,
    gain_e_ref,
    qkv_r_hbm,
    proj_r_hbm,
    up_hbm,
    down_hbm,
    qkv_s_hbm,
    proj_s_hbm,
    own_in,
    own_out,
    enc_ref,
    qkv_r,
    proj_r,
    up,
    down,
    qkv_s,
    proj_s,
    load_sem,
    pad,
    bias_r,
    bias_s,
    tiles,
    qkv_buf,
    edge_buf,
    heads,
    third_buf,
    to_left,
    to_right,
    from_left,
    from_right,
    send_sem,
    recv_sem,
    shard_send,
    shard_recv,
    w_in,
    w_out,
    place,
    take,
    outgoing,
    arrived,
    result,
    returned,
    go_send,
    go_recv,
    back_send,
    back_recv,
    heads_sem,
    ready_sem,
):
    band = lax.axis_index("band")
    bands = lax.axis_size("band")
    right = lax.rem(band + 1, bands)
    left = lax.rem(band + bands - 1, bands)
    me = lax.axis_index("expert")
    my_z, my_x, my_core = me // 8, (me // 2) % 4, me % 2
    hosted = band // 2
    mirror = bands - 1 - band
    beside = hosted * 4 + 1 - band
    served = jnp.where(my_core == 0, band, mirror)
    keeper = my_core == hosted
    sibling = me + 1 - 2 * my_core

    def chip(n, sign):
        z, x = AWAY[n // 2]
        return ((my_z + 4 + sign * z) % 4 * 4 + (my_x + 4 + sign * x) % 4) * 2

    barrier = pltpu.get_barrier_semaphore()

    def tell(sem, expert, level):
        to = {"band": level, "expert": expert}
        pl.semaphore_signal(sem, inc=1, device_id=to, device_id_type=MESH)

    head = my_z * 8
    is_head = me == head
    other_heads = [
        ((head + 8 * n) % PEERS, level) for level in (band, mirror) for n in range(4)
    ][1:]
    tell(barrier, me, left)
    tell(barrier, me, right)
    tell(barrier, sibling, band)

    @pl.when(is_head)
    def _():
        for other in other_heads:
            tell(barrier, *other)

    @pl.when(jnp.logical_not(is_head))
    def _():
        tell(barrier, head, band)

    loads = [
        pltpu.make_async_copy(src, dst, load_sem.at[n])
        for n, (src, dst) in enumerate(
            (
                (qkv_r_hbm, qkv_r),
                (proj_r_hbm, proj_r),
                (up_hbm, up),
                (down_hbm, down),
                (qkv_s_hbm, qkv_s),
                (proj_s_hbm, proj_s),
                (own_in.at[0], w_in.at[0]),
                (own_out.at[0], w_out.at[0]),
            )
        )
    ]
    for load in loads[:6]:
        load.start()

    def remote(src, dst, send_sem, recv_sem, to):
        return pltpu.make_async_remote_copy(
            src_ref=src,
            dst_ref=dst,
            send_sem=send_sem,
            recv_sem=recv_sem,
            device_id=to,
            device_id_type=MESH,
        )

    shelves = (w_in, w_out)
    own = (own_in.at[0], own_out.at[0])

    def shard(src, slot, array, n, expert, level):
        return remote(
            src,
            shelves[array].at[slot],
            shard_send.at[n],
            shard_recv.at[slot * 2 + array],
            {"band": level, "expert": expert},
        )

    def leave(array):
        slot = jnp.where(keeper, 2, 1)
        return shard(own[array], slot, array, array, me, jnp.where(keeper, beside, mirror))

    def forward(array):
        return shard(shelves[array].at[1], 3, array, 2 + array, me, beside)

    def share(slot, array):
        src = own[array] if slot == 0 else shelves[array].at[slot]
        return shard(src, slot, array, 4 + slot * 2 + array, sibling, band)

    def came(slot, array):
        share(slot, array).wait_recv()

    def go(n):
        to = {"band": mirror if n % 2 else band, "expert": chip(n, 1) + n % 2}
        slot = n // 2 * 2 + my_core
        return remote(outgoing.at[n], arrived.at[slot], go_send.at[n], go_recv.at[slot], to)

    def back(n):
        to = {"band": served, "expert": chip(n, -1) + n % 2}
        slot = n // 2 * 2 + my_core
        return remote(result.at[n], returned.at[slot], back_send.at[n], back_recv.at[slot], to)

    def landed(buffer, sem, n):
        to = {"band": band, "expert": sibling}
        remote(buffer.at[n], buffer.at[n], shard_send.at[0], sem.at[n], to).wait_recv()

    def each(places, act):
        for n in places:
            if n:
                act(n)
            else:
                pl.when(my_core == 1)(functools.partial(act, n))

    @pl.when(is_head)
    def _():
        pl.semaphore_wait(barrier, 3 + 7 + 7)
        for other in other_heads:
            tell(heads_sem, *other)

    @pl.when(jnp.logical_not(is_head))
    def _():
        pl.semaphore_wait(barrier, 3)

    for array in range(2):
        leave(array).start()

    @pl.when(keeper)
    def _():
        for array in range(2):
            share(0, array).start()
        for load in loads[6:]:
            load.start()

    routes = token_routes(routes_ref)
    code = (((routes >> 3) - my_z) & 3) * 4 + (((routes >> 1) - my_x) & 3)
    spot = jnp.zeros_like(routes)
    for n, (z, x) in enumerate(AWAY):
        spot = jnp.where(code == z * 4 + x, n, spot)
    spot = spot * 2 + ((routes - hosted) & 1)
    chosen = lax.broadcasted_iota(jnp.int32, (PEERS, 512), 0) == spot
    onehot = jnp.where(chosen, 1.0, 0.0)
    before = lax.broadcasted_iota(jnp.int32, (512, 512), 0) < lax.broadcasted_iota(
        jnp.int32, (512, 512), 1
    )
    ahead = dot(onehot.astype(BF16), jnp.where(before, 1.0, 0.0).astype(BF16))
    slot = spot.astype(F32) * CAP + jnp.sum(onehot * ahead, axis=0, keepdims=True)
    for g in range(GROUPS):
        rows = (lax.broadcasted_iota(jnp.int32, (ROWS, 512), 0) + g * ROWS).astype(F32)
        place[g * ROWS : (g + 1) * ROWS] = jnp.where(rows == slot, 1.0, 0.0).astype(BF16)
    slot_column = jnp.transpose(jnp.broadcast_to(slot, (LANES, 512)))
    lane = lax.broadcasted_iota(jnp.int32, (512, LANES), 1).astype(F32)
    for n in range(PEERS * CAP // LANES):
        take[:, n * LANES : (n + 1) * LANES] = jnp.where(
            slot_column == lane + n * LANES, 1.0, 0.0
        ).astype(BF16)
    scale = LOG2E * 32**-0.5
    window_bias(table_r_ref, pad, bias_r)
    window_bias(table_s_ref, pad, bias_s)


    @pl.when(is_head)
    def _():
        pl.semaphore_wait(heads_sem, 7)
        for n in range(1, 8):
            tell(ready_sem, head + n, band)

    for load in loads[:4]:
        load.wait()

    def sends(part):
        return [
            remote(
                to_left.at[part],
                from_right.at[part],
                send_sem.at[0, part],
                recv_sem.at[0, part],
                {"band": left},
            ),
            remote(
                to_right.at[part],
                from_left.at[part],
                send_sem.at[1, part],
                recv_sem.at[1, part],
                {"band": right},
            ),
        ]

    low_cell = cell_is_low((1, WIN, 512))

    def first_part(part, carry):
        x3 = x_ref[0, pl.ds(part * 16, 16)].astype(F32)
        xf = jnp.concatenate(
            [
                x3[r * 8 : r * 8 + 8, c * 8 : c * 8 + 8, :].reshape(CELLS, 512)
                for r in range(2)
                for c in range(2)
            ],
            axis=0,
        )
        qkv_buf[...] = dot(xf.astype(BF16), qkv_r[...]).astype(BF16)
        for w in range(4):
            rows = slice(w * CELLS, (w + 1) * CELLS)
            for g in range(4):
                q = qkv_buf[rows, g * 128 : g * 128 + 128]
                k = qkv_buf[rows, 512 + g * 128 : 640 + g * 128]
                v = qkv_buf[rows, 1024 + g * 128 : 1152 + g * 128]
                s = dot_over(k, spread_heads(q), 1, 1) * scale + bias_r[g]
                heads[rows, g * 128 : g * 128 + 128] = gather_heads(
                    dot_over(soften(s), v, 0, 0)
                ).astype(BF16)
        first = (xf + layer_norm(dot(heads[...], proj_r[...]), gain_r_ref[...])).astype(BF16)
        total = jnp.zeros((256, 512), F32)
        for f in range(4):
            hidden = gelu(dot(first, up[:, f * 512 : f * 512 + 512])).astype(BF16)
            total = total + dot(hidden, down[f * 512 : f * 512 + 512, :])
        second = (first.astype(F32) + layer_norm(total, gain_m_ref[...])).astype(BF16).astype(F32)
        for r in range(2):
            rows = pl.ds(part * 16 + r * 8, 8)
            w0 = second[r * 128 : r * 128 + 64].reshape(WIN, WIN, 512)
            w1 = second[r * 128 + 64 : r * 128 + 128].reshape(WIN, WIN, 512)
            tiles[rows, 1] = w0
            tiles[rows, 2] = w1
            to_left[part, r * 32 : r * 32 + 32] = (
                jnp.where(low_cell, w0[:HALF], turn(w0[HALF:])).reshape(32, 512).astype(BF16)
            )
            to_right[part, r * 32 : r * 32 + 32] = (
                jnp.where(low_cell, turn(w1[HALF:]), w1[:HALF]).reshape(32, 512).astype(BF16)
            )
        for send in sends(part):
            send.start()

        @pl.when((part == 0) & keeper)
        def _():
            came(1, 0)
            forward(0).start()
            share(1, 0).start()

        return carry

    lax.fori_loop(0, 2, first_part, 0)

    @pl.when(keeper)
    def _():
        came(1, 1)
        forward(1).start()
        share(1, 1).start()
        for array in range(2):
            came(2, array)
            share(2, array).start()

    def shifted(column):
        pieces = []
        for w in range(4):
            for start in (w * 8 + 4, (w * 8 + 8) % 32):
                a = tiles[start : start + 4, column]
                b = tiles[start : start + 4, column + 1]
                pieces.append(turn(jnp.where(low_cell, b, a)))
        return jnp.concatenate(pieces, axis=0)

    def finish(x, first_row):
        third = x + layer_norm(dot(heads[...], proj_s[...]), gain_s_ref[...])
        third_buf[first_row : first_row + 256, :] = third.astype(BF16)

    key = lax.broadcasted_iota(jnp.int32, (CELLS, 256), 0)
    lane = lax.broadcasted_iota(jnp.int32, (CELLS, 256), 1)
    low_j = lane % 8 < HALF
    row_apart = (key // 8 < HALF) != ((lane // 16) % 8 < HALF)
    col_apart = ((key % 8 < HALF) != low_j) & (
        (low_j & (band == bands - 1)) | (jnp.logical_not(low_j) & (band == 0))
    )
    mask_row = jnp.where(row_apart, -100.0 * LOG2E, 0.0)
    mask_col = jnp.where(col_apart, -100.0 * LOG2E, 0.0)
    mask_both = jnp.where(row_apart | col_apart, -100.0 * LOG2E, 0.0)

    for load in loads[4:6]:
        load.wait()
    mid = shifted(1).reshape(256, 512)
    qkv_buf[...] = dot(mid.astype(BF16), qkv_s[...]).astype(BF16)
    for w in range(4):
        rows = slice(w * CELLS, (w + 1) * CELLS)
        for g in range(4):
            q = qkv_buf[rows, g * 128 : g * 128 + 128]
            k = qkv_buf[rows, 512 + g * 128 : 640 + g * 128]
            v = qkv_buf[rows, 1024 + g * 128 : 1152 + g * 128]
            s = dot_over(k, spread_heads(q), 1, 1) * scale + bias_s[g]
            if w == 3:
                s = s + mask_row
            heads[rows, g * 128 : g * 128 + 128] = gather_heads(
                dot_over(soften(s), v, 0, 0)
            ).astype(BF16)
    finish(mid, 0)

    for part in range(2):
        for send in sends(part):
            send.wait()
        for r in range(2):
            top = part * 16 + r * 8
            h = from_left[part, r * 32 : r * 32 + 32].astype(F32).reshape(HALF, WIN, 512)
            tiles[top : top + 4, 0] = h
            tiles[top + 4 : top + 8, 0] = turn(h)
            h = from_right[part, r * 32 : r * 32 + 32].astype(F32).reshape(HALF, WIN, 512)
            tiles[top : top + 4, 3] = h
            tiles[top + 4 : top + 8, 3] = turn(h)
    edge0 = shifted(0)
    edge2 = shifted(2)
    edge = jnp.where(low_cell, edge2, edge0).reshape(256, 512)
    qkv_buf[:, :512] = dot(edge.astype(BF16), qkv_s[:, :512]).astype(BF16)
    qkv_buf[:, 512:] = dot(edge0.reshape(256, 512).astype(BF16), qkv_s[:, 512:]).astype(BF16)
    edge_buf[...] = dot(edge2.reshape(256, 512).astype(BF16), qkv_s[:, 512:]).astype(BF16)
    for w in range(4):
        rows = slice(w * CELLS, (w + 1) * CELLS)
        for g in range(4):
            q = spread_heads(qkv_buf[rows, g * 128 : g * 128 + 128])
            k0 = qkv_buf[rows, 512 + g * 128 : 640 + g * 128]
            v0 = qkv_buf[rows, 1024 + g * 128 : 1152 + g * 128]
            k2 = edge_buf[rows, g * 128 : g * 128 + 128]
            v2 = edge_buf[rows, 512 + g * 128 : 640 + g * 128]
            s = jnp.where(low_j, dot_over(k2, q, 1, 1), dot_over(k0, q, 1, 1))
            s = s * scale + bias_s[g] + (mask_both if w == 3 else mask_col)
            p = soften(s).astype(F32)
            p = jnp.concatenate([jnp.where(low_j, p, 0.0), jnp.where(low_j, 0.0, p)], axis=0)
            v = jnp.concatenate([v2, v0], axis=0)
            heads[rows, g * 128 : g * 128 + 128] = gather_heads(
                dot_over(p.astype(BF16), v, 0, 0)
            ).astype(BF16)
    finish(edge, 256)

    @pl.when(jnp.logical_not(is_head))
    def _():
        pl.semaphore_wait(ready_sem, 1)

    groups = range(GROUPS)[::-1]

    def places(g):
        return range(g * PER_GROUP, (g + 1) * PER_GROUP)[::-1]

    def keep(block, buffer):
        @pl.when(my_core == 0)
        def _():
            buffer[0] = block

    third = third_buf[...]
    for g in groups:
        block = dot(place[g * ROWS : (g + 1) * ROWS], third).astype(BF16)
        block = block.reshape(PER_GROUP, CAP, 512)
        outgoing[g * PER_GROUP : (g + 1) * PER_GROUP] = block
        if g == 0:
            keep(block[0], arrived)
        each(places(g), lambda n: go(n).start())

    @pl.when(keeper)
    def _():
        came(3, 0)
        share(3, 0).start()
        for load in loads[6:]:
            load.wait()

    @pl.when(jnp.logical_not(keeper))
    def _():
        for slot in range(3):
            for array in range(2):
                came(slot, array)
        came(3, 0)

    def layer(rows, n):
        hidden = gelu(dot(rows, w_in[n])).astype(BF16)
        return dot(hidden, w_out[n])

    for g in groups:
        each(places(g), lambda n: landed(arrived, go_recv, n))
        rows = arrived[g * PER_GROUP : (g + 1) * PER_GROUP].reshape(ROWS, 512)
        total = layer(rows, 0) + layer(rows, 1) + layer(rows, 2)
        if g == GROUPS - 1:
            came(3, 1)

            @pl.when(keeper)
            def _():
                share(3, 1).start()

        block = (total + layer(rows, 3)).astype(BF16).reshape(PER_GROUP, CAP, 512)
        result[g * PER_GROUP : (g + 1) * PER_GROUP] = block
        if g == 0:
            keep(block[0], returned)
        each(places(g), lambda n: back(n).start())

    for array in range(2):
        leave(array).wait_send()

    @pl.when(keeper)
    def _():
        for array in range(2):
            forward(array).wait_send()
            for slot in range(4):
                share(slot, array).wait_send()

    rows = jnp.zeros((512, 512), F32)
    for g in groups:
        each(places(g), lambda n: landed(returned, back_recv, n))
        block = returned[g * PER_GROUP : (g + 1) * PER_GROUP].reshape(ROWS, 512)
        rows = rows + dot(take[:, g * ROWS : (g + 1) * ROWS], block)
    encoded = third_buf[...].astype(F32) + layer_norm(rows, gain_e_ref[...])
    for w in range(4):
        mid = encoded[w * CELLS : (w + 1) * CELLS].reshape(WIN, WIN, 512)
        edge = encoded[256 + w * CELLS : 256 + (w + 1) * CELLS].reshape(WIN, WIN, 512)
        w0 = turn(jnp.where(low_cell, mid, edge))
        w1 = turn(jnp.where(low_cell, edge, mid))
        block = jnp.concatenate([w0, w1], axis=1).astype(BF16)
        for half in range(2):
            top = (w * 8 + 4 + half * 4) % 32
            enc_ref[0, top : top + 4] = block[half * 4 : half * 4 + 4]
    for g in groups:
        each(places(g), lambda n: go(n).wait_send())
        each(places(g), lambda n: back(n).wait_send())


def block_pair(features, routes, tables, gains, weights, shards):
    vmem = pl.BlockSpec(memory_space=pltpu.VMEM)
    hbm = pl.BlockSpec(memory_space=pl.ANY)
    dma = pltpu.SemaphoreType.DMA
    return pl.pallas_call(
        kernel,
        out_shape=jax.ShapeDtypeStruct((1, 32, 16, 512), BF16),
        in_specs=[vmem] * 8 + [hbm] * 8,
        out_specs=vmem,
        scratch_shapes=[pltpu.VMEM(w.shape, BF16) for w in weights]
        + [
            dma((8,)),
            pltpu.VMEM((16, 256), F32),
            pltpu.VMEM((4, CELLS, 256), F32),
            pltpu.VMEM((4, CELLS, 256), F32),
            pltpu.VMEM((32, 4, WIN, 512), F32),
            pltpu.VMEM((256, 1536), BF16),
            pltpu.VMEM((256, 1024), BF16),
            pltpu.VMEM((256, 512), BF16),
            pltpu.VMEM((512, 512), BF16),
        ]
        + [pltpu.VMEM((2, 64, 512), BF16)] * 4
        + [dma((2, 2)), dma((2, 2)), dma((12,)), dma((8,))]
        + [
            pltpu.VMEM((4, 512, 512), BF16),
            pltpu.VMEM((4, 512, 512), BF16),
            pltpu.VMEM((PEERS * CAP, 512), BF16),
            pltpu.VMEM((512, PEERS * CAP), BF16),
        ]
        + [pltpu.VMEM((PEERS, CAP, 512), BF16)] * 4
        + [dma((PEERS,))] * 4
        + [pltpu.SemaphoreType.REGULAR] * 2,
        compiler_params=pltpu.CompilerParams(
            collective_id=0, has_side_effects=True, vmem_limit_bytes=62 * 1024 * 1024
        ),
        name="block_pair",
    )(features, routes, *tables, *gains, *weights, *shards)


def local(
    features,
    routes,
    qkv_regular,
    proj_regular,
    table_regular,
    gain_regular,
    mlp_up,
    mlp_down,
    gain_mlp,
    qkv_shifted,
    proj_shifted,
    table_shifted,
    gain_shifted,
    expert_in,
    expert_out,
    gain_expert,
):
    gains = (gain_regular, gain_mlp, gain_shifted, gain_expert)
    return block_pair(
        features,
        routes.reshape(32, 16).T.reshape(16, 1, 32),
        (table_regular.T, table_shifted.T),
        [g.reshape(1, 512) for g in gains],
        (qkv_regular, proj_regular, mlp_up, mlp_down, qkv_shifted, proj_shifted),
        (expert_in, expert_out),
    )


def solution(mesh):
    return jax.shard_map(
        local,
        mesh=mesh,
        in_specs=(
            P("expert", None, "band", None),
            P("expert", "band", None, None, None),
        )
        + (P(),) * 11
        + (P("expert", None, "band"), P("expert", "band", None), P()),
        out_specs=P("expert", None, "band", None),
        check_vma=False,
    )
```

```python
import functools
import jax
import jax.numpy as jnp
from jax import lax
from jax.experimental import pallas as pl
from jax.experimental.pallas import tpu as pltpu
from jax.sharding import PartitionSpec as P

MESH = pl.DeviceIdType.MESH
F32 = jnp.float32
BF16 = jnp.bfloat16
WIN = 8
HALF = WIN // 2
CELLS = WIN * WIN
LANES = 128
LOG2E = 1.4426950408889634
ROOT_HALF = 0.7071067811865476


def dot(a, b):
    return jnp.dot(a, b, preferred_element_type=F32)


def dot_over(a, b, dim_a, dim_b):
    return lax.dot_general(a, b, (((dim_a,), (dim_b,)), ((), ())), preferred_element_type=F32)


def gelu(v):
    return (0.5 * v) * (1.0 + lax.erf(v * ROOT_HALF))


def layer_norm(values, gain_vec):
    centre = jnp.mean(values, axis=-1, keepdims=True)
    offsets = values - centre
    spread = jnp.mean(offsets * offsets, axis=-1, keepdims=True)
    return offsets * lax.rsqrt(spread + 1e-05) * gain_vec


def turn(tiles):
    return pltpu.roll(tiles, HALF, axis=tiles.ndim - 2)


def cell_is_low(shape):
    return lax.broadcasted_iota(jnp.int32, shape, len(shape) - 2) < HALF


def window_bias(table_ref, pad_ref, bias_ref):
    span = 2 * WIN - 1
    pitch = 2 * WIN
    width = pitch * pitch
    pad_ref[...] = jnp.zeros(pad_ref.shape, F32)
    pad_ref[:, : span * span] = table_ref[...] * LOG2E
    packed = pad_ref[...]
    line = lax.broadcasted_iota(jnp.int32, packed.shape, 1) // pitch
    flat = packed
    for a in range(1, span):
        flat = jnp.where(line == a, pltpu.roll(packed, a, axis=1), flat)
    even = lax.broadcasted_iota(jnp.int32, (WIN, LANES), 1) % pitch < WIN
    for group in range(4):
        for pair in range(2):
            head = group * 4 + pair * 2
            row_even = jnp.broadcast_to(flat[head : head + 1, :], (WIN, width))
            row_odd = jnp.broadcast_to(flat[head + 1 : head + 2, :], (WIN, width))
            for key_row in range(WIN):
                back = (WIN - 1 - key_row) * pitch + WIN - 1
                a = pltpu.roll(row_even, (width - back) % width, axis=1, stride=1, stride_axis=0)
                b = pltpu.roll(
                    row_odd, (width - back + WIN) % width, axis=1, stride=1, stride_axis=0
                )
                bias_ref[
                    group,
                    key_row * WIN : (key_row + 1) * WIN,
                    pair * LANES : (pair + 1) * LANES,
                ] = jnp.where(even, a[:, :LANES], b[:, :LANES])


def spread_heads(q):
    head = lax.broadcasted_iota(jnp.int32, (1, 1, LANES), 2) // 32
    tiles = q.astype(F32).reshape(WIN, WIN, LANES)
    pieces = []
    for pair in range(2):
        both = [jnp.where(head == pair * 2 + k, tiles, 0.0)[:, None] for k in range(2)]
        pieces.append(jnp.concatenate(both, axis=1).reshape(2 * CELLS, LANES))
    return jnp.concatenate(pieces, axis=0).astype(BF16)


def gather_heads(o):
    head = lax.broadcasted_iota(jnp.int32, (1, 1, LANES), 2) // 32
    parts = o.reshape(2, WIN, 2, WIN, LANES)
    low = jnp.where(head == 0, parts[0, :, 0], parts[0, :, 1])
    high = jnp.where(head == 2, parts[1, :, 0], parts[1, :, 1])
    return jnp.where(head < 2, low, high).reshape(CELLS, LANES)


def soften(s):
    e = jnp.exp2(s - jnp.max(s, axis=0, keepdims=True))
    return (e * (1.0 / jnp.sum(e, axis=0, keepdims=True))).astype(BF16)


AWAY = sorted(
    ((z, x) for z in range(4) for x in range(4)),
    key=lambda d: (min(d[0], 4 - d[0]) + min(d[1], 4 - d[1]), d),
)
PEERS = 32
CAP = 32
GROUPS = 4
PER_GROUP = PEERS // GROUPS
ROWS = PER_GROUP * CAP


def token_routes(routes_ref):
    grid = routes_ref[...].reshape(16, 32).astype(F32).astype(BF16)
    token = lax.broadcasted_iota(jnp.int32, (32, 512), 1)
    row = ((token // 64) % 4 * 8 + 4 + (token // 8) % 8) % 32
    at_row = jnp.where(lax.broadcasted_iota(jnp.int32, (32, 512), 0) == row, 1.0, 0.0)
    token = lax.broadcasted_iota(jnp.int32, (16, 512), 1)
    cell = token % 8
    column = jnp.where(token < 256, HALF + cell, (cell + 12) % 16)
    at_column = lax.broadcasted_iota(jnp.int32, (16, 512), 0) == column
    picked = jnp.where(at_column, dot(grid, at_row.astype(BF16)), 0.0)
    return jnp.sum(picked, axis=0, keepdims=True).astype(jnp.int32)


def kernel(
    x_ref,
    routes_ref,
    table_r_ref,
    table_s_ref,
    gain_r_ref,
    gain_m_ref,
    gain_s_ref,
    gain_e_ref,
    qkv_r_hbm,
    proj_r_hbm,
    up_hbm,
    down_hbm,
    qkv_s_hbm,
    proj_s_hbm,
    own_in,
    own_out,
    enc_ref,
    qkv_r,
    proj_r,
    up,
    down,
    qkv_s,
    proj_s,
    load_sem,
    pad,
    bias_r,
    bias_s,
    tiles,
    qkv_buf,
    edge_buf,
    heads,
    third_buf,
    to_left,
    to_right,
    from_left,
    from_right,
    send_sem,
    recv_sem,
    shard_send,
    shard_recv,
    w_in,
    w_out,
    place,
    take,
    outgoing,
    arrived,
    result,
    returned,
    go_send,
    go_recv,
    back_send,
    back_recv,
    heads_sem,
    ready_sem,
):
    band = lax.axis_index("band")
    bands = lax.axis_size("band")
    right = lax.rem(band + 1, bands)
    left = lax.rem(band + bands - 1, bands)
    me = lax.axis_index("expert")
    my_z, my_x, my_core = me // 8, (me // 2) % 4, me % 2
    hosted = band // 2
    mirror = bands - 1 - band
    beside = hosted * 4 + 1 - band
    served = jnp.where(my_core == 0, band, mirror)
    keeper = my_core == hosted
    sibling = me + 1 - 2 * my_core

    def chip(n, sign):
        z, x = AWAY[n // 2]
        return ((my_z + 4 + sign * z) % 4 * 4 + (my_x + 4 + sign * x) % 4) * 2

    barrier = pltpu.get_barrier_semaphore()

    def tell(sem, expert, level):
        to = {"band": level, "expert": expert}
        pl.semaphore_signal(sem, inc=1, device_id=to, device_id_type=MESH)

    head = my_z * 8
    is_head = me == head
    other_heads = [
        ((head + 8 * n) % PEERS, level) for level in (band, mirror) for n in range(4)
    ][1:]
    tell(barrier, me, left)
    tell(barrier, me, right)
    tell(barrier, sibling, band)

    @pl.when(is_head)
    def _():
        for other in other_heads:
            tell(barrier, *other)

    @pl.when(jnp.logical_not(is_head))
    def _():
        tell(barrier, head, band)

    loads = [
        pltpu.make_async_copy(src, dst, load_sem.at[n])
        for n, (src, dst) in enumerate(
            (
                (qkv_r_hbm, qkv_r),
                (proj_r_hbm, proj_r),
                (up_hbm, up),
                (down_hbm, down),
                (qkv_s_hbm, qkv_s),
                (proj_s_hbm, proj_s),
                (own_in.at[0], w_in.at[0]),
                (own_out.at[0], w_out.at[0]),
            )
        )
    ]
    for load in loads[:6]:
        load.start()

    def remote(src, dst, send_sem, recv_sem, to):
        return pltpu.make_async_remote_copy(
            src_ref=src,
            dst_ref=dst,
            send_sem=send_sem,
            recv_sem=recv_sem,
            device_id=to,
            device_id_type=MESH,
        )

    shelves = (w_in, w_out)
    own = (own_in.at[0], own_out.at[0])

    def shard(src, slot, array, n, expert, level):
        return remote(
            src,
            shelves[array].at[slot],
            shard_send.at[n],
            shard_recv.at[slot * 2 + array],
            {"band": level, "expert": expert},
        )

    def leave(array):
        slot = jnp.where(keeper, 2, 1)
        return shard(own[array], slot, array, array, me, jnp.where(keeper, beside, mirror))

    def forward(array):
        return shard(shelves[array].at[1], 3, array, 2 + array, me, beside)

    def share(slot, array):
        src = own[array] if slot == 0 else shelves[array].at[slot]
        return shard(src, slot, array, 4 + slot * 2 + array, sibling, band)

    def came(slot, array):
        share(slot, array).wait_recv()

    def go(n):
        to = {"band": mirror if n % 2 else band, "expert": chip(n, 1) + n % 2}
        slot = n // 2 * 2 + my_core
        return remote(outgoing.at[n], arrived.at[slot], go_send.at[n], go_recv.at[slot], to)

    def back(n):
        to = {"band": served, "expert": chip(n, -1) + n % 2}
        slot = n // 2 * 2 + my_core
        return remote(result.at[n], returned.at[slot], back_send.at[n], back_recv.at[slot], to)

    def landed(buffer, sem, n):
        to = {"band": band, "expert": sibling}
        remote(buffer.at[n], buffer.at[n], shard_send.at[0], sem.at[n], to).wait_recv()

    def each(places, act):
        for n in places:
            if n:
                act(n)
            else:
                pl.when(my_core == 1)(functools.partial(act, n))

    routes = token_routes(routes_ref)
    code = (((routes >> 3) - my_z) & 3) * 4 + (((routes >> 1) - my_x) & 3)
    spot = jnp.zeros_like(routes)
    for n, (z, x) in enumerate(AWAY):
        spot = jnp.where(code == z * 4 + x, n, spot)
    spot = spot * 2 + ((routes - hosted) & 1)
    chosen = lax.broadcasted_iota(jnp.int32, (PEERS, 512), 0) == spot
    onehot = jnp.where(chosen, 1.0, 0.0)
    before = lax.broadcasted_iota(jnp.int32, (512, 512), 0) < lax.broadcasted_iota(
        jnp.int32, (512, 512), 1
    )
    ahead = dot(onehot.astype(BF16), jnp.where(before, 1.0, 0.0).astype(BF16))
    slot = spot.astype(F32) * CAP + jnp.sum(onehot * ahead, axis=0, keepdims=True)
    for g in range(GROUPS):
        rows = (lax.broadcasted_iota(jnp.int32, (ROWS, 512), 0) + g * ROWS).astype(F32)
        place[g * ROWS : (g + 1) * ROWS] = jnp.where(rows == slot, 1.0, 0.0).astype(BF16)

    @pl.when(is_head)
    def _():
        pl.semaphore_wait(barrier, 3 + 7 + 7)
        for other in other_heads:
            tell(heads_sem, *other)

    @pl.when(jnp.logical_not(is_head))
    def _():
        pl.semaphore_wait(barrier, 3)

    for array in range(2):
        leave(array).start()

    @pl.when(keeper)
    def _():
        for array in range(2):
            share(0, array).start()
        for load in loads[6:]:
            load.start()

    scale = LOG2E * 32**-0.5
    window_bias(table_r_ref, pad, bias_r)
    window_bias(table_s_ref, pad, bias_s)


    @pl.when(is_head)
    def _():
        pl.semaphore_wait(heads_sem, 7)
        for n in range(1, 8):
            tell(ready_sem, head + n, band)

    for load in loads[:4]:
        load.wait()

    def sends(part):
        return [
            remote(
                to_left.at[part],
                from_right.at[part],
                send_sem.at[0, part],
                recv_sem.at[0, part],
                {"band": left},
            ),
            remote(
                to_right.at[part],
                from_left.at[part],
                send_sem.at[1, part],
                recv_sem.at[1, part],
                {"band": right},
            ),
        ]

    low_cell = cell_is_low((1, WIN, 512))

    def first_part(part, carry):
        x3 = x_ref[0, pl.ds(part * 16, 16)].astype(F32)
        xf = jnp.concatenate(
            [
                x3[r * 8 : r * 8 + 8, c * 8 : c * 8 + 8, :].reshape(CELLS, 512)
                for r in range(2)
                for c in range(2)
            ],
            axis=0,
        )
        qkv_buf[...] = dot(xf.astype(BF16), qkv_r[...]).astype(BF16)
        for w in range(4):
            rows = slice(w * CELLS, (w + 1) * CELLS)
            for g in range(4):
                q = qkv_buf[rows, g * 128 : g * 128 + 128]
                k = qkv_buf[rows, 512 + g * 128 : 640 + g * 128]
                v = qkv_buf[rows, 1024 + g * 128 : 1152 + g * 128]
                s = dot_over(k, spread_heads(q), 1, 1) * scale + bias_r[g]
                heads[rows, g * 128 : g * 128 + 128] = gather_heads(
                    dot_over(soften(s), v, 0, 0)
                ).astype(BF16)
        first = (xf + layer_norm(dot(heads[...], proj_r[...]), gain_r_ref[...])).astype(BF16)
        total = jnp.zeros((256, 512), F32)
        for f in range(4):
            hidden = gelu(dot(first, up[:, f * 512 : f * 512 + 512])).astype(BF16)
            total = total + dot(hidden, down[f * 512 : f * 512 + 512, :])
        second = (first.astype(F32) + layer_norm(total, gain_m_ref[...])).astype(BF16).astype(F32)
        for r in range(2):
            rows = pl.ds(part * 16 + r * 8, 8)
            w0 = second[r * 128 : r * 128 + 64].reshape(WIN, WIN, 512)
            w1 = second[r * 128 + 64 : r * 128 + 128].reshape(WIN, WIN, 512)
            tiles[rows, 1] = w0
            tiles[rows, 2] = w1
            to_left[part, r * 32 : r * 32 + 32] = (
                jnp.where(low_cell, w0[:HALF], turn(w0[HALF:])).reshape(32, 512).astype(BF16)
            )
            to_right[part, r * 32 : r * 32 + 32] = (
                jnp.where(low_cell, turn(w1[HALF:]), w1[:HALF]).reshape(32, 512).astype(BF16)
            )
        for send in sends(part):
            send.start()

        @pl.when((part == 0) & keeper)
        def _():
            came(1, 0)
            forward(0).start()
            share(1, 0).start()

        return carry

    lax.fori_loop(0, 2, first_part, 0)

    @pl.when(keeper)
    def _():
        came(1, 1)
        forward(1).start()
        share(1, 1).start()
        for array in range(2):
            came(2, array)
            share(2, array).start()

    def shifted(column):
        pieces = []
        for w in range(4):
            for start in (w * 8 + 4, (w * 8 + 8) % 32):
                a = tiles[start : start + 4, column]
                b = tiles[start : start + 4, column + 1]
                pieces.append(turn(jnp.where(low_cell, b, a)))
        return jnp.concatenate(pieces, axis=0)

    def finish(x, first_row):
        third = x + layer_norm(dot(heads[...], proj_s[...]), gain_s_ref[...])
        third_buf[first_row : first_row + 256, :] = third.astype(BF16)

    key = lax.broadcasted_iota(jnp.int32, (CELLS, 256), 0)
    lane = lax.broadcasted_iota(jnp.int32, (CELLS, 256), 1)
    low_j = lane % 8 < HALF
    row_apart = (key // 8 < HALF) != ((lane // 16) % 8 < HALF)
    col_apart = ((key % 8 < HALF) != low_j) & (
        (low_j & (band == bands - 1)) | (jnp.logical_not(low_j) & (band == 0))
    )
    mask_row = jnp.where(row_apart, -100.0 * LOG2E, 0.0)
    mask_col = jnp.where(col_apart, -100.0 * LOG2E, 0.0)
    mask_both = jnp.where(row_apart | col_apart, -100.0 * LOG2E, 0.0)

    for load in loads[4:6]:
        load.wait()
    mid = shifted(1).reshape(256, 512)
    qkv_buf[...] = dot(mid.astype(BF16), qkv_s[...]).astype(BF16)
    for w in range(4):
        rows = slice(w * CELLS, (w + 1) * CELLS)
        for g in range(4):
            q = qkv_buf[rows, g * 128 : g * 128 + 128]
            k = qkv_buf[rows, 512 + g * 128 : 640 + g * 128]
            v = qkv_buf[rows, 1024 + g * 128 : 1152 + g * 128]
            s = dot_over(k, spread_heads(q), 1, 1) * scale + bias_s[g]
            if w == 3:
                s = s + mask_row
            heads[rows, g * 128 : g * 128 + 128] = gather_heads(
                dot_over(soften(s), v, 0, 0)
            ).astype(BF16)
    finish(mid, 0)

    for part in range(2):
        for send in sends(part):
            send.wait()
        for r in range(2):
            top = part * 16 + r * 8
            h = from_left[part, r * 32 : r * 32 + 32].astype(F32).reshape(HALF, WIN, 512)
            tiles[top : top + 4, 0] = h
            tiles[top + 4 : top + 8, 0] = turn(h)
            h = from_right[part, r * 32 : r * 32 + 32].astype(F32).reshape(HALF, WIN, 512)
            tiles[top : top + 4, 3] = h
            tiles[top + 4 : top + 8, 3] = turn(h)
    edge0 = shifted(0)
    edge2 = shifted(2)
    edge = jnp.where(low_cell, edge2, edge0).reshape(256, 512)
    qkv_buf[:, :512] = dot(edge.astype(BF16), qkv_s[:, :512]).astype(BF16)
    qkv_buf[:, 512:] = dot(edge0.reshape(256, 512).astype(BF16), qkv_s[:, 512:]).astype(BF16)
    edge_buf[...] = dot(edge2.reshape(256, 512).astype(BF16), qkv_s[:, 512:]).astype(BF16)
    for w in range(4):
        rows = slice(w * CELLS, (w + 1) * CELLS)
        for g in range(4):
            q = spread_heads(qkv_buf[rows, g * 128 : g * 128 + 128])
            k0 = qkv_buf[rows, 512 + g * 128 : 640 + g * 128]
            v0 = qkv_buf[rows, 1024 + g * 128 : 1152 + g * 128]
            k2 = edge_buf[rows, g * 128 : g * 128 + 128]
            v2 = edge_buf[rows, 512 + g * 128 : 640 + g * 128]
            s = jnp.where(low_j, dot_over(k2, q, 1, 1), dot_over(k0, q, 1, 1))
            s = s * scale + bias_s[g] + (mask_both if w == 3 else mask_col)
            o = dot_over(soften(s), jnp.concatenate([v2, v0], axis=1), 0, 0)
            o2 = gather_heads(o[:, :LANES]).reshape(WIN, WIN, LANES)
            o0 = gather_heads(o[:, LANES:]).reshape(WIN, WIN, LANES)
            heads[rows, g * 128 : g * 128 + 128] = (
                jnp.where(cell_is_low((1, WIN, LANES)), o2, o0).reshape(CELLS, LANES).astype(BF16)
            )
    finish(edge, 256)

    @pl.when(jnp.logical_not(is_head))
    def _():
        pl.semaphore_wait(ready_sem, 1)

    groups = range(GROUPS)[::-1]

    def places(g):
        return range(g * PER_GROUP, (g + 1) * PER_GROUP)[::-1]

    def keep(block, buffer):
        @pl.when(my_core == 0)
        def _():
            buffer[0] = block

    third = third_buf[...]
    for g in groups:
        block = dot(place[g * ROWS : (g + 1) * ROWS], third).astype(BF16)
        block = block.reshape(PER_GROUP, CAP, 512)
        outgoing[g * PER_GROUP : (g + 1) * PER_GROUP] = block
        if g == 0:
            keep(block[0], arrived)
        each(places(g), lambda n: go(n).start())

    slot_column = jnp.transpose(jnp.broadcast_to(slot, (LANES, 512)))
    lane = lax.broadcasted_iota(jnp.int32, (512, LANES), 1).astype(F32)
    for n in range(PEERS * CAP // LANES):
        take[:, n * LANES : (n + 1) * LANES] = jnp.where(
            slot_column == lane + n * LANES, 1.0, 0.0
        ).astype(BF16)

    @pl.when(keeper)
    def _():
        came(3, 0)
        share(3, 0).start()
        for load in loads[6:]:
            load.wait()

    @pl.when(jnp.logical_not(keeper))
    def _():
        for slot in range(3):
            for array in range(2):
                came(slot, array)
        came(3, 0)

    def layer(rows, n):
        hidden = gelu(dot(rows, w_in[n])).astype(BF16)
        return dot(hidden, w_out[n])

    for g in groups:
        each(places(g), lambda n: landed(arrived, go_recv, n))
        rows = arrived[g * PER_GROUP : (g + 1) * PER_GROUP].reshape(ROWS, 512)
        total = layer(rows, 0) + layer(rows, 1) + layer(rows, 2)
        if g == GROUPS - 1:
            came(3, 1)

            @pl.when(keeper)
            def _():
                share(3, 1).start()

        block = (total + layer(rows, 3)).astype(BF16).reshape(PER_GROUP, CAP, 512)
        result[g * PER_GROUP : (g + 1) * PER_GROUP] = block
        if g == 0:
            keep(block[0], returned)
        each(places(g), lambda n: back(n).start())

    for array in range(2):
        leave(array).wait_send()

    @pl.when(keeper)
    def _():
        for array in range(2):
            forward(array).wait_send()
            for slot in range(4):
                share(slot, array).wait_send()

    rows = jnp.zeros((512, 512), F32)
    for g in groups:
        each(places(g), lambda n: landed(returned, back_recv, n))
        block = returned[g * PER_GROUP : (g + 1) * PER_GROUP].reshape(ROWS, 512)
        rows = rows + dot(take[:, g * ROWS : (g + 1) * ROWS], block)
    encoded = third_buf[...].astype(F32) + layer_norm(rows, gain_e_ref[...])
    for w in range(4):
        mid = encoded[w * CELLS : (w + 1) * CELLS].reshape(WIN, WIN, 512)
        edge = encoded[256 + w * CELLS : 256 + (w + 1) * CELLS].reshape(WIN, WIN, 512)
        w0 = turn(jnp.where(low_cell, mid, edge))
        w1 = turn(jnp.where(low_cell, edge, mid))
        block = jnp.concatenate([w0, w1], axis=1).astype(BF16)
        for half in range(2):
            top = (w * 8 + 4 + half * 4) % 32
            enc_ref[0, top : top + 4] = block[half * 4 : half * 4 + 4]
    for g in groups:
        each(places(g), lambda n: go(n).wait_send())
        each(places(g), lambda n: back(n).wait_send())


def block_pair(features, routes, tables, gains, weights, shards):
    vmem = pl.BlockSpec(memory_space=pltpu.VMEM)
    hbm = pl.BlockSpec(memory_space=pl.ANY)
    dma = pltpu.SemaphoreType.DMA
    return pl.pallas_call(
        kernel,
        out_shape=jax.ShapeDtypeStruct((1, 32, 16, 512), BF16),
        in_specs=[vmem] * 8 + [hbm] * 8,
        out_specs=vmem,
        scratch_shapes=[pltpu.VMEM(w.shape, BF16) for w in weights]
        + [
            dma((8,)),
            pltpu.VMEM((16, 256), F32),
            pltpu.VMEM((4, CELLS, 256), F32),
            pltpu.VMEM((4, CELLS, 256), F32),
            pltpu.VMEM((32, 4, WIN, 512), F32),
            pltpu.VMEM((256, 1536), BF16),
            pltpu.VMEM((256, 1024), BF16),
            pltpu.VMEM((256, 512), BF16),
            pltpu.VMEM((512, 512), BF16),
        ]
        + [pltpu.VMEM((2, 64, 512), BF16)] * 4
        + [dma((2, 2)), dma((2, 2)), dma((12,)), dma((8,))]
        + [
            pltpu.VMEM((4, 512, 512), BF16),
            pltpu.VMEM((4, 512, 512), BF16),
            pltpu.VMEM((PEERS * CAP, 512), BF16),
            pltpu.VMEM((512, PEERS * CAP), BF16),
        ]
        + [pltpu.VMEM((PEERS, CAP, 512), BF16)] * 4
        + [dma((PEERS,))] * 4
        + [pltpu.SemaphoreType.REGULAR] * 2,
        compiler_params=pltpu.CompilerParams(
            collective_id=0, has_side_effects=True, vmem_limit_bytes=62 * 1024 * 1024
        ),
        name="block_pair",
    )(features, routes, *tables, *gains, *weights, *shards)


def local(
    features,
    routes,
    qkv_regular,
    proj_regular,
    table_regular,
    gain_regular,
    mlp_up,
    mlp_down,
    gain_mlp,
    qkv_shifted,
    proj_shifted,
    table_shifted,
    gain_shifted,
    expert_in,
    expert_out,
    gain_expert,
):
    gains = (gain_regular, gain_mlp, gain_shifted, gain_expert)
    return block_pair(
        features,
        routes.reshape(32, 16).T.reshape(16, 1, 32),
        (table_regular.T, table_shifted.T),
        [g.reshape(1, 512) for g in gains],
        (qkv_regular, proj_regular, mlp_up, mlp_down, qkv_shifted, proj_shifted),
        (expert_in, expert_out),
    )


def solution(mesh):
    return jax.shard_map(
        local,
        mesh=mesh,
        in_specs=(
            P("expert", None, "band", None),
            P("expert", "band", None, None, None),
        )
        + (P(),) * 11
        + (P("expert", None, "band"), P("expert", "band", None), P()),
        out_specs=P("expert", None, "band", None),
        check_vma=False,
    )
```

```python
import functools
import jax
import jax.numpy as jnp
from jax import lax
from jax.experimental import pallas as pl
from jax.experimental.pallas import tpu as pltpu
from jax.sharding import PartitionSpec as P

MESH = pl.DeviceIdType.MESH
F32 = jnp.float32
BF16 = jnp.bfloat16
WIN = 8
HALF = WIN // 2
CELLS = WIN * WIN
LANES = 128
LOG2E = 1.4426950408889634
ROOT_HALF = 0.7071067811865476


def dot(a, b):
    return jnp.dot(a, b, preferred_element_type=F32)


def dot_over(a, b, dim_a, dim_b):
    return lax.dot_general(a, b, (((dim_a,), (dim_b,)), ((), ())), preferred_element_type=F32)


def gelu(v):
    return (0.5 * v) * (1.0 + lax.erf(v * ROOT_HALF))


def layer_norm(values, gain_vec):
    centre = jnp.mean(values, axis=-1, keepdims=True)
    offsets = values - centre
    spread = jnp.mean(offsets * offsets, axis=-1, keepdims=True)
    return offsets * lax.rsqrt(spread + 1e-05) * gain_vec


def turn(tiles):
    return pltpu.roll(tiles, HALF, axis=tiles.ndim - 2)


def cell_is_low(shape):
    return lax.broadcasted_iota(jnp.int32, shape, len(shape) - 2) < HALF


def window_bias(table_ref, pad_ref, bias_ref):
    span = 2 * WIN - 1
    pitch = 2 * WIN
    width = pitch * pitch
    pad_ref[...] = jnp.zeros(pad_ref.shape, F32)
    pad_ref[:, : span * span] = table_ref[...] * LOG2E
    packed = pad_ref[...]
    line = lax.broadcasted_iota(jnp.int32, packed.shape, 1) // pitch
    flat = packed
    for a in range(1, span):
        flat = jnp.where(line == a, pltpu.roll(packed, a, axis=1), flat)
    even = lax.broadcasted_iota(jnp.int32, (WIN, LANES), 1) % pitch < WIN
    for group in range(4):
        for pair in range(2):
            head = group * 4 + pair * 2
            row_even = jnp.broadcast_to(flat[head : head + 1, :], (WIN, width))
            row_odd = jnp.broadcast_to(flat[head + 1 : head + 2, :], (WIN, width))
            for key_row in range(WIN):
                back = (WIN - 1 - key_row) * pitch + WIN - 1
                a = pltpu.roll(row_even, (width - back) % width, axis=1, stride=1, stride_axis=0)
                b = pltpu.roll(
                    row_odd, (width - back + WIN) % width, axis=1, stride=1, stride_axis=0
                )
                bias_ref[
                    group,
                    key_row * WIN : (key_row + 1) * WIN,
                    pair * LANES : (pair + 1) * LANES,
                ] = jnp.where(even, a[:, :LANES], b[:, :LANES])


def spread_heads(q):
    head = lax.broadcasted_iota(jnp.int32, (1, 1, LANES), 2) // 32
    tiles = q.astype(F32).reshape(WIN, WIN, LANES)
    pieces = []
    for pair in range(2):
        both = [jnp.where(head == pair * 2 + k, tiles, 0.0)[:, None] for k in range(2)]
        pieces.append(jnp.concatenate(both, axis=1).reshape(2 * CELLS, LANES))
    return jnp.concatenate(pieces, axis=0).astype(BF16)


def gather_heads(o):
    head = lax.broadcasted_iota(jnp.int32, (1, 1, LANES), 2) // 32
    parts = o.reshape(2, WIN, 2, WIN, LANES)
    low = jnp.where(head == 0, parts[0, :, 0], parts[0, :, 1])
    high = jnp.where(head == 2, parts[1, :, 0], parts[1, :, 1])
    return jnp.where(head < 2, low, high).reshape(CELLS, LANES)


def soften(s):
    e = jnp.exp2(s - jnp.max(s, axis=0, keepdims=True))
    return (e * (1.0 / jnp.sum(e, axis=0, keepdims=True))).astype(BF16)


AWAY = sorted(
    ((z, x) for z in range(4) for x in range(4)),
    key=lambda d: (min(d[0], 4 - d[0]) + min(d[1], 4 - d[1]), d),
)
PEERS = 32
CAP = 32
GROUPS = 4
PER_GROUP = PEERS // GROUPS
ROWS = PER_GROUP * CAP


def token_routes(routes_ref):
    grid = routes_ref[...].reshape(16, 32).astype(F32).astype(BF16)
    token = lax.broadcasted_iota(jnp.int32, (32, 512), 1)
    row = ((token // 64) % 4 * 8 + 4 + (token // 8) % 8) % 32
    at_row = jnp.where(lax.broadcasted_iota(jnp.int32, (32, 512), 0) == row, 1.0, 0.0)
    token = lax.broadcasted_iota(jnp.int32, (16, 512), 1)
    cell = token % 8
    column = jnp.where(token < 256, HALF + cell, (cell + 12) % 16)
    at_column = lax.broadcasted_iota(jnp.int32, (16, 512), 0) == column
    picked = jnp.where(at_column, dot(grid, at_row.astype(BF16)), 0.0)
    return jnp.sum(picked, axis=0, keepdims=True).astype(jnp.int32)


def kernel(
    x_ref,
    routes_ref,
    table_r_ref,
    table_s_ref,
    gain_r_ref,
    gain_m_ref,
    gain_s_ref,
    gain_e_ref,
    qkv_r_hbm,
    proj_r_hbm,
    up_hbm,
    down_hbm,
    qkv_s_hbm,
    proj_s_hbm,
    own_in,
    own_out,
    enc_ref,
    qkv_r,
    proj_r,
    up,
    down,
    qkv_s,
    proj_s,
    load_sem,
    pad,
    bias_r,
    bias_s,
    tiles,
    qkv_buf,
    edge_buf,
    heads,
    third_buf,
    to_left,
    to_right,
    from_left,
    from_right,
    send_sem,
    recv_sem,
    shard_send,
    shard_recv,
    w_in,
    w_out,
    place,
    take,
    outgoing,
    arrived,
    result,
    returned,
    go_send,
    go_recv,
    back_send,
    back_recv,
    heads_sem,
    ready_sem,
):
    band = lax.axis_index("band")
    bands = lax.axis_size("band")
    right = lax.rem(band + 1, bands)
    left = lax.rem(band + bands - 1, bands)
    me = lax.axis_index("expert")
    my_z, my_x, my_core = me // 8, (me // 2) % 4, me % 2
    hosted = band // 2
    mirror = bands - 1 - band
    beside = hosted * 4 + 1 - band
    served = jnp.where(my_core == 0, band, mirror)
    keeper = my_core == hosted
    sibling = me + 1 - 2 * my_core

    def chip(n, sign):
        z, x = AWAY[n // 2]
        return ((my_z + 4 + sign * z) % 4 * 4 + (my_x + 4 + sign * x) % 4) * 2

    barrier = pltpu.get_barrier_semaphore()

    def tell(sem, expert, level):
        to = {"band": level, "expert": expert}
        pl.semaphore_signal(sem, inc=1, device_id=to, device_id_type=MESH)

    head = my_z * 8
    is_head = me == head
    other_heads = [
        ((head + 8 * n) % PEERS, level) for level in (band, mirror) for n in range(4)
    ][1:]
    tell(barrier, me, left)
    tell(barrier, me, right)
    tell(barrier, sibling, band)

    @pl.when(is_head)
    def _():
        for other in other_heads:
            tell(barrier, *other)

    @pl.when(jnp.logical_not(is_head))
    def _():
        tell(barrier, head, band)

    loads = [
        pltpu.make_async_copy(src, dst, load_sem.at[n])
        for n, (src, dst) in enumerate(
            (
                (qkv_r_hbm, qkv_r),
                (proj_r_hbm, proj_r),
                (up_hbm, up),
                (down_hbm, down),
                (qkv_s_hbm, qkv_s),
                (proj_s_hbm, proj_s),
                (own_in.at[0], w_in.at[0]),
                (own_out.at[0], w_out.at[0]),
            )
        )
    ]
    for load in loads[:6]:
        load.start()

    def remote(src, dst, send_sem, recv_sem, to):
        return pltpu.make_async_remote_copy(
            src_ref=src,
            dst_ref=dst,
            send_sem=send_sem,
            recv_sem=recv_sem,
            device_id=to,
            device_id_type=MESH,
        )

    shelves = (w_in, w_out)
    own = (own_in.at[0], own_out.at[0])

    def shard(src, slot, array, n, expert, level):
        return remote(
            src,
            shelves[array].at[slot],
            shard_send.at[n],
            shard_recv.at[slot * 2 + array],
            {"band": level, "expert": expert},
        )

    def leave(array):
        slot = jnp.where(keeper, 2, 1)
        return shard(own[array], slot, array, array, me, jnp.where(keeper, beside, mirror))

    def forward(array):
        return shard(shelves[array].at[1], 3, array, 2 + array, me, beside)

    def share(slot, array):
        src = own[array] if slot == 0 else shelves[array].at[slot]
        return shard(src, slot, array, 4 + slot * 2 + array, sibling, band)

    def came(slot, array):
        share(slot, array).wait_recv()

    def go(n):
        to = {"band": mirror if n % 2 else band, "expert": chip(n, 1) + n % 2}
        slot = n // 2 * 2 + my_core
        return remote(outgoing.at[n], arrived.at[slot], go_send.at[n], go_recv.at[slot], to)

    def back(n):
        to = {"band": served, "expert": chip(n, -1) + n % 2}
        slot = n // 2 * 2 + my_core
        return remote(result.at[n], returned.at[slot], back_send.at[n], back_recv.at[slot], to)

    def landed(buffer, sem, n):
        to = {"band": band, "expert": sibling}
        remote(buffer.at[n], buffer.at[n], shard_send.at[0], sem.at[n], to).wait_recv()

    def each(places, act):
        for n in places:
            if n:
                act(n)
            else:
                pl.when(my_core == 1)(functools.partial(act, n))

    routes = token_routes(routes_ref)
    code = (((routes >> 3) - my_z) & 3) * 4 + (((routes >> 1) - my_x) & 3)
    spot = jnp.zeros_like(routes)
    for n, (z, x) in enumerate(AWAY):
        spot = jnp.where(code == z * 4 + x, n, spot)
    spot = spot * 2 + ((routes - hosted) & 1)
    chosen = lax.broadcasted_iota(jnp.int32, (PEERS, 512), 0) == spot
    onehot = jnp.where(chosen, 1.0, 0.0)
    before = lax.broadcasted_iota(jnp.int32, (512, 512), 0) < lax.broadcasted_iota(
        jnp.int32, (512, 512), 1
    )
    ahead = dot(onehot.astype(BF16), jnp.where(before, 1.0, 0.0).astype(BF16))
    slot = spot.astype(F32) * CAP + jnp.sum(onehot * ahead, axis=0, keepdims=True)
    for g in range(GROUPS):
        rows = (lax.broadcasted_iota(jnp.int32, (ROWS, 512), 0) + g * ROWS).astype(F32)
        place[g * ROWS : (g + 1) * ROWS] = jnp.where(rows == slot, 1.0, 0.0).astype(BF16)

    @pl.when(is_head)
    def _():
        pl.semaphore_wait(barrier, 3 + 7 + 7)
        for other in other_heads:
            tell(heads_sem, *other)

    @pl.when(jnp.logical_not(is_head))
    def _():
        pl.semaphore_wait(barrier, 3)

    for array in range(2):
        leave(array).start()

    @pl.when(keeper)
    def _():
        for array in range(2):
            share(0, array).start()
        for load in loads[6:]:
            load.start()

    scale = LOG2E * 32**-0.5
    window_bias(table_r_ref, pad, bias_r)
    window_bias(table_s_ref, pad, bias_s)


    @pl.when(is_head)
    def _():
        pl.semaphore_wait(heads_sem, 7)
        for n in range(1, 8):
            tell(ready_sem, head + n, band)

    for load in loads[:4]:
        load.wait()

    def sends(part):
        return [
            remote(
                to_left.at[part],
                from_right.at[part],
                send_sem.at[0, part],
                recv_sem.at[0, part],
                {"band": left},
            ),
            remote(
                to_right.at[part],
                from_left.at[part],
                send_sem.at[1, part],
                recv_sem.at[1, part],
                {"band": right},
            ),
        ]

    low_cell = cell_is_low((1, WIN, 512))

    def first_part(part, carry):
        x3 = x_ref[0, pl.ds(part * 16, 16)].astype(F32)
        xf = jnp.concatenate(
            [
                x3[r * 8 : r * 8 + 8, c * 8 : c * 8 + 8, :].reshape(CELLS, 512)
                for r in range(2)
                for c in range(2)
            ],
            axis=0,
        )
        qkv_buf[...] = dot(xf.astype(BF16), qkv_r[...]).astype(BF16)
        for w in range(4):
            rows = slice(w * CELLS, (w + 1) * CELLS)
            for g in range(4):
                q = qkv_buf[rows, g * 128 : g * 128 + 128]
                k = qkv_buf[rows, 512 + g * 128 : 640 + g * 128]
                v = qkv_buf[rows, 1024 + g * 128 : 1152 + g * 128]
                s = dot_over(k, spread_heads(q), 1, 1) * scale + bias_r[g]
                heads[rows, g * 128 : g * 128 + 128] = gather_heads(
                    dot_over(soften(s), v, 0, 0)
                ).astype(BF16)
        first = (xf + layer_norm(dot(heads[...], proj_r[...]), gain_r_ref[...])).astype(BF16)
        total = jnp.zeros((256, 512), F32)
        for f in range(4):
            hidden = gelu(dot(first, up[:, f * 512 : f * 512 + 512])).astype(BF16)
            total = total + dot(hidden, down[f * 512 : f * 512 + 512, :])
        second = (first.astype(F32) + layer_norm(total, gain_m_ref[...])).astype(BF16).astype(F32)
        for r in range(2):
            rows = pl.ds(part * 16 + r * 8, 8)
            w0 = second[r * 128 : r * 128 + 64].reshape(WIN, WIN, 512)
            w1 = second[r * 128 + 64 : r * 128 + 128].reshape(WIN, WIN, 512)
            tiles[rows, 1] = w0
            tiles[rows, 2] = w1
            to_left[part, r * 32 : r * 32 + 32] = (
                jnp.where(low_cell, w0[:HALF], turn(w0[HALF:])).reshape(32, 512).astype(BF16)
            )
            to_right[part, r * 32 : r * 32 + 32] = (
                jnp.where(low_cell, turn(w1[HALF:]), w1[:HALF]).reshape(32, 512).astype(BF16)
            )
        for send in sends(part):
            send.start()

        return carry

    lax.fori_loop(0, 2, first_part, 0)

    @pl.when(keeper)
    def _():
        for array in range(2):
            came(1, array)
            forward(array).start()
            share(1, array).start()
        for array in range(2):
            came(2, array)
            share(2, array).start()

    def shifted(column):
        pieces = []
        for w in range(4):
            for start in (w * 8 + 4, (w * 8 + 8) % 32):
                a = tiles[start : start + 4, column]
                b = tiles[start : start + 4, column + 1]
                pieces.append(turn(jnp.where(low_cell, b, a)))
        return jnp.concatenate(pieces, axis=0)

    def finish(x, first_row):
        third = x + layer_norm(dot(heads[...], proj_s[...]), gain_s_ref[...])
        third_buf[first_row : first_row + 256, :] = third.astype(BF16)

    key = lax.broadcasted_iota(jnp.int32, (CELLS, 256), 0)
    lane = lax.broadcasted_iota(jnp.int32, (CELLS, 256), 1)
    low_j = lane % 8 < HALF
    row_apart = (key // 8 < HALF) != ((lane // 16) % 8 < HALF)
    col_apart = ((key % 8 < HALF) != low_j) & (
        (low_j & (band == bands - 1)) | (jnp.logical_not(low_j) & (band == 0))
    )
    mask_row = jnp.where(row_apart, -100.0 * LOG2E, 0.0)
    mask_col = jnp.where(col_apart, -100.0 * LOG2E, 0.0)
    mask_both = jnp.where(row_apart | col_apart, -100.0 * LOG2E, 0.0)

    for load in loads[4:6]:
        load.wait()
    mid = shifted(1).reshape(256, 512)
    qkv_buf[...] = dot(mid.astype(BF16), qkv_s[...]).astype(BF16)
    for w in range(4):
        rows = slice(w * CELLS, (w + 1) * CELLS)
        for g in range(4):
            q = qkv_buf[rows, g * 128 : g * 128 + 128]
            k = qkv_buf[rows, 512 + g * 128 : 640 + g * 128]
            v = qkv_buf[rows, 1024 + g * 128 : 1152 + g * 128]
            s = dot_over(k, spread_heads(q), 1, 1) * scale + bias_s[g]
            if w == 3:
                s = s + mask_row
            heads[rows, g * 128 : g * 128 + 128] = gather_heads(
                dot_over(soften(s), v, 0, 0)
            ).astype(BF16)
    finish(mid, 0)

    for part in range(2):
        for send in sends(part):
            send.wait()
        for r in range(2):
            top = part * 16 + r * 8
            h = from_left[part, r * 32 : r * 32 + 32].astype(F32).reshape(HALF, WIN, 512)
            tiles[top : top + 4, 0] = h
            tiles[top + 4 : top + 8, 0] = turn(h)
            h = from_right[part, r * 32 : r * 32 + 32].astype(F32).reshape(HALF, WIN, 512)
            tiles[top : top + 4, 3] = h
            tiles[top + 4 : top + 8, 3] = turn(h)
    edge0 = shifted(0)
    edge2 = shifted(2)
    edge = jnp.where(low_cell, edge2, edge0).reshape(256, 512)
    qkv_buf[:, :512] = dot(edge.astype(BF16), qkv_s[:, :512]).astype(BF16)
    qkv_buf[:, 512:] = dot(edge0.reshape(256, 512).astype(BF16), qkv_s[:, 512:]).astype(BF16)
    edge_buf[...] = dot(edge2.reshape(256, 512).astype(BF16), qkv_s[:, 512:]).astype(BF16)
    for w in range(4):
        rows = slice(w * CELLS, (w + 1) * CELLS)
        for g in range(4):
            q = spread_heads(qkv_buf[rows, g * 128 : g * 128 + 128])
            k0 = qkv_buf[rows, 512 + g * 128 : 640 + g * 128]
            v0 = qkv_buf[rows, 1024 + g * 128 : 1152 + g * 128]
            k2 = edge_buf[rows, g * 128 : g * 128 + 128]
            v2 = edge_buf[rows, 512 + g * 128 : 640 + g * 128]
            s = jnp.where(low_j, dot_over(k2, q, 1, 1), dot_over(k0, q, 1, 1))
            s = s * scale + bias_s[g] + (mask_both if w == 3 else mask_col)
            o = dot_over(soften(s), jnp.concatenate([v2, v0], axis=1), 0, 0)
            o2 = gather_heads(o[:, :LANES]).reshape(WIN, WIN, LANES)
            o0 = gather_heads(o[:, LANES:]).reshape(WIN, WIN, LANES)
            heads[rows, g * 128 : g * 128 + 128] = (
                jnp.where(cell_is_low((1, WIN, LANES)), o2, o0).reshape(CELLS, LANES).astype(BF16)
            )
    finish(edge, 256)

    @pl.when(jnp.logical_not(is_head))
    def _():
        pl.semaphore_wait(ready_sem, 1)

    groups = range(GROUPS)[::-1]

    def places(g):
        return range(g * PER_GROUP, (g + 1) * PER_GROUP)[::-1]

    def keep(block, buffer):
        @pl.when(my_core == 0)
        def _():
            buffer[0] = block

    third = third_buf[...]
    for g in groups:
        block = dot(place[g * ROWS : (g + 1) * ROWS], third).astype(BF16)
        block = block.reshape(PER_GROUP, CAP, 512)
        outgoing[g * PER_GROUP : (g + 1) * PER_GROUP] = block
        if g == 0:
            keep(block[0], arrived)
        each(places(g), lambda n: go(n).start())

    slot_column = jnp.transpose(jnp.broadcast_to(slot, (LANES, 512)))
    lane = lax.broadcasted_iota(jnp.int32, (512, LANES), 1).astype(F32)
    for n in range(PEERS * CAP // LANES):
        take[:, n * LANES : (n + 1) * LANES] = jnp.where(
            slot_column == lane + n * LANES, 1.0, 0.0
        ).astype(BF16)

    @pl.when(keeper)
    def _():
        came(3, 0)
        share(3, 0).start()
        for load in loads[6:]:
            load.wait()

    @pl.when(jnp.logical_not(keeper))
    def _():
        for slot in range(3):
            for array in range(2):
                came(slot, array)
        came(3, 0)

    def layer(rows, n):
        hidden = gelu(dot(rows, w_in[n])).astype(BF16)
        return dot(hidden, w_out[n])

    for g in groups:
        each(places(g), lambda n: landed(arrived, go_recv, n))
        rows = arrived[g * PER_GROUP : (g + 1) * PER_GROUP].reshape(ROWS, 512)
        total = layer(rows, 0) + layer(rows, 1) + layer(rows, 2)
        if g == GROUPS - 1:
            came(3, 1)

            @pl.when(keeper)
            def _():
                share(3, 1).start()

        block = (total + layer(rows, 3)).astype(BF16).reshape(PER_GROUP, CAP, 512)
        result[g * PER_GROUP : (g + 1) * PER_GROUP] = block
        if g == 0:
            keep(block[0], returned)
        each(places(g), lambda n: back(n).start())

    for array in range(2):
        leave(array).wait_send()

    @pl.when(keeper)
    def _():
        for array in range(2):
            forward(array).wait_send()
            for slot in range(4):
                share(slot, array).wait_send()

    rows = jnp.zeros((512, 512), F32)
    for g in groups:
        each(places(g), lambda n: landed(returned, back_recv, n))
        block = returned[g * PER_GROUP : (g + 1) * PER_GROUP].reshape(ROWS, 512)
        rows = rows + dot(take[:, g * ROWS : (g + 1) * ROWS], block)
    encoded = third_buf[...].astype(F32) + layer_norm(rows, gain_e_ref[...])
    for w in range(4):
        mid = encoded[w * CELLS : (w + 1) * CELLS].reshape(WIN, WIN, 512)
        edge = encoded[256 + w * CELLS : 256 + (w + 1) * CELLS].reshape(WIN, WIN, 512)
        w0 = turn(jnp.where(low_cell, mid, edge))
        w1 = turn(jnp.where(low_cell, edge, mid))
        block = jnp.concatenate([w0, w1], axis=1).astype(BF16)
        for half in range(2):
            top = (w * 8 + 4 + half * 4) % 32
            enc_ref[0, top : top + 4] = block[half * 4 : half * 4 + 4]
    for g in groups:
        each(places(g), lambda n: go(n).wait_send())
        each(places(g), lambda n: back(n).wait_send())


def block_pair(features, routes, tables, gains, weights, shards):
    vmem = pl.BlockSpec(memory_space=pltpu.VMEM)
    hbm = pl.BlockSpec(memory_space=pl.ANY)
    dma = pltpu.SemaphoreType.DMA
    return pl.pallas_call(
        kernel,
        out_shape=jax.ShapeDtypeStruct((1, 32, 16, 512), BF16),
        in_specs=[vmem] * 8 + [hbm] * 8,
        out_specs=vmem,
        scratch_shapes=[pltpu.VMEM(w.shape, BF16) for w in weights]
        + [
            dma((8,)),
            pltpu.VMEM((16, 256), F32),
            pltpu.VMEM((4, CELLS, 256), F32),
            pltpu.VMEM((4, CELLS, 256), F32),
            pltpu.VMEM((32, 4, WIN, 512), F32),
            pltpu.VMEM((256, 1536), BF16),
            pltpu.VMEM((256, 1024), BF16),
            pltpu.VMEM((256, 512), BF16),
            pltpu.VMEM((512, 512), BF16),
        ]
        + [pltpu.VMEM((2, 64, 512), BF16)] * 4
        + [dma((2, 2)), dma((2, 2)), dma((12,)), dma((8,))]
        + [
            pltpu.VMEM((4, 512, 512), BF16),
            pltpu.VMEM((4, 512, 512), BF16),
            pltpu.VMEM((PEERS * CAP, 512), BF16),
            pltpu.VMEM((512, PEERS * CAP), BF16),
        ]
        + [pltpu.VMEM((PEERS, CAP, 512), BF16)] * 4
        + [dma((PEERS,))] * 4
        + [pltpu.SemaphoreType.REGULAR] * 2,
        compiler_params=pltpu.CompilerParams(
            collective_id=0, has_side_effects=True, vmem_limit_bytes=62 * 1024 * 1024
        ),
        name="block_pair",
    )(features, routes, *tables, *gains, *weights, *shards)


def local(
    features,
    routes,
    qkv_regular,
    proj_regular,
    table_regular,
    gain_regular,
    mlp_up,
    mlp_down,
    gain_mlp,
    qkv_shifted,
    proj_shifted,
    table_shifted,
    gain_shifted,
    expert_in,
    expert_out,
    gain_expert,
):
    gains = (gain_regular, gain_mlp, gain_shifted, gain_expert)
    return block_pair(
        features,
        routes.reshape(32, 16).T.reshape(16, 1, 32),
        (table_regular.T, table_shifted.T),
        [g.reshape(1, 512) for g in gains],
        (qkv_regular, proj_regular, mlp_up, mlp_down, qkv_shifted, proj_shifted),
        (expert_in, expert_out),
    )


def solution(mesh):
    return jax.shard_map(
        local,
        mesh=mesh,
        in_specs=(
            P("expert", None, "band", None),
            P("expert", "band", None, None, None),
        )
        + (P(),) * 11
        + (P("expert", None, "band"), P("expert", "band", None), P()),
        out_specs=P("expert", None, "band", None),
        check_vma=False,
    )
```

```python
import functools
import jax
import jax.numpy as jnp
from jax import lax
from jax.experimental import pallas as pl
from jax.experimental.pallas import tpu as pltpu
from jax.sharding import PartitionSpec as P

MESH = pl.DeviceIdType.MESH
F32 = jnp.float32
BF16 = jnp.bfloat16
WIN = 8
HALF = WIN // 2
CELLS = WIN * WIN
LANES = 128
LOG2E = 1.4426950408889634
ROOT_HALF = 0.7071067811865476


def dot(a, b):
    return jnp.dot(a, b, preferred_element_type=F32)


def dot_over(a, b, dim_a, dim_b):
    return lax.dot_general(a, b, (((dim_a,), (dim_b,)), ((), ())), preferred_element_type=F32)


def gelu(v):
    return (0.5 * v) * (1.0 + lax.erf(v * ROOT_HALF))


def layer_norm(values, gain_vec):
    centre = jnp.mean(values, axis=-1, keepdims=True)
    offsets = values - centre
    spread = jnp.mean(offsets * offsets, axis=-1, keepdims=True)
    return offsets * lax.rsqrt(spread + 1e-05) * gain_vec


def turn(tiles):
    return pltpu.roll(tiles, HALF, axis=tiles.ndim - 2)


def cell_is_low(shape):
    return lax.broadcasted_iota(jnp.int32, shape, len(shape) - 2) < HALF


def window_bias(table_ref, pad_ref, bias_ref):
    span = 2 * WIN - 1
    pitch = 2 * WIN
    width = pitch * pitch
    pad_ref[...] = jnp.zeros(pad_ref.shape, F32)
    pad_ref[:, : span * span] = table_ref[...] * LOG2E
    packed = pad_ref[...]
    line = lax.broadcasted_iota(jnp.int32, packed.shape, 1) // pitch
    flat = packed
    for a in range(1, span):
        flat = jnp.where(line == a, pltpu.roll(packed, a, axis=1), flat)
    even = lax.broadcasted_iota(jnp.int32, (WIN, LANES), 1) % pitch < WIN
    for group in range(4):
        for pair in range(2):
            head = group * 4 + pair * 2
            row_even = jnp.broadcast_to(flat[head : head + 1, :], (WIN, width))
            row_odd = jnp.broadcast_to(flat[head + 1 : head + 2, :], (WIN, width))
            for key_row in range(WIN):
                back = (WIN - 1 - key_row) * pitch + WIN - 1
                a = pltpu.roll(row_even, (width - back) % width, axis=1, stride=1, stride_axis=0)
                b = pltpu.roll(
                    row_odd, (width - back + WIN) % width, axis=1, stride=1, stride_axis=0
                )
                bias_ref[
                    group,
                    key_row * WIN : (key_row + 1) * WIN,
                    pair * LANES : (pair + 1) * LANES,
                ] = jnp.where(even, a[:, :LANES], b[:, :LANES])


def spread_heads(q):
    head = lax.broadcasted_iota(jnp.int32, (1, 1, LANES), 2) // 32
    tiles = q.astype(F32).reshape(WIN, WIN, LANES)
    pieces = []
    for pair in range(2):
        both = [jnp.where(head == pair * 2 + k, tiles, 0.0)[:, None] for k in range(2)]
        pieces.append(jnp.concatenate(both, axis=1).reshape(2 * CELLS, LANES))
    return jnp.concatenate(pieces, axis=0).astype(BF16)


def gather_heads(o):
    head = lax.broadcasted_iota(jnp.int32, (1, 1, LANES), 2) // 32
    parts = o.reshape(2, WIN, 2, WIN, LANES)
    low = jnp.where(head == 0, parts[0, :, 0], parts[0, :, 1])
    high = jnp.where(head == 2, parts[1, :, 0], parts[1, :, 1])
    return jnp.where(head < 2, low, high).reshape(CELLS, LANES)


def soften(s):
    e = jnp.exp2(s - jnp.max(s, axis=0, keepdims=True))
    return (e * (1.0 / jnp.sum(e, axis=0, keepdims=True))).astype(BF16)


AWAY = sorted(
    ((z, x) for z in range(4) for x in range(4)),
    key=lambda d: (min(d[0], 4 - d[0]) + min(d[1], 4 - d[1]), d),
)
PEERS = 32
CAP = 32
GROUPS = 4
PER_GROUP = PEERS // GROUPS
ROWS = PER_GROUP * CAP


def token_routes(routes_ref):
    grid = routes_ref[...].reshape(16, 32).astype(F32).astype(BF16)
    token = lax.broadcasted_iota(jnp.int32, (32, 512), 1)
    row = ((token // 64) % 4 * 8 + 4 + (token // 8) % 8) % 32
    at_row = jnp.where(lax.broadcasted_iota(jnp.int32, (32, 512), 0) == row, 1.0, 0.0)
    token = lax.broadcasted_iota(jnp.int32, (16, 512), 1)
    cell = token % 8
    column = jnp.where(token < 256, HALF + cell, (cell + 12) % 16)
    at_column = lax.broadcasted_iota(jnp.int32, (16, 512), 0) == column
    picked = jnp.where(at_column, dot(grid, at_row.astype(BF16)), 0.0)
    return jnp.sum(picked, axis=0, keepdims=True).astype(jnp.int32)


def kernel(
    x_ref,
    routes_ref,
    table_r_ref,
    table_s_ref,
    gain_r_ref,
    gain_m_ref,
    gain_s_ref,
    gain_e_ref,
    qkv_r_hbm,
    proj_r_hbm,
    up_hbm,
    down_hbm,
    qkv_s_hbm,
    proj_s_hbm,
    own_in,
    own_out,
    enc_ref,
    qkv_r,
    proj_r,
    up,
    down,
    qkv_s,
    proj_s,
    load_sem,
    pad,
    bias_r,
    bias_s,
    tiles,
    qkv_buf,
    edge_buf,
    heads,
    third_buf,
    to_left,
    to_right,
    from_left,
    from_right,
    send_sem,
    recv_sem,
    shard_send,
    shard_recv,
    w_in,
    w_out,
    place,
    take,
    outgoing,
    arrived,
    result,
    returned,
    go_send,
    go_recv,
    back_send,
    back_recv,
    heads_sem,
    ready_sem,
):
    band = lax.axis_index("band")
    bands = lax.axis_size("band")
    right = lax.rem(band + 1, bands)
    left = lax.rem(band + bands - 1, bands)
    me = lax.axis_index("expert")
    my_z, my_x, my_core = me // 8, (me // 2) % 4, me % 2
    hosted = band // 2
    mirror = bands - 1 - band
    beside = hosted * 4 + 1 - band
    served = jnp.where(my_core == 0, band, mirror)
    keeper = my_core == hosted
    sibling = me + 1 - 2 * my_core

    def chip(n, sign):
        z, x = AWAY[n // 2]
        return ((my_z + 4 + sign * z) % 4 * 4 + (my_x + 4 + sign * x) % 4) * 2

    barrier = pltpu.get_barrier_semaphore()

    def tell(sem, expert, level):
        to = {"band": level, "expert": expert}
        pl.semaphore_signal(sem, inc=1, device_id=to, device_id_type=MESH)

    head = my_z * 8
    is_head = me == head
    other_heads = [
        ((head + 8 * n) % PEERS, level) for level in (band, mirror) for n in range(4)
    ][1:]
    tell(barrier, me, left)
    tell(barrier, me, right)
    tell(barrier, sibling, band)

    @pl.when(is_head)
    def _():
        for other in other_heads:
            tell(barrier, *other)

    @pl.when(jnp.logical_not(is_head))
    def _():
        tell(barrier, head, band)

    loads = [
        pltpu.make_async_copy(src, dst, load_sem.at[n])
        for n, (src, dst) in enumerate(
            (
                (qkv_r_hbm, qkv_r),
                (proj_r_hbm, proj_r),
                (up_hbm, up),
                (down_hbm, down),
                (qkv_s_hbm, qkv_s),
                (proj_s_hbm, proj_s),
                (own_in.at[0], w_in.at[0]),
                (own_out.at[0], w_out.at[0]),
            )
        )
    ]
    for load in loads[:6]:
        load.start()

    def remote(src, dst, send_sem, recv_sem, to):
        return pltpu.make_async_remote_copy(
            src_ref=src,
            dst_ref=dst,
            send_sem=send_sem,
            recv_sem=recv_sem,
            device_id=to,
            device_id_type=MESH,
        )

    shelves = (w_in, w_out)
    own = (own_in.at[0], own_out.at[0])

    def shard(src, slot, array, n, expert, level):
        return remote(
            src,
            shelves[array].at[slot],
            shard_send.at[n],
            shard_recv.at[slot * 2 + array],
            {"band": level, "expert": expert},
        )

    def leave(array):
        slot = jnp.where(keeper, 2, 1)
        return shard(own[array], slot, array, array, me, jnp.where(keeper, beside, mirror))

    def forward(array):
        return shard(shelves[array].at[1], 3, array, 2 + array, me, beside)

    def share(slot, array):
        src = own[array] if slot == 0 else shelves[array].at[slot]
        return shard(src, slot, array, 4 + slot * 2 + array, sibling, band)

    def came(slot, array):
        share(slot, array).wait_recv()

    def go(n):
        to = {"band": mirror if n % 2 else band, "expert": chip(n, 1) + n % 2}
        slot = n // 2 * 2 + my_core
        return remote(outgoing.at[n], arrived.at[slot], go_send.at[n], go_recv.at[slot], to)

    def back(n):
        to = {"band": served, "expert": chip(n, -1) + n % 2}
        slot = n // 2 * 2 + my_core
        return remote(result.at[n], returned.at[slot], back_send.at[n], back_recv.at[slot], to)

    def landed(buffer, sem, n):
        to = {"band": band, "expert": sibling}
        remote(buffer.at[n], buffer.at[n], shard_send.at[0], sem.at[n], to).wait_recv()

    def each(places, act):
        for n in places:
            if n:
                act(n)
            else:
                pl.when(my_core == 1)(functools.partial(act, n))

    routes = token_routes(routes_ref)
    code = (((routes >> 3) - my_z) & 3) * 4 + (((routes >> 1) - my_x) & 3)
    spot = jnp.zeros_like(routes)
    for n, (z, x) in enumerate(AWAY):
        spot = jnp.where(code == z * 4 + x, n, spot)
    spot = spot * 2 + ((routes - hosted) & 1)
    chosen = lax.broadcasted_iota(jnp.int32, (PEERS, 512), 0) == spot
    onehot = jnp.where(chosen, 1.0, 0.0)
    before = lax.broadcasted_iota(jnp.int32, (512, 512), 0) < lax.broadcasted_iota(
        jnp.int32, (512, 512), 1
    )
    ahead = dot(onehot.astype(BF16), jnp.where(before, 1.0, 0.0).astype(BF16))
    slot = spot.astype(F32) * CAP + jnp.sum(onehot * ahead, axis=0, keepdims=True)
    for g in range(GROUPS):
        rows = (lax.broadcasted_iota(jnp.int32, (ROWS, 512), 0) + g * ROWS).astype(F32)
        place[g * ROWS : (g + 1) * ROWS] = jnp.where(rows == slot, 1.0, 0.0).astype(BF16)

    @pl.when(is_head)
    def _():
        pl.semaphore_wait(barrier, 3 + 7 + 7)
        for other in other_heads:
            tell(heads_sem, *other)

    @pl.when(jnp.logical_not(is_head))
    def _():
        pl.semaphore_wait(barrier, 3)

    for array in range(2):
        leave(array).start()

    @pl.when(keeper)
    def _():
        for array in range(2):
            share(0, array).start()
        for load in loads[6:]:
            load.start()

    scale = LOG2E * 32**-0.5
    window_bias(table_r_ref, pad, bias_r)
    window_bias(table_s_ref, pad, bias_s)


    @pl.when(is_head)
    def _():
        pl.semaphore_wait(heads_sem, 7)
        for n in range(1, 8):
            tell(ready_sem, head + n, band)

    for load in loads[:4]:
        load.wait()

    def sends(part):
        return [
            remote(
                to_left.at[part],
                from_right.at[part],
                send_sem.at[0, part],
                recv_sem.at[0, part],
                {"band": left},
            ),
            remote(
                to_right.at[part],
                from_left.at[part],
                send_sem.at[1, part],
                recv_sem.at[1, part],
                {"band": right},
            ),
        ]

    low_cell = cell_is_low((1, WIN, 512))

    def first_part(part, carry):
        x3 = x_ref[0, pl.ds(part * 16, 16)].astype(F32)
        xf = jnp.concatenate(
            [
                x3[r * 8 : r * 8 + 8, c * 8 : c * 8 + 8, :].reshape(CELLS, 512)
                for r in range(2)
                for c in range(2)
            ],
            axis=0,
        )
        qkv_buf[...] = dot(xf.astype(BF16), qkv_r[...]).astype(BF16)
        for w in range(4):
            rows = slice(w * CELLS, (w + 1) * CELLS)
            for g in range(4):
                q = qkv_buf[rows, g * 128 : g * 128 + 128]
                k = qkv_buf[rows, 512 + g * 128 : 640 + g * 128]
                v = qkv_buf[rows, 1024 + g * 128 : 1152 + g * 128]
                s = dot_over(k, spread_heads(q), 1, 1) * scale + bias_r[g]
                heads[rows, g * 128 : g * 128 + 128] = gather_heads(
                    dot_over(soften(s), v, 0, 0)
                ).astype(BF16)
        first = (xf + layer_norm(dot(heads[...], proj_r[...]), gain_r_ref[...])).astype(BF16)
        total = jnp.zeros((256, 512), F32)
        for f in range(4):
            hidden = gelu(dot(first, up[:, f * 512 : f * 512 + 512])).astype(BF16)
            total = total + dot(hidden, down[f * 512 : f * 512 + 512, :])
        second = (first.astype(F32) + layer_norm(total, gain_m_ref[...])).astype(BF16).astype(F32)
        for r in range(2):
            rows = pl.ds(part * 16 + r * 8, 8)
            w0 = second[r * 128 : r * 128 + 64].reshape(WIN, WIN, 512)
            w1 = second[r * 128 + 64 : r * 128 + 128].reshape(WIN, WIN, 512)
            tiles[rows, 1] = w0
            tiles[rows, 2] = w1
            to_left[part, r * 32 : r * 32 + 32] = (
                jnp.where(low_cell, w0[:HALF], turn(w0[HALF:])).reshape(32, 512).astype(BF16)
            )
            to_right[part, r * 32 : r * 32 + 32] = (
                jnp.where(low_cell, turn(w1[HALF:]), w1[:HALF]).reshape(32, 512).astype(BF16)
            )
        for send in sends(part):
            send.start()

        return carry

    lax.fori_loop(0, 2, first_part, 0)

    @pl.when(keeper)
    def _():
        came(1, 0)
        forward(0).start()
        share(1, 0).start()

    def shifted(column):
        pieces = []
        for w in range(4):
            for start in (w * 8 + 4, (w * 8 + 8) % 32):
                a = tiles[start : start + 4, column]
                b = tiles[start : start + 4, column + 1]
                pieces.append(turn(jnp.where(low_cell, b, a)))
        return jnp.concatenate(pieces, axis=0)

    def finish(x, first_row):
        third = x + layer_norm(dot(heads[...], proj_s[...]), gain_s_ref[...])
        third_buf[first_row : first_row + 256, :] = third.astype(BF16)

    key = lax.broadcasted_iota(jnp.int32, (CELLS, 256), 0)
    lane = lax.broadcasted_iota(jnp.int32, (CELLS, 256), 1)
    low_j = lane % 8 < HALF
    row_apart = (key // 8 < HALF) != ((lane // 16) % 8 < HALF)
    col_apart = ((key % 8 < HALF) != low_j) & (
        (low_j & (band == bands - 1)) | (jnp.logical_not(low_j) & (band == 0))
    )
    mask_row = jnp.where(row_apart, -100.0 * LOG2E, 0.0)
    mask_col = jnp.where(col_apart, -100.0 * LOG2E, 0.0)
    mask_both = jnp.where(row_apart | col_apart, -100.0 * LOG2E, 0.0)

    for load in loads[4:6]:
        load.wait()
    mid = shifted(1).reshape(256, 512)
    qkv_buf[...] = dot(mid.astype(BF16), qkv_s[...]).astype(BF16)
    for w in range(4):
        rows = slice(w * CELLS, (w + 1) * CELLS)
        for g in range(4):
            q = qkv_buf[rows, g * 128 : g * 128 + 128]
            k = qkv_buf[rows, 512 + g * 128 : 640 + g * 128]
            v = qkv_buf[rows, 1024 + g * 128 : 1152 + g * 128]
            s = dot_over(k, spread_heads(q), 1, 1) * scale + bias_s[g]
            if w == 3:
                s = s + mask_row
            heads[rows, g * 128 : g * 128 + 128] = gather_heads(
                dot_over(soften(s), v, 0, 0)
            ).astype(BF16)
    finish(mid, 0)

    @pl.when(keeper)
    def _():
        came(1, 1)
        forward(1).start()
        share(1, 1).start()
        for array in range(2):
            came(2, array)
            share(2, array).start()

    for part in range(2):
        for send in sends(part):
            send.wait()
        for r in range(2):
            top = part * 16 + r * 8
            h = from_left[part, r * 32 : r * 32 + 32].astype(F32).reshape(HALF, WIN, 512)
            tiles[top : top + 4, 0] = h
            tiles[top + 4 : top + 8, 0] = turn(h)
            h = from_right[part, r * 32 : r * 32 + 32].astype(F32).reshape(HALF, WIN, 512)
            tiles[top : top + 4, 3] = h
            tiles[top + 4 : top + 8, 3] = turn(h)
    edge0 = shifted(0)
    edge2 = shifted(2)
    edge = jnp.where(low_cell, edge2, edge0).reshape(256, 512)
    qkv_buf[:, :512] = dot(edge.astype(BF16), qkv_s[:, :512]).astype(BF16)
    qkv_buf[:, 512:] = dot(edge0.reshape(256, 512).astype(BF16), qkv_s[:, 512:]).astype(BF16)
    edge_buf[...] = dot(edge2.reshape(256, 512).astype(BF16), qkv_s[:, 512:]).astype(BF16)
    for w in range(4):
        rows = slice(w * CELLS, (w + 1) * CELLS)
        for g in range(4):
            q = spread_heads(qkv_buf[rows, g * 128 : g * 128 + 128])
            k0 = qkv_buf[rows, 512 + g * 128 : 640 + g * 128]
            v0 = qkv_buf[rows, 1024 + g * 128 : 1152 + g * 128]
            k2 = edge_buf[rows, g * 128 : g * 128 + 128]
            v2 = edge_buf[rows, 512 + g * 128 : 640 + g * 128]
            s = jnp.where(low_j, dot_over(k2, q, 1, 1), dot_over(k0, q, 1, 1))
            s = s * scale + bias_s[g] + (mask_both if w == 3 else mask_col)
            o = dot_over(soften(s), jnp.concatenate([v2, v0], axis=1), 0, 0)
            o2 = gather_heads(o[:, :LANES]).reshape(WIN, WIN, LANES)
            o0 = gather_heads(o[:, LANES:]).reshape(WIN, WIN, LANES)
            heads[rows, g * 128 : g * 128 + 128] = (
                jnp.where(cell_is_low((1, WIN, LANES)), o2, o0).reshape(CELLS, LANES).astype(BF16)
            )
    finish(edge, 256)

    @pl.when(jnp.logical_not(is_head))
    def _():
        pl.semaphore_wait(ready_sem, 1)

    groups = range(GROUPS)

    def places(g):
        return range(g * PER_GROUP, (g + 1) * PER_GROUP)[::-1]

    def keep(block, buffer):
        @pl.when(my_core == 0)
        def _():
            buffer[0] = block

    third = third_buf[...]
    for g in groups:
        block = dot(place[g * ROWS : (g + 1) * ROWS], third).astype(BF16)
        block = block.reshape(PER_GROUP, CAP, 512)
        outgoing[g * PER_GROUP : (g + 1) * PER_GROUP] = block
        if g == 0:
            keep(block[0], arrived)
        each(places(g), lambda n: go(n).start())

    slot_column = jnp.transpose(jnp.broadcast_to(slot, (LANES, 512)))
    lane = lax.broadcasted_iota(jnp.int32, (512, LANES), 1).astype(F32)
    for n in range(PEERS * CAP // LANES):
        take[:, n * LANES : (n + 1) * LANES] = jnp.where(
            slot_column == lane + n * LANES, 1.0, 0.0
        ).astype(BF16)

    @pl.when(keeper)
    def _():
        came(3, 0)
        share(3, 0).start()
        for load in loads[6:]:
            load.wait()

    @pl.when(jnp.logical_not(keeper))
    def _():
        for slot in range(3):
            for array in range(2):
                came(slot, array)
        came(3, 0)

    def layer(rows, n):
        hidden = gelu(dot(rows, w_in[n])).astype(BF16)
        return dot(hidden, w_out[n])

    for g in groups:
        each(places(g), lambda n: landed(arrived, go_recv, n))
        rows = arrived[g * PER_GROUP : (g + 1) * PER_GROUP].reshape(ROWS, 512)
        total = layer(rows, 0) + layer(rows, 1) + layer(rows, 2)
        if g == groups[0]:
            came(3, 1)

            @pl.when(keeper)
            def _():
                share(3, 1).start()

        block = (total + layer(rows, 3)).astype(BF16).reshape(PER_GROUP, CAP, 512)
        result[g * PER_GROUP : (g + 1) * PER_GROUP] = block
        if g == 0:
            keep(block[0], returned)
        each(places(g), lambda n: back(n).start())

    for array in range(2):
        leave(array).wait_send()

    @pl.when(keeper)
    def _():
        for array in range(2):
            forward(array).wait_send()
            for slot in range(4):
                share(slot, array).wait_send()

    rows = jnp.zeros((512, 512), F32)
    for g in groups:
        each(places(g), lambda n: landed(returned, back_recv, n))
        block = returned[g * PER_GROUP : (g + 1) * PER_GROUP].reshape(ROWS, 512)
        rows = rows + dot(take[:, g * ROWS : (g + 1) * ROWS], block)
    encoded = third_buf[...].astype(F32) + layer_norm(rows, gain_e_ref[...])
    for w in range(4):
        mid = encoded[w * CELLS : (w + 1) * CELLS].reshape(WIN, WIN, 512)
        edge = encoded[256 + w * CELLS : 256 + (w + 1) * CELLS].reshape(WIN, WIN, 512)
        w0 = turn(jnp.where(low_cell, mid, edge))
        w1 = turn(jnp.where(low_cell, edge, mid))
        block = jnp.concatenate([w0, w1], axis=1).astype(BF16)
        for half in range(2):
            top = (w * 8 + 4 + half * 4) % 32
            enc_ref[0, top : top + 4] = block[half * 4 : half * 4 + 4]
    for g in groups:
        each(places(g), lambda n: go(n).wait_send())
        each(places(g), lambda n: back(n).wait_send())


def block_pair(features, routes, tables, gains, weights, shards):
    vmem = pl.BlockSpec(memory_space=pltpu.VMEM)
    hbm = pl.BlockSpec(memory_space=pl.ANY)
    dma = pltpu.SemaphoreType.DMA
    return pl.pallas_call(
        kernel,
        out_shape=jax.ShapeDtypeStruct((1, 32, 16, 512), BF16),
        in_specs=[vmem] * 8 + [hbm] * 8,
        out_specs=vmem,
        scratch_shapes=[pltpu.VMEM(w.shape, BF16) for w in weights]
        + [
            dma((8,)),
            pltpu.VMEM((16, 256), F32),
            pltpu.VMEM((4, CELLS, 256), F32),
            pltpu.VMEM((4, CELLS, 256), F32),
            pltpu.VMEM((32, 4, WIN, 512), F32),
            pltpu.VMEM((256, 1536), BF16),
            pltpu.VMEM((256, 1024), BF16),
            pltpu.VMEM((256, 512), BF16),
            pltpu.VMEM((512, 512), BF16),
        ]
        + [pltpu.VMEM((2, 64, 512), BF16)] * 4
        + [dma((2, 2)), dma((2, 2)), dma((12,)), dma((8,))]
        + [
            pltpu.VMEM((4, 512, 512), BF16),
            pltpu.VMEM((4, 512, 512), BF16),
            pltpu.VMEM((PEERS * CAP, 512), BF16),
            pltpu.VMEM((512, PEERS * CAP), BF16),
        ]
        + [pltpu.VMEM((PEERS, CAP, 512), BF16)] * 4
        + [dma((PEERS,))] * 4
        + [pltpu.SemaphoreType.REGULAR] * 2,
        compiler_params=pltpu.CompilerParams(
            collective_id=0, has_side_effects=True, vmem_limit_bytes=62 * 1024 * 1024
        ),
        name="block_pair",
    )(features, routes, *tables, *gains, *weights, *shards)


def local(
    features,
    routes,
    qkv_regular,
    proj_regular,
    table_regular,
    gain_regular,
    mlp_up,
    mlp_down,
    gain_mlp,
    qkv_shifted,
    proj_shifted,
    table_shifted,
    gain_shifted,
    expert_in,
    expert_out,
    gain_expert,
):
    gains = (gain_regular, gain_mlp, gain_shifted, gain_expert)
    return block_pair(
        features,
        routes.reshape(32, 16).T.reshape(16, 1, 32),
        (table_regular.T, table_shifted.T),
        [g.reshape(1, 512) for g in gains],
        (qkv_regular, proj_regular, mlp_up, mlp_down, qkv_shifted, proj_shifted),
        (expert_in, expert_out),
    )


def solution(mesh):
    return jax.shard_map(
        local,
        mesh=mesh,
        in_specs=(
            P("expert", None, "band", None),
            P("expert", "band", None, None, None),
        )
        + (P(),) * 11
        + (P("expert", None, "band"), P("expert", "band", None), P()),
        out_specs=P("expert", None, "band", None),
        check_vma=False,
    )
```

```python
import functools
import jax
import jax.numpy as jnp
from jax import lax
from jax.experimental import pallas as pl
from jax.experimental.pallas import tpu as pltpu
from jax.sharding import PartitionSpec as P

MESH = pl.DeviceIdType.MESH
F32 = jnp.float32
BF16 = jnp.bfloat16
WIN = 8
HALF = WIN // 2
CELLS = WIN * WIN
LANES = 128
LOG2E = 1.4426950408889634
ROOT_HALF = 0.7071067811865476


def dot(a, b):
    return jnp.dot(a, b, preferred_element_type=F32)


def dot_over(a, b, dim_a, dim_b):
    return lax.dot_general(a, b, (((dim_a,), (dim_b,)), ((), ())), preferred_element_type=F32)


def gelu(v):
    return (0.5 * v) * (1.0 + lax.erf(v * ROOT_HALF))


def layer_norm(values, gain_vec):
    centre = jnp.mean(values, axis=-1, keepdims=True)
    offsets = values - centre
    spread = jnp.mean(offsets * offsets, axis=-1, keepdims=True)
    return offsets * lax.rsqrt(spread + 1e-05) * gain_vec


def turn(tiles):
    return pltpu.roll(tiles, HALF, axis=tiles.ndim - 2)


def cell_is_low(shape):
    return lax.broadcasted_iota(jnp.int32, shape, len(shape) - 2) < HALF


def window_bias(table_ref, pad_ref, bias_ref):
    span = 2 * WIN - 1
    pitch = 2 * WIN
    width = pitch * pitch
    pad_ref[...] = jnp.zeros(pad_ref.shape, F32)
    pad_ref[:, : span * span] = table_ref[...] * LOG2E
    packed = pad_ref[...]
    line = lax.broadcasted_iota(jnp.int32, packed.shape, 1) // pitch
    flat = packed
    for a in range(1, span):
        flat = jnp.where(line == a, pltpu.roll(packed, a, axis=1), flat)
    even = lax.broadcasted_iota(jnp.int32, (WIN, LANES), 1) % pitch < WIN
    for group in range(4):
        for pair in range(2):
            head = group * 4 + pair * 2
            row_even = jnp.broadcast_to(flat[head : head + 1, :], (WIN, width))
            row_odd = jnp.broadcast_to(flat[head + 1 : head + 2, :], (WIN, width))
            for key_row in range(WIN):
                back = (WIN - 1 - key_row) * pitch + WIN - 1
                a = pltpu.roll(row_even, (width - back) % width, axis=1, stride=1, stride_axis=0)
                b = pltpu.roll(
                    row_odd, (width - back + WIN) % width, axis=1, stride=1, stride_axis=0
                )
                bias_ref[
                    group,
                    key_row * WIN : (key_row + 1) * WIN,
                    pair * LANES : (pair + 1) * LANES,
                ] = jnp.where(even, a[:, :LANES], b[:, :LANES])


def spread_heads(q):
    head = lax.broadcasted_iota(jnp.int32, (1, 1, LANES), 2) // 32
    tiles = q.astype(F32).reshape(WIN, WIN, LANES)
    pieces = []
    for pair in range(2):
        both = [jnp.where(head == pair * 2 + k, tiles, 0.0)[:, None] for k in range(2)]
        pieces.append(jnp.concatenate(both, axis=1).reshape(2 * CELLS, LANES))
    return jnp.concatenate(pieces, axis=0).astype(BF16)


def gather_heads(o):
    head = lax.broadcasted_iota(jnp.int32, (1, 1, LANES), 2) // 32
    parts = o.reshape(2, WIN, 2, WIN, LANES)
    low = jnp.where(head == 0, parts[0, :, 0], parts[0, :, 1])
    high = jnp.where(head == 2, parts[1, :, 0], parts[1, :, 1])
    return jnp.where(head < 2, low, high).reshape(CELLS, LANES)


def soften(s):
    e = jnp.exp2(s - jnp.max(s, axis=0, keepdims=True))
    return (e * (1.0 / jnp.sum(e, axis=0, keepdims=True))).astype(BF16)


AWAY = sorted(
    ((z, x) for z in range(4) for x in range(4)),
    key=lambda d: (min(d[0], 4 - d[0]) + min(d[1], 4 - d[1]), d),
)
PEERS = 32
CAP = 32
GROUPS = 4
PER_GROUP = PEERS // GROUPS
ROWS = PER_GROUP * CAP


def token_routes(routes_ref):
    grid = routes_ref[...].reshape(16, 32).astype(F32).astype(BF16)
    token = lax.broadcasted_iota(jnp.int32, (32, 512), 1)
    row = ((token // 64) % 4 * 8 + 4 + (token // 8) % 8) % 32
    at_row = jnp.where(lax.broadcasted_iota(jnp.int32, (32, 512), 0) == row, 1.0, 0.0)
    token = lax.broadcasted_iota(jnp.int32, (16, 512), 1)
    cell = token % 8
    column = jnp.where(token < 256, HALF + cell, (cell + 12) % 16)
    at_column = lax.broadcasted_iota(jnp.int32, (16, 512), 0) == column
    picked = jnp.where(at_column, dot(grid, at_row.astype(BF16)), 0.0)
    return jnp.sum(picked, axis=0, keepdims=True).astype(jnp.int32)


def kernel(
    x_ref,
    routes_ref,
    table_r_ref,
    table_s_ref,
    gain_r_ref,
    gain_m_ref,
    gain_s_ref,
    gain_e_ref,
    qkv_r_hbm,
    proj_r_hbm,
    up_hbm,
    down_hbm,
    qkv_s_hbm,
    proj_s_hbm,
    own_in,
    own_out,
    enc_ref,
    qkv_r,
    proj_r,
    up,
    down,
    qkv_s,
    proj_s,
    load_sem,
    pad,
    bias_r,
    bias_s,
    tiles,
    qkv_buf,
    edge_buf,
    heads,
    third_buf,
    to_left,
    to_right,
    from_left,
    from_right,
    send_sem,
    recv_sem,
    shard_send,
    shard_recv,
    w_in,
    w_out,
    place,
    take,
    outgoing,
    arrived,
    result,
    returned,
    go_send,
    go_recv,
    back_send,
    back_recv,
    heads_sem,
    ready_sem,
):
    band = lax.axis_index("band")
    bands = lax.axis_size("band")
    right = lax.rem(band + 1, bands)
    left = lax.rem(band + bands - 1, bands)
    me = lax.axis_index("expert")
    my_z, my_x, my_core = me // 8, (me // 2) % 4, me % 2
    hosted = band // 2
    mirror = bands - 1 - band
    beside = hosted * 4 + 1 - band
    served = jnp.where(my_core == 0, band, mirror)
    keeper = my_core == hosted
    sibling = me + 1 - 2 * my_core

    def chip(n, sign):
        z, x = AWAY[n // 2]
        return ((my_z + 4 + sign * z) % 4 * 4 + (my_x + 4 + sign * x) % 4) * 2

    barrier = pltpu.get_barrier_semaphore()

    def tell(sem, expert, level):
        to = {"band": level, "expert": expert}
        pl.semaphore_signal(sem, inc=1, device_id=to, device_id_type=MESH)

    head = my_z * 8
    is_head = me == head
    other_heads = [
        ((head + 8 * n) % PEERS, level) for level in (band, mirror) for n in range(4)
    ][1:]
    tell(barrier, me, left)
    tell(barrier, me, right)
    tell(barrier, sibling, band)

    @pl.when(is_head)
    def _():
        for other in other_heads:
            tell(barrier, *other)

    @pl.when(jnp.logical_not(is_head))
    def _():
        tell(barrier, head, band)

    loads = [
        pltpu.make_async_copy(src, dst, load_sem.at[n])
        for n, (src, dst) in enumerate(
            (
                (qkv_r_hbm, qkv_r),
                (proj_r_hbm, proj_r),
                (up_hbm, up),
                (down_hbm, down),
                (qkv_s_hbm, qkv_s),
                (proj_s_hbm, proj_s),
                (own_in.at[0], w_in.at[0]),
                (own_out.at[0], w_out.at[0]),
            )
        )
    ]
    for load in loads[:6]:
        load.start()

    def remote(src, dst, send_sem, recv_sem, to):
        return pltpu.make_async_remote_copy(
            src_ref=src,
            dst_ref=dst,
            send_sem=send_sem,
            recv_sem=recv_sem,
            device_id=to,
            device_id_type=MESH,
        )

    shelves = (w_in, w_out)
    own = (own_in.at[0], own_out.at[0])

    def shard(src, slot, array, n, expert, level):
        return remote(
            src,
            shelves[array].at[slot],
            shard_send.at[n],
            shard_recv.at[slot * 2 + array],
            {"band": level, "expert": expert},
        )

    def leave(array):
        slot = jnp.where(keeper, 2, 1)
        return shard(own[array], slot, array, array, me, jnp.where(keeper, beside, mirror))

    def forward(array):
        return shard(shelves[array].at[1], 3, array, 2 + array, me, beside)

    def share(slot, array):
        src = own[array] if slot == 0 else shelves[array].at[slot]
        return shard(src, slot, array, 4 + slot * 2 + array, sibling, band)

    def came(slot, array):
        share(slot, array).wait_recv()

    def go(n):
        to = {"band": mirror if n % 2 else band, "expert": chip(n, 1) + n % 2}
        slot = n // 2 * 2 + my_core
        return remote(outgoing.at[n], arrived.at[slot], go_send.at[n], go_recv.at[slot], to)

    def back(n):
        to = {"band": served, "expert": chip(n, -1) + n % 2}
        slot = n // 2 * 2 + my_core
        return remote(result.at[n], returned.at[slot], back_send.at[n], back_recv.at[slot], to)

    def landed(buffer, sem, n):
        to = {"band": band, "expert": sibling}
        remote(buffer.at[n], buffer.at[n], shard_send.at[0], sem.at[n], to).wait_recv()

    def each(places, act):
        for n in places:
            if n:
                act(n)
            else:
                pl.when(my_core == 1)(functools.partial(act, n))

    routes = token_routes(routes_ref)
    code = (((routes >> 3) - my_z) & 3) * 4 + (((routes >> 1) - my_x) & 3)
    spot = jnp.zeros_like(routes)
    for n, (z, x) in enumerate(AWAY):
        spot = jnp.where(code == z * 4 + x, n, spot)
    spot = spot * 2 + ((routes - hosted) & 1)
    chosen = lax.broadcasted_iota(jnp.int32, (PEERS, 512), 0) == spot
    onehot = jnp.where(chosen, 1.0, 0.0)
    before = lax.broadcasted_iota(jnp.int32, (512, 512), 0) < lax.broadcasted_iota(
        jnp.int32, (512, 512), 1
    )
    ahead = dot(onehot.astype(BF16), jnp.where(before, 1.0, 0.0).astype(BF16))
    slot = spot.astype(F32) * CAP + jnp.sum(onehot * ahead, axis=0, keepdims=True)
    for g in range(GROUPS):
        rows = (lax.broadcasted_iota(jnp.int32, (ROWS, 512), 0) + g * ROWS).astype(F32)
        place[g * ROWS : (g + 1) * ROWS] = jnp.where(rows == slot, 1.0, 0.0).astype(BF16)

    window_bias(table_r_ref, pad, bias_r)
    window_bias(table_s_ref, pad, bias_s)

    @pl.when(is_head)
    def _():
        pl.semaphore_wait(barrier, 3 + 7 + 7)
        for other in other_heads:
            tell(heads_sem, *other)

    @pl.when(jnp.logical_not(is_head))
    def _():
        pl.semaphore_wait(barrier, 3)

    for array in range(2):
        leave(array).start()

    @pl.when(keeper)
    def _():
        for array in range(2):
            share(0, array).start()
        for load in loads[6:]:
            load.start()

    scale = LOG2E * 32**-0.5


    @pl.when(is_head)
    def _():
        pl.semaphore_wait(heads_sem, 7)
        for n in range(1, 8):
            tell(ready_sem, head + n, band)

    for load in loads[:4]:
        load.wait()

    def sends(part):
        return [
            remote(
                to_left.at[part],
                from_right.at[part],
                send_sem.at[0, part],
                recv_sem.at[0, part],
                {"band": left},
            ),
            remote(
                to_right.at[part],
                from_left.at[part],
                send_sem.at[1, part],
                recv_sem.at[1, part],
                {"band": right},
            ),
        ]

    low_cell = cell_is_low((1, WIN, 512))

    def first_part(part, carry):
        x3 = x_ref[0, pl.ds(part * 16, 16)].astype(F32)
        xf = jnp.concatenate(
            [
                x3[r * 8 : r * 8 + 8, c * 8 : c * 8 + 8, :].reshape(CELLS, 512)
                for r in range(2)
                for c in range(2)
            ],
            axis=0,
        )
        qkv_buf[...] = dot(xf.astype(BF16), qkv_r[...]).astype(BF16)
        for w in range(4):
            rows = slice(w * CELLS, (w + 1) * CELLS)
            for g in range(4):
                q = qkv_buf[rows, g * 128 : g * 128 + 128]
                k = qkv_buf[rows, 512 + g * 128 : 640 + g * 128]
                v = qkv_buf[rows, 1024 + g * 128 : 1152 + g * 128]
                s = dot_over(k, spread_heads(q), 1, 1) * scale + bias_r[g]
                heads[rows, g * 128 : g * 128 + 128] = gather_heads(
                    dot_over(soften(s), v, 0, 0)
                ).astype(BF16)
        first = (xf + layer_norm(dot(heads[...], proj_r[...]), gain_r_ref[...])).astype(BF16)
        total = jnp.zeros((256, 512), F32)
        for f in range(4):
            hidden = gelu(dot(first, up[:, f * 512 : f * 512 + 512])).astype(BF16)
            total = total + dot(hidden, down[f * 512 : f * 512 + 512, :])
        second = (first.astype(F32) + layer_norm(total, gain_m_ref[...])).astype(BF16).astype(F32)
        for r in range(2):
            rows = pl.ds(part * 16 + r * 8, 8)
            w0 = second[r * 128 : r * 128 + 64].reshape(WIN, WIN, 512)
            w1 = second[r * 128 + 64 : r * 128 + 128].reshape(WIN, WIN, 512)
            tiles[rows, 1] = w0
            tiles[rows, 2] = w1
            to_left[part, r * 32 : r * 32 + 32] = (
                jnp.where(low_cell, w0[:HALF], turn(w0[HALF:])).reshape(32, 512).astype(BF16)
            )
            to_right[part, r * 32 : r * 32 + 32] = (
                jnp.where(low_cell, turn(w1[HALF:]), w1[:HALF]).reshape(32, 512).astype(BF16)
            )
        for send in sends(part):
            send.start()

        return carry

    lax.fori_loop(0, 2, first_part, 0)

    @pl.when(keeper)
    def _():
        for array in range(2):
            came(1, array)
            forward(array).start()
            share(1, array).start()
        for array in range(2):
            came(2, array)
            share(2, array).start()

    def shifted(column):
        pieces = []
        for w in range(4):
            for start in (w * 8 + 4, (w * 8 + 8) % 32):
                a = tiles[start : start + 4, column]
                b = tiles[start : start + 4, column + 1]
                pieces.append(turn(jnp.where(low_cell, b, a)))
        return jnp.concatenate(pieces, axis=0)

    def finish(x, first_row):
        third = x + layer_norm(dot(heads[...], proj_s[...]), gain_s_ref[...])
        third_buf[first_row : first_row + 256, :] = third.astype(BF16)

    key = lax.broadcasted_iota(jnp.int32, (CELLS, 256), 0)
    lane = lax.broadcasted_iota(jnp.int32, (CELLS, 256), 1)
    low_j = lane % 8 < HALF
    row_apart = (key // 8 < HALF) != ((lane // 16) % 8 < HALF)
    col_apart = ((key % 8 < HALF) != low_j) & (
        (low_j & (band == bands - 1)) | (jnp.logical_not(low_j) & (band == 0))
    )
    mask_row = jnp.where(row_apart, -100.0 * LOG2E, 0.0)
    mask_col = jnp.where(col_apart, -100.0 * LOG2E, 0.0)
    mask_both = jnp.where(row_apart | col_apart, -100.0 * LOG2E, 0.0)

    for load in loads[4:6]:
        load.wait()
    mid = shifted(1).reshape(256, 512)
    qkv_buf[...] = dot(mid.astype(BF16), qkv_s[...]).astype(BF16)
    for w in range(4):
        rows = slice(w * CELLS, (w + 1) * CELLS)
        for g in range(4):
            q = qkv_buf[rows, g * 128 : g * 128 + 128]
            k = qkv_buf[rows, 512 + g * 128 : 640 + g * 128]
            v = qkv_buf[rows, 1024 + g * 128 : 1152 + g * 128]
            s = dot_over(k, spread_heads(q), 1, 1) * scale + bias_s[g]
            if w == 3:
                s = s + mask_row
            heads[rows, g * 128 : g * 128 + 128] = gather_heads(
                dot_over(soften(s), v, 0, 0)
            ).astype(BF16)
    finish(mid, 0)

    for part in range(2):
        for send in sends(part):
            send.wait()
        for r in range(2):
            top = part * 16 + r * 8
            h = from_left[part, r * 32 : r * 32 + 32].astype(F32).reshape(HALF, WIN, 512)
            tiles[top : top + 4, 0] = h
            tiles[top + 4 : top + 8, 0] = turn(h)
            h = from_right[part, r * 32 : r * 32 + 32].astype(F32).reshape(HALF, WIN, 512)
            tiles[top : top + 4, 3] = h
            tiles[top + 4 : top + 8, 3] = turn(h)
    edge0 = shifted(0)
    edge2 = shifted(2)
    edge = jnp.where(low_cell, edge2, edge0).reshape(256, 512)
    qkv_buf[:, :512] = dot(edge.astype(BF16), qkv_s[:, :512]).astype(BF16)
    qkv_buf[:, 512:] = dot(edge0.reshape(256, 512).astype(BF16), qkv_s[:, 512:]).astype(BF16)
    edge_buf[...] = dot(edge2.reshape(256, 512).astype(BF16), qkv_s[:, 512:]).astype(BF16)
    for w in range(4):
        rows = slice(w * CELLS, (w + 1) * CELLS)
        for g in range(4):
            q = spread_heads(qkv_buf[rows, g * 128 : g * 128 + 128])
            k0 = qkv_buf[rows, 512 + g * 128 : 640 + g * 128]
            v0 = qkv_buf[rows, 1024 + g * 128 : 1152 + g * 128]
            k2 = edge_buf[rows, g * 128 : g * 128 + 128]
            v2 = edge_buf[rows, 512 + g * 128 : 640 + g * 128]
            s = jnp.where(low_j, dot_over(k2, q, 1, 1), dot_over(k0, q, 1, 1))
            s = s * scale + bias_s[g] + (mask_both if w == 3 else mask_col)
            o = dot_over(soften(s), jnp.concatenate([v2, v0], axis=1), 0, 0)
            o2 = gather_heads(o[:, :LANES]).reshape(WIN, WIN, LANES)
            o0 = gather_heads(o[:, LANES:]).reshape(WIN, WIN, LANES)
            heads[rows, g * 128 : g * 128 + 128] = (
                jnp.where(cell_is_low((1, WIN, LANES)), o2, o0).reshape(CELLS, LANES).astype(BF16)
            )
    finish(edge, 256)

    @pl.when(jnp.logical_not(is_head))
    def _():
        pl.semaphore_wait(ready_sem, 1)

    groups = range(GROUPS)

    def places(g):
        return range(g * PER_GROUP, (g + 1) * PER_GROUP)[::-1]

    def keep(block, buffer):
        @pl.when(my_core == 0)
        def _():
            buffer[0] = block

    third = third_buf[...]
    for g in groups:
        block = dot(place[g * ROWS : (g + 1) * ROWS], third).astype(BF16)
        block = block.reshape(PER_GROUP, CAP, 512)
        outgoing[g * PER_GROUP : (g + 1) * PER_GROUP] = block
        if g == 0:
            keep(block[0], arrived)
        each(places(g), lambda n: go(n).start())

    slot_column = jnp.transpose(jnp.broadcast_to(slot, (LANES, 512)))
    lane = lax.broadcasted_iota(jnp.int32, (512, LANES), 1).astype(F32)
    for n in range(PEERS * CAP // LANES):
        take[:, n * LANES : (n + 1) * LANES] = jnp.where(
            slot_column == lane + n * LANES, 1.0, 0.0
        ).astype(BF16)

    @pl.when(keeper)
    def _():
        came(3, 0)
        share(3, 0).start()
        for load in loads[6:]:
            load.wait()

    @pl.when(jnp.logical_not(keeper))
    def _():
        for slot in range(3):
            for array in range(2):
                came(slot, array)
        came(3, 0)

    def layer(rows, n):
        hidden = gelu(dot(rows, w_in[n])).astype(BF16)
        return dot(hidden, w_out[n])

    for g in groups:
        each(places(g), lambda n: landed(arrived, go_recv, n))
        rows = arrived[g * PER_GROUP : (g + 1) * PER_GROUP].reshape(ROWS, 512)
        total = layer(rows, 0) + layer(rows, 1) + layer(rows, 2)
        if g == groups[0]:
            came(3, 1)

            @pl.when(keeper)
            def _():
                share(3, 1).start()

        block = (total + layer(rows, 3)).astype(BF16).reshape(PER_GROUP, CAP, 512)
        result[g * PER_GROUP : (g + 1) * PER_GROUP] = block
        if g == 0:
            keep(block[0], returned)
        each(places(g), lambda n: back(n).start())

    for array in range(2):
        leave(array).wait_send()

    @pl.when(keeper)
    def _():
        for array in range(2):
            forward(array).wait_send()
            for slot in range(4):
                share(slot, array).wait_send()

    rows = jnp.zeros((512, 512), F32)
    for g in groups:
        each(places(g), lambda n: landed(returned, back_recv, n))
        block = returned[g * PER_GROUP : (g + 1) * PER_GROUP].reshape(ROWS, 512)
        rows = rows + dot(take[:, g * ROWS : (g + 1) * ROWS], block)
    encoded = third_buf[...].astype(F32) + layer_norm(rows, gain_e_ref[...])
    for w in range(4):
        mid = encoded[w * CELLS : (w + 1) * CELLS].reshape(WIN, WIN, 512)
        edge = encoded[256 + w * CELLS : 256 + (w + 1) * CELLS].reshape(WIN, WIN, 512)
        w0 = turn(jnp.where(low_cell, mid, edge))
        w1 = turn(jnp.where(low_cell, edge, mid))
        block = jnp.concatenate([w0, w1], axis=1).astype(BF16)
        for half in range(2):
            top = (w * 8 + 4 + half * 4) % 32
            enc_ref[0, top : top + 4] = block[half * 4 : half * 4 + 4]
    for g in groups:
        each(places(g), lambda n: go(n).wait_send())
        each(places(g), lambda n: back(n).wait_send())


def block_pair(features, routes, tables, gains, weights, shards):
    vmem = pl.BlockSpec(memory_space=pltpu.VMEM)
    hbm = pl.BlockSpec(memory_space=pl.ANY)
    dma = pltpu.SemaphoreType.DMA
    return pl.pallas_call(
        kernel,
        out_shape=jax.ShapeDtypeStruct((1, 32, 16, 512), BF16),
        in_specs=[vmem] * 8 + [hbm] * 8,
        out_specs=vmem,
        scratch_shapes=[pltpu.VMEM(w.shape, BF16) for w in weights]
        + [
            dma((8,)),
            pltpu.VMEM((16, 256), F32),
            pltpu.VMEM((4, CELLS, 256), F32),
            pltpu.VMEM((4, CELLS, 256), F32),
            pltpu.VMEM((32, 4, WIN, 512), F32),
            pltpu.VMEM((256, 1536), BF16),
            pltpu.VMEM((256, 1024), BF16),
            pltpu.VMEM((256, 512), BF16),
            pltpu.VMEM((512, 512), BF16),
        ]
        + [pltpu.VMEM((2, 64, 512), BF16)] * 4
        + [dma((2, 2)), dma((2, 2)), dma((12,)), dma((8,))]
        + [
            pltpu.VMEM((4, 512, 512), BF16),
            pltpu.VMEM((4, 512, 512), BF16),
            pltpu.VMEM((PEERS * CAP, 512), BF16),
            pltpu.VMEM((512, PEERS * CAP), BF16),
        ]
        + [pltpu.VMEM((PEERS, CAP, 512), BF16)] * 4
        + [dma((PEERS,))] * 4
        + [pltpu.SemaphoreType.REGULAR] * 2,
        compiler_params=pltpu.CompilerParams(
            collective_id=0, has_side_effects=True, vmem_limit_bytes=62 * 1024 * 1024
        ),
        name="block_pair",
    )(features, routes, *tables, *gains, *weights, *shards)


def local(
    features,
    routes,
    qkv_regular,
    proj_regular,
    table_regular,
    gain_regular,
    mlp_up,
    mlp_down,
    gain_mlp,
    qkv_shifted,
    proj_shifted,
    table_shifted,
    gain_shifted,
    expert_in,
    expert_out,
    gain_expert,
):
    gains = (gain_regular, gain_mlp, gain_shifted, gain_expert)
    return block_pair(
        features,
        routes.reshape(32, 16).T.reshape(16, 1, 32),
        (table_regular.T, table_shifted.T),
        [g.reshape(1, 512) for g in gains],
        (qkv_regular, proj_regular, mlp_up, mlp_down, qkv_shifted, proj_shifted),
        (expert_in, expert_out),
    )


def solution(mesh):
    return jax.shard_map(
        local,
        mesh=mesh,
        in_specs=(
            P("expert", None, "band", None),
            P("expert", "band", None, None, None),
        )
        + (P(),) * 11
        + (P("expert", None, "band"), P("expert", "band", None), P()),
        out_specs=P("expert", None, "band", None),
        check_vma=False,
    )
```

```python
import functools
import jax
import jax.numpy as jnp
from jax import lax
from jax.experimental import pallas as pl
from jax.experimental.pallas import tpu as pltpu
from jax.sharding import PartitionSpec as P

MESH = pl.DeviceIdType.MESH
F32 = jnp.float32
BF16 = jnp.bfloat16
WIN = 8
HALF = WIN // 2
CELLS = WIN * WIN
LANES = 128
LOG2E = 1.4426950408889634
ROOT_HALF = 0.7071067811865476


def dot(a, b):
    return jnp.dot(a, b, preferred_element_type=F32)


def dot_over(a, b, dim_a, dim_b):
    return lax.dot_general(a, b, (((dim_a,), (dim_b,)), ((), ())), preferred_element_type=F32)


def gelu(v):
    return (0.5 * v) * (1.0 + lax.erf(v * ROOT_HALF))


def layer_norm(values, gain_vec):
    centre = jnp.mean(values, axis=-1, keepdims=True)
    offsets = values - centre
    spread = jnp.mean(offsets * offsets, axis=-1, keepdims=True)
    return offsets * lax.rsqrt(spread + 1e-05) * gain_vec


def turn(tiles):
    return pltpu.roll(tiles, HALF, axis=tiles.ndim - 2)


def cell_is_low(shape):
    return lax.broadcasted_iota(jnp.int32, shape, len(shape) - 2) < HALF


def window_bias(table_ref, pad_ref, bias_ref):
    span = 2 * WIN - 1
    pitch = 2 * WIN
    width = pitch * pitch
    pad_ref[...] = jnp.zeros(pad_ref.shape, F32)
    pad_ref[:, : span * span] = table_ref[...] * LOG2E
    packed = pad_ref[...]
    line = lax.broadcasted_iota(jnp.int32, packed.shape, 1) // pitch
    flat = packed
    for a in range(1, span):
        flat = jnp.where(line == a, pltpu.roll(packed, a, axis=1), flat)
    even = lax.broadcasted_iota(jnp.int32, (WIN, LANES), 1) % pitch < WIN
    for group in range(4):
        for pair in range(2):
            head = group * 4 + pair * 2
            row_even = jnp.broadcast_to(flat[head : head + 1, :], (WIN, width))
            row_odd = jnp.broadcast_to(flat[head + 1 : head + 2, :], (WIN, width))
            for key_row in range(WIN):
                back = (WIN - 1 - key_row) * pitch + WIN - 1
                a = pltpu.roll(row_even, (width - back) % width, axis=1, stride=1, stride_axis=0)
                b = pltpu.roll(
                    row_odd, (width - back + WIN) % width, axis=1, stride=1, stride_axis=0
                )
                bias_ref[
                    group,
                    key_row * WIN : (key_row + 1) * WIN,
                    pair * LANES : (pair + 1) * LANES,
                ] = jnp.where(even, a[:, :LANES], b[:, :LANES])


def spread_heads(q):
    head = lax.broadcasted_iota(jnp.int32, (1, 1, LANES), 2) // 32
    tiles = q.astype(F32).reshape(WIN, WIN, LANES)
    pieces = []
    for pair in range(2):
        both = [jnp.where(head == pair * 2 + k, tiles, 0.0)[:, None] for k in range(2)]
        pieces.append(jnp.concatenate(both, axis=1).reshape(2 * CELLS, LANES))
    return jnp.concatenate(pieces, axis=0).astype(BF16)


def gather_heads(o):
    head = lax.broadcasted_iota(jnp.int32, (1, 1, LANES), 2) // 32
    parts = o.reshape(2, WIN, 2, WIN, LANES)
    low = jnp.where(head == 0, parts[0, :, 0], parts[0, :, 1])
    high = jnp.where(head == 2, parts[1, :, 0], parts[1, :, 1])
    return jnp.where(head < 2, low, high).reshape(CELLS, LANES)


def soften(s):
    e = jnp.exp2(s - jnp.max(s, axis=0, keepdims=True))
    return (e * (1.0 / jnp.sum(e, axis=0, keepdims=True))).astype(BF16)


AWAY = sorted(
    ((z, x) for z in range(4) for x in range(4)),
    key=lambda d: (min(d[0], 4 - d[0]) + min(d[1], 4 - d[1]), d),
)
PEERS = 32
CAP = 32
GROUPS = 4
PER_GROUP = PEERS // GROUPS
ROWS = PER_GROUP * CAP


def token_routes(routes_ref):
    grid = routes_ref[...].reshape(16, 32).astype(F32).astype(BF16)
    token = lax.broadcasted_iota(jnp.int32, (32, 512), 1)
    row = ((token // 64) % 4 * 8 + 4 + (token // 8) % 8) % 32
    at_row = jnp.where(lax.broadcasted_iota(jnp.int32, (32, 512), 0) == row, 1.0, 0.0)
    token = lax.broadcasted_iota(jnp.int32, (16, 512), 1)
    cell = token % 8
    column = jnp.where(token < 256, HALF + cell, (cell + 12) % 16)
    at_column = lax.broadcasted_iota(jnp.int32, (16, 512), 0) == column
    picked = jnp.where(at_column, dot(grid, at_row.astype(BF16)), 0.0)
    return jnp.sum(picked, axis=0, keepdims=True).astype(jnp.int32)


def kernel(
    x_ref,
    routes_ref,
    table_r_ref,
    table_s_ref,
    gain_r_ref,
    gain_m_ref,
    gain_s_ref,
    gain_e_ref,
    qkv_r_hbm,
    proj_r_hbm,
    up_hbm,
    down_hbm,
    qkv_s_hbm,
    proj_s_hbm,
    own_in,
    own_out,
    enc_ref,
    qkv_r,
    proj_r,
    up,
    down,
    qkv_s,
    proj_s,
    load_sem,
    pad,
    bias_r,
    bias_s,
    tiles,
    qkv_buf,
    edge_buf,
    heads,
    third_buf,
    to_left,
    to_right,
    from_left,
    from_right,
    send_sem,
    recv_sem,
    shard_send,
    shard_recv,
    w_in,
    w_out,
    place,
    take,
    outgoing,
    arrived,
    result,
    returned,
    go_send,
    go_recv,
    back_send,
    back_recv,
    heads_sem,
    ready_sem,
):
    band = lax.axis_index("band")
    bands = lax.axis_size("band")
    right = lax.rem(band + 1, bands)
    left = lax.rem(band + bands - 1, bands)
    me = lax.axis_index("expert")
    my_z, my_x, my_core = me // 8, (me // 2) % 4, me % 2
    hosted = band // 2
    mirror = bands - 1 - band
    beside = hosted * 4 + 1 - band
    served = jnp.where(my_core == 0, band, mirror)
    keeper = my_core == hosted
    sibling = me + 1 - 2 * my_core

    def chip(n, sign):
        z, x = AWAY[n // 2]
        return ((my_z + 4 + sign * z) % 4 * 4 + (my_x + 4 + sign * x) % 4) * 2

    barrier = pltpu.get_barrier_semaphore()

    def tell(sem, expert, level):
        to = {"band": level, "expert": expert}
        pl.semaphore_signal(sem, inc=1, device_id=to, device_id_type=MESH)

    head = my_z * 8
    is_head = me == head
    other_heads = [
        ((head + 8 * n) % PEERS, level) for level in (band, mirror) for n in range(4)
    ][1:]
    tell(barrier, me, left)
    tell(barrier, me, right)
    tell(barrier, sibling, band)

    @pl.when(is_head)
    def _():
        for other in other_heads:
            tell(barrier, *other)

    @pl.when(jnp.logical_not(is_head))
    def _():
        tell(barrier, head, band)

    loads = [
        pltpu.make_async_copy(src, dst, load_sem.at[n])
        for n, (src, dst) in enumerate(
            (
                (qkv_r_hbm, qkv_r),
                (proj_r_hbm, proj_r),
                (up_hbm, up),
                (down_hbm, down),
                (qkv_s_hbm, qkv_s),
                (proj_s_hbm, proj_s),
                (own_in.at[0], w_in.at[0]),
                (own_out.at[0], w_out.at[0]),
            )
        )
    ]
    for load in loads[:6]:
        load.start()

    def remote(src, dst, send_sem, recv_sem, to):
        return pltpu.make_async_remote_copy(
            src_ref=src,
            dst_ref=dst,
            send_sem=send_sem,
            recv_sem=recv_sem,
            device_id=to,
            device_id_type=MESH,
        )

    shelves = (w_in, w_out)
    own = (own_in.at[0], own_out.at[0])

    def shard(src, slot, array, n, expert, level):
        return remote(
            src,
            shelves[array].at[slot],
            shard_send.at[n],
            shard_recv.at[slot * 2 + array],
            {"band": level, "expert": expert},
        )

    def leave(array):
        slot = jnp.where(keeper, 2, 1)
        return shard(own[array], slot, array, array, me, jnp.where(keeper, beside, mirror))

    def forward(array):
        return shard(shelves[array].at[1], 3, array, 2 + array, me, beside)

    def share(slot, array):
        src = own[array] if slot == 0 else shelves[array].at[slot]
        return shard(src, slot, array, 4 + slot * 2 + array, sibling, band)

    def came(slot, array):
        share(slot, array).wait_recv()

    def go(n):
        to = {"band": mirror if n % 2 else band, "expert": chip(n, 1) + n % 2}
        slot = n // 2 * 2 + my_core
        return remote(outgoing.at[n], arrived.at[slot], go_send.at[n], go_recv.at[slot], to)

    def back(n):
        to = {"band": served, "expert": chip(n, -1) + n % 2}
        slot = n // 2 * 2 + my_core
        return remote(result.at[n], returned.at[slot], back_send.at[n], back_recv.at[slot], to)

    def landed(buffer, sem, n):
        to = {"band": band, "expert": sibling}
        remote(buffer.at[n], buffer.at[n], shard_send.at[0], sem.at[n], to).wait_recv()

    def each(places, act):
        for n in places:
            if n:
                act(n)
            else:
                pl.when(my_core == 1)(functools.partial(act, n))

    routes = token_routes(routes_ref)
    code = (((routes >> 3) - my_z) & 3) * 4 + (((routes >> 1) - my_x) & 3)
    spot = jnp.zeros_like(routes)
    for n, (z, x) in enumerate(AWAY):
        spot = jnp.where(code == z * 4 + x, n, spot)
    spot = spot * 2 + ((routes - hosted) & 1)
    chosen = lax.broadcasted_iota(jnp.int32, (PEERS, 512), 0) == spot
    onehot = jnp.where(chosen, 1.0, 0.0)
    before = lax.broadcasted_iota(jnp.int32, (512, 512), 0) < lax.broadcasted_iota(
        jnp.int32, (512, 512), 1
    )
    ahead = dot(onehot.astype(BF16), jnp.where(before, 1.0, 0.0).astype(BF16))
    slot = spot.astype(F32) * CAP + jnp.sum(onehot * ahead, axis=0, keepdims=True)
    for g in range(GROUPS):
        rows = (lax.broadcasted_iota(jnp.int32, (ROWS, 512), 0) + g * ROWS).astype(F32)
        place[g * ROWS : (g + 1) * ROWS] = jnp.where(rows == slot, 1.0, 0.0).astype(BF16)

    window_bias(table_r_ref, pad, bias_r)
    window_bias(table_s_ref, pad, bias_s)

    @pl.when(is_head)
    def _():
        pl.semaphore_wait(barrier, 3 + 7 + 7)
        for other in other_heads:
            tell(heads_sem, *other)

    @pl.when(jnp.logical_not(is_head))
    def _():
        pl.semaphore_wait(barrier, 3)

    for array in range(2):
        leave(array).start()

    @pl.when(keeper)
    def _():
        for array in range(2):
            share(0, array).start()
        for load in loads[6:]:
            load.start()

    scale = LOG2E * 32**-0.5


    @pl.when(is_head)
    def _():
        pl.semaphore_wait(heads_sem, 7)
        for n in range(1, 8):
            tell(ready_sem, head + n, band)

    for load in loads[:4]:
        load.wait()

    def sends(part):
        return [
            remote(
                to_left.at[part],
                from_right.at[part],
                send_sem.at[0, part],
                recv_sem.at[0, part],
                {"band": left},
            ),
            remote(
                to_right.at[part],
                from_left.at[part],
                send_sem.at[1, part],
                recv_sem.at[1, part],
                {"band": right},
            ),
        ]

    low_cell = cell_is_low((1, WIN, 512))

    def first_part(part, carry):
        x3 = x_ref[0, pl.ds(part * 16, 16)].astype(F32)
        xf = jnp.concatenate(
            [
                x3[r * 8 : r * 8 + 8, c * 8 : c * 8 + 8, :].reshape(CELLS, 512)
                for r in range(2)
                for c in range(2)
            ],
            axis=0,
        )
        qkv_buf[...] = dot(xf.astype(BF16), qkv_r[...]).astype(BF16)
        for w in range(4):
            rows = slice(w * CELLS, (w + 1) * CELLS)
            for g in range(4):
                q = qkv_buf[rows, g * 128 : g * 128 + 128]
                k = qkv_buf[rows, 512 + g * 128 : 640 + g * 128]
                v = qkv_buf[rows, 1024 + g * 128 : 1152 + g * 128]
                s = dot_over(k, spread_heads(q), 1, 1) * scale + bias_r[g]
                heads[rows, g * 128 : g * 128 + 128] = gather_heads(
                    dot_over(soften(s), v, 0, 0)
                ).astype(BF16)
        first = (xf + layer_norm(dot(heads[...], proj_r[...]), gain_r_ref[...])).astype(BF16)
        total = jnp.zeros((256, 512), F32)
        for f in range(4):
            hidden = gelu(dot(first, up[:, f * 512 : f * 512 + 512])).astype(BF16)
            total = total + dot(hidden, down[f * 512 : f * 512 + 512, :])
        second = (first.astype(F32) + layer_norm(total, gain_m_ref[...])).astype(BF16).astype(F32)
        for r in range(2):
            rows = pl.ds(part * 16 + r * 8, 8)
            w0 = second[r * 128 : r * 128 + 64].reshape(WIN, WIN, 512)
            w1 = second[r * 128 + 64 : r * 128 + 128].reshape(WIN, WIN, 512)
            tiles[rows, 1] = w0
            tiles[rows, 2] = w1
            to_left[part, r * 32 : r * 32 + 32] = (
                jnp.where(low_cell, w0[:HALF], turn(w0[HALF:])).reshape(32, 512).astype(BF16)
            )
            to_right[part, r * 32 : r * 32 + 32] = (
                jnp.where(low_cell, turn(w1[HALF:]), w1[:HALF]).reshape(32, 512).astype(BF16)
            )
        for send in sends(part):
            send.start()

        return carry

    lax.fori_loop(0, 2, first_part, 0)

    @pl.when(keeper)
    def _():
        for array in range(2):
            came(1, array)
            forward(array).start()
            share(1, array).start()

    def shifted(column):
        pieces = []
        for w in range(4):
            for start in (w * 8 + 4, (w * 8 + 8) % 32):
                a = tiles[start : start + 4, column]
                b = tiles[start : start + 4, column + 1]
                pieces.append(turn(jnp.where(low_cell, b, a)))
        return jnp.concatenate(pieces, axis=0)

    def finish(x, first_row):
        third = x + layer_norm(dot(heads[...], proj_s[...]), gain_s_ref[...])
        third_buf[first_row : first_row + 256, :] = third.astype(BF16)

    key = lax.broadcasted_iota(jnp.int32, (CELLS, 256), 0)
    lane = lax.broadcasted_iota(jnp.int32, (CELLS, 256), 1)
    low_j = lane % 8 < HALF
    row_apart = (key // 8 < HALF) != ((lane // 16) % 8 < HALF)
    col_apart = ((key % 8 < HALF) != low_j) & (
        (low_j & (band == bands - 1)) | (jnp.logical_not(low_j) & (band == 0))
    )
    mask_row = jnp.where(row_apart, -100.0 * LOG2E, 0.0)
    mask_col = jnp.where(col_apart, -100.0 * LOG2E, 0.0)
    mask_both = jnp.where(row_apart | col_apart, -100.0 * LOG2E, 0.0)

    for load in loads[4:6]:
        load.wait()
    mid = shifted(1).reshape(256, 512)
    qkv_buf[...] = dot(mid.astype(BF16), qkv_s[...]).astype(BF16)
    for w in range(4):
        rows = slice(w * CELLS, (w + 1) * CELLS)
        for g in range(4):
            q = qkv_buf[rows, g * 128 : g * 128 + 128]
            k = qkv_buf[rows, 512 + g * 128 : 640 + g * 128]
            v = qkv_buf[rows, 1024 + g * 128 : 1152 + g * 128]
            s = dot_over(k, spread_heads(q), 1, 1) * scale + bias_s[g]
            if w == 3:
                s = s + mask_row
            heads[rows, g * 128 : g * 128 + 128] = gather_heads(
                dot_over(soften(s), v, 0, 0)
            ).astype(BF16)
    finish(mid, 0)

    @pl.when(keeper)
    def _():
        for array in range(2):
            came(2, array)
            share(2, array).start()

    for part in range(2):
        for send in sends(part):
            send.wait()
        for r in range(2):
            top = part * 16 + r * 8
            h = from_left[part, r * 32 : r * 32 + 32].astype(F32).reshape(HALF, WIN, 512)
            tiles[top : top + 4, 0] = h
            tiles[top + 4 : top + 8, 0] = turn(h)
            h = from_right[part, r * 32 : r * 32 + 32].astype(F32).reshape(HALF, WIN, 512)
            tiles[top : top + 4, 3] = h
            tiles[top + 4 : top + 8, 3] = turn(h)
    edge0 = shifted(0)
    edge2 = shifted(2)
    edge = jnp.where(low_cell, edge2, edge0).reshape(256, 512)
    qkv_buf[:, :512] = dot(edge.astype(BF16), qkv_s[:, :512]).astype(BF16)
    qkv_buf[:, 512:] = dot(edge0.reshape(256, 512).astype(BF16), qkv_s[:, 512:]).astype(BF16)
    edge_buf[...] = dot(edge2.reshape(256, 512).astype(BF16), qkv_s[:, 512:]).astype(BF16)
    for w in range(4):
        rows = slice(w * CELLS, (w + 1) * CELLS)
        for g in range(4):
            q = spread_heads(qkv_buf[rows, g * 128 : g * 128 + 128])
            k0 = qkv_buf[rows, 512 + g * 128 : 640 + g * 128]
            v0 = qkv_buf[rows, 1024 + g * 128 : 1152 + g * 128]
            k2 = edge_buf[rows, g * 128 : g * 128 + 128]
            v2 = edge_buf[rows, 512 + g * 128 : 640 + g * 128]
            s = jnp.where(low_j, dot_over(k2, q, 1, 1), dot_over(k0, q, 1, 1))
            s = s * scale + bias_s[g] + (mask_both if w == 3 else mask_col)
            o = dot_over(soften(s), jnp.concatenate([v2, v0], axis=1), 0, 0)
            o2 = gather_heads(o[:, :LANES]).reshape(WIN, WIN, LANES)
            o0 = gather_heads(o[:, LANES:]).reshape(WIN, WIN, LANES)
            heads[rows, g * 128 : g * 128 + 128] = (
                jnp.where(cell_is_low((1, WIN, LANES)), o2, o0).reshape(CELLS, LANES).astype(BF16)
            )
    finish(edge, 256)

    @pl.when(jnp.logical_not(is_head))
    def _():
        pl.semaphore_wait(ready_sem, 1)

    groups = range(GROUPS)

    def places(g):
        return range(g * PER_GROUP, (g + 1) * PER_GROUP)[::-1]

    def keep(block, buffer):
        @pl.when(my_core == 0)
        def _():
            buffer[0] = block

    third = third_buf[...]
    for g in groups:
        block = dot(place[g * ROWS : (g + 1) * ROWS], third).astype(BF16)
        block = block.reshape(PER_GROUP, CAP, 512)
        outgoing[g * PER_GROUP : (g + 1) * PER_GROUP] = block
        if g == 0:
            keep(block[0], arrived)
        each(places(g), lambda n: go(n).start())

    slot_column = jnp.transpose(jnp.broadcast_to(slot, (LANES, 512)))
    lane = lax.broadcasted_iota(jnp.int32, (512, LANES), 1).astype(F32)
    for n in range(PEERS * CAP // LANES):
        take[:, n * LANES : (n + 1) * LANES] = jnp.where(
            slot_column == lane + n * LANES, 1.0, 0.0
        ).astype(BF16)

    @pl.when(keeper)
    def _():
        came(3, 0)
        share(3, 0).start()
        for load in loads[6:]:
            load.wait()

    @pl.when(jnp.logical_not(keeper))
    def _():
        for slot in range(3):
            for array in range(2):
                came(slot, array)
        came(3, 0)

    def layer(rows, n):
        hidden = gelu(dot(rows, w_in[n])).astype(BF16)
        return dot(hidden, w_out[n])

    for g in groups:
        each(places(g), lambda n: landed(arrived, go_recv, n))
        rows = arrived[g * PER_GROUP : (g + 1) * PER_GROUP].reshape(ROWS, 512)
        total = layer(rows, 0) + layer(rows, 1) + layer(rows, 2)
        if g == groups[0]:
            came(3, 1)

            @pl.when(keeper)
            def _():
                share(3, 1).start()

        block = (total + layer(rows, 3)).astype(BF16).reshape(PER_GROUP, CAP, 512)
        result[g * PER_GROUP : (g + 1) * PER_GROUP] = block
        if g == 0:
            keep(block[0], returned)
        each(places(g), lambda n: back(n).start())

    for array in range(2):
        leave(array).wait_send()

    @pl.when(keeper)
    def _():
        for array in range(2):
            forward(array).wait_send()
            for slot in range(4):
                share(slot, array).wait_send()

    rows = jnp.zeros((512, 512), F32)
    for g in groups:
        each(places(g), lambda n: landed(returned, back_recv, n))
        block = returned[g * PER_GROUP : (g + 1) * PER_GROUP].reshape(ROWS, 512)
        rows = rows + dot(take[:, g * ROWS : (g + 1) * ROWS], block)
    encoded = third_buf[...].astype(F32) + layer_norm(rows, gain_e_ref[...])
    for w in range(4):
        mid = encoded[w * CELLS : (w + 1) * CELLS].reshape(WIN, WIN, 512)
        edge = encoded[256 + w * CELLS : 256 + (w + 1) * CELLS].reshape(WIN, WIN, 512)
        w0 = turn(jnp.where(low_cell, mid, edge))
        w1 = turn(jnp.where(low_cell, edge, mid))
        block = jnp.concatenate([w0, w1], axis=1).astype(BF16)
        for half in range(2):
            top = (w * 8 + 4 + half * 4) % 32
            enc_ref[0, top : top + 4] = block[half * 4 : half * 4 + 4]
    for g in groups:
        each(places(g), lambda n: go(n).wait_send())
        each(places(g), lambda n: back(n).wait_send())


def block_pair(features, routes, tables, gains, weights, shards):
    vmem = pl.BlockSpec(memory_space=pltpu.VMEM)
    hbm = pl.BlockSpec(memory_space=pl.ANY)
    dma = pltpu.SemaphoreType.DMA
    return pl.pallas_call(
        kernel,
        out_shape=jax.ShapeDtypeStruct((1, 32, 16, 512), BF16),
        in_specs=[vmem] * 8 + [hbm] * 8,
        out_specs=vmem,
        scratch_shapes=[pltpu.VMEM(w.shape, BF16) for w in weights]
        + [
            dma((8,)),
            pltpu.VMEM((16, 256), F32),
            pltpu.VMEM((4, CELLS, 256), F32),
            pltpu.VMEM((4, CELLS, 256), F32),
            pltpu.VMEM((32, 4, WIN, 512), F32),
            pltpu.VMEM((256, 1536), BF16),
            pltpu.VMEM((256, 1024), BF16),
            pltpu.VMEM((256, 512), BF16),
            pltpu.VMEM((512, 512), BF16),
        ]
        + [pltpu.VMEM((2, 64, 512), BF16)] * 4
        + [dma((2, 2)), dma((2, 2)), dma((12,)), dma((8,))]
        + [
            pltpu.VMEM((4, 512, 512), BF16),
            pltpu.VMEM((4, 512, 512), BF16),
            pltpu.VMEM((PEERS * CAP, 512), BF16),
            pltpu.VMEM((512, PEERS * CAP), BF16),
        ]
        + [pltpu.VMEM((PEERS, CAP, 512), BF16)] * 4
        + [dma((PEERS,))] * 4
        + [pltpu.SemaphoreType.REGULAR] * 2,
        compiler_params=pltpu.CompilerParams(
            collective_id=0, has_side_effects=True, vmem_limit_bytes=62 * 1024 * 1024
        ),
        name="block_pair",
    )(features, routes, *tables, *gains, *weights, *shards)


def local(
    features,
    routes,
    qkv_regular,
    proj_regular,
    table_regular,
    gain_regular,
    mlp_up,
    mlp_down,
    gain_mlp,
    qkv_shifted,
    proj_shifted,
    table_shifted,
    gain_shifted,
    expert_in,
    expert_out,
    gain_expert,
):
    gains = (gain_regular, gain_mlp, gain_shifted, gain_expert)
    return block_pair(
        features,
        routes.reshape(32, 16).T.reshape(16, 1, 32),
        (table_regular.T, table_shifted.T),
        [g.reshape(1, 512) for g in gains],
        (qkv_regular, proj_regular, mlp_up, mlp_down, qkv_shifted, proj_shifted),
        (expert_in, expert_out),
    )


def solution(mesh):
    return jax.shard_map(
        local,
        mesh=mesh,
        in_specs=(
            P("expert", None, "band", None),
            P("expert", "band", None, None, None),
        )
        + (P(),) * 11
        + (P("expert", None, "band"), P("expert", "band", None), P()),
        out_specs=P("expert", None, "band", None),
        check_vma=False,
    )
```
